128 devices in a mesh: node: 32 (over y_hi, z, x), query: 4 (over y_lo, core).
Axes of the slice: x: 4, y: 4 (y_hi: 2, y_lo: 2; y = y_hi * 2 + y_lo), z: 4, core: 2. Of those that a mesh axis runs over, the one named last changes fastest.
Arguments:
- entity_state: bfloat16 [32768, 2048], P('node', 'query'), may hold values from -6 to 6
- edge_tiles: int32 [512, 3, 512], P('node'), may hold values from 0 to 4095, as said below
- query_head: int32 [64], P('query'), may hold values from 0 to 32767
- query_relation: int32 [64], P('query'), may hold values from 0 to 821
- query_table: float32 [822, 32], replicated, may hold values from -6 to 6
- rel_vectors: float32 [2, 822, 32], replicated, may hold values from -1.8 to 1.8
- mix_weight: float32 [2, 32, 32], replicated, may hold values from -1 to 1
- mix_bias: float32 [2, 32], replicated, may hold values from -3 to 3
- cotangent: bfloat16 [32768, 2048], P('node', 'query'), may hold values from -6 to 6
Outputs:
- final_state: bfloat16 [32768, 2048], P('node', 'query')
- weight_grads: float32 [2, 32, 32], replicated
- bias_grads: float32 [2, 32], replicated
The draws below stay inside these ranges and needn't reach their ends.
Inputs may be any that keep to these rules, and one draw needn't show every extreme that they name: edge_tiles[t,0,:] lies in 0 to 4095, edge_tiles[t,1,:] in 0 to 63, edge_tiles[t,2,:] in 0 to 821.
All inputs are finite; a program needn't handle non-finite values.
Results may differ from the reference program's by a relative error of at most 0.0056.
Values may be sent and summed in bfloat16 or wider, within the bound.
A program may use at most 192 MiB of HBM per device.

```python
import jax
import jax.numpy as jnp
from jax import lax

DIM = 32
NREL = 822
EDGE_SLOTS = 512
TILES = 16
ROWS_DEV = 1024
NENT = 32768
NTILES = 512
QUERIES = 64
N_NODE = 32


def draw_edge_tiles(key, part):
    keys = jax.random.split(jax.random.fold_in(key, 7), 5)
    shape = (NTILES, 1, EDGE_SLOTS)
    slots = jax.random.randint(keys[0], shape, 0, 4 * ROWS_DEV, dtype=jnp.int32)
    rows_first = jax.random.randint(keys[1], shape, 0, 64, dtype=jnp.int32)
    rows_second = jax.random.randint(keys[2], shape, 0, 64, dtype=jnp.int32)
    rels_first = jax.random.randint(keys[3], shape, 0, NREL, dtype=jnp.int32)
    rels_second = jax.random.randint(keys[4], shape, 0, NREL, dtype=jnp.int32)
    target_rows = jnp.minimum(rows_first, rows_second)
    relations = jnp.minimum(rels_first, rels_second)
    return jnp.concatenate([slots, target_rows, relations], axis=1).astype(jnp.int32)


def touch_ends(values, own_key, least, top_value):
    longest = values.shape.index(max(values.shape))
    spots = []
    for shift in (0, 1):
        where = [jax.random.randint(jax.random.fold_in(own_key, axis), (), 0, length) for axis, length in enumerate(values.shape)]
        where[longest] = (where[longest] + shift) % values.shape[longest]
        spots.append(tuple(where))
    return values.at[spots[0]].set(least).at[spots[1]].set(top_value)


def shard_levels(key, extent, pieces, least, high):
    gain, own = 1.0, jax.random.fold_in(key, 6)
    for axis_at, blocks in pieces:
        heights = jnp.exp(jax.random.uniform(jax.random.fold_in(own, axis_at), (blocks,), jnp.float32, least / len(pieces), high / len(pieces)))
        gain = gain * jnp.repeat(heights, extent[axis_at] // blocks).reshape([-1 if axis == axis_at else 1 for axis in range(len(extent))])
    return gain


def scatter_about(stream_key, shape, width, limit, shards=(), kind=jnp.bfloat16):
    values = jax.random.normal(stream_key, shape, jnp.float32) * width
    if len(shards) > 0:
        values = shard_levels(stream_key, shape, shards, -0.22, 0.18) * values
    return jnp.clip(values, min=-limit, max=limit).astype(kind)


def setup_inputs(seed: int = 0) -> dict:
    splits = jax.random.split(jax.random.key(seed), 10)
    entity_state = scatter_about(splits[0], (NENT, QUERIES * DIM), 1.0, 6.0, ((0, 32), (1, 4)))
    edge_tiles = draw_edge_tiles(jax.random.fold_in(splits[9], 71), 0)
    query_head = touch_ends(jax.random.randint(splits[2], (QUERIES,), 0, NENT), jax.random.fold_in(splits[2], 1), 0, NENT - 1).astype(jnp.int32)
    query_relation = touch_ends(jax.random.randint(splits[3], (QUERIES,), 0, NREL), jax.random.fold_in(splits[3], 1), 0, NREL - 1).astype(jnp.int32)
    query_table = scatter_about(splits[4], (NREL, DIM), 1.0, 6.0, (), jnp.float32)
    rel_vectors = scatter_about(splits[5], (2, NREL, DIM), 0.3, 1.8, (), jnp.float32)
    mix_weight = scatter_about(splits[6], (2, DIM, DIM), DIM ** -0.5, 1.0, (), jnp.float32)
    mix_bias = scatter_about(splits[7], (2, DIM), 0.5, 3.0, (), jnp.float32)
    cotangent = scatter_about(splits[8], (NENT, QUERIES * DIM), 1.0, 6.0, ((0, 32), (1, 4)))
    return dict(entity_state=entity_state, edge_tiles=edge_tiles, query_head=query_head, query_relation=query_relation, query_table=query_table, rel_vectors=rel_vectors, mix_weight=mix_weight, mix_bias=mix_bias, cotangent=cotangent)


def silu_slope(values):
    sigma = jax.nn.sigmoid(values)
    return sigma * (1.0 + values * (1.0 - sigma))


def source_ids(block, part_index):
    slots = block[:, 0, :]
    quarter = slots // ROWS_DEV
    offsets = jnp.array([-1, 0, 1, N_NODE // 2], dtype=jnp.int32)[quarter]
    return (((part_index + offsets) % N_NODE) * ROWS_DEV + slots % ROWS_DEV).astype(jnp.int32)


def propagate(state, rel_table, edge_tiles):
    col_count = state.shape[1]

    def one_part(part_index):
        block = lax.dynamic_slice_in_dim(edge_tiles, (part_index * TILES).astype(jnp.int32), TILES, 0)
        sources = source_ids(block, part_index).reshape(-1)
        targets = (lax.iota(jnp.int32, TILES)[:, None] * 64 + block[:, 1, :]).reshape(-1)
        rel_scale = rel_table[block[:, 2, :].reshape(-1)]
        picked = state[sources].astype(jnp.float32).reshape(-1, col_count // DIM, DIM)
        message = (picked * rel_scale[:, None, :]).astype(jnp.bfloat16).reshape(-1, col_count)
        return jax.ops.segment_sum(message.astype(jnp.float32), targets, num_segments=ROWS_DEV)

    parts = lax.map(one_part, jnp.arange(N_NODE, dtype=jnp.int32))
    return parts.reshape(NENT, col_count)


def adjoint(grad_panel, rel_table, edge_tiles):
    col_count = grad_panel.shape[1]

    def add_part(total, part_index):
        block = lax.dynamic_slice_in_dim(edge_tiles, (part_index * TILES).astype(jnp.int32), TILES, 0)
        slots = block[:, 0, :].reshape(-1)
        targets = (part_index * ROWS_DEV + lax.iota(jnp.int32, TILES)[:, None] * 64 + block[:, 1, :]).reshape(-1)
        rel_scale = rel_table[block[:, 2, :].reshape(-1)]
        picked = grad_panel[targets].astype(jnp.float32).reshape(-1, col_count // DIM, DIM)
        edge_terms = (picked * rel_scale[:, None, :]).reshape(-1, col_count)
        window_terms = jax.ops.segment_sum(edge_terms, slots, num_segments=4 * ROWS_DEV).reshape(4, ROWS_DEV, col_count)
        rounded = lax.optimization_barrier(window_terms.astype(jnp.bfloat16)).astype(jnp.float32)
        keep_own = (lax.iota(jnp.int32, 4) == 1)[:, None, None]
        window_terms = jnp.where(keep_own, window_terms, rounded)
        offsets = jnp.array([-1, 0, 1, N_NODE // 2], dtype=jnp.int32)
        rows = (((part_index + offsets) % N_NODE) * ROWS_DEV)[:, None] + lax.iota(jnp.int32, ROWS_DEV)[None, :]
        return total.at[rows.reshape(-1)].add(window_terms.reshape(-1, col_count)), None

    start = jnp.zeros((NENT, col_count), jnp.float32)
    total, unused = lax.scan(add_part, start, jnp.arange(N_NODE, dtype=jnp.int32))
    return total


def reference(entity_state, edge_tiles, query_head, query_relation, query_table, rel_vectors, mix_weight, mix_bias, cotangent):
    highest = lax.Precision.HIGHEST
    col_count = entity_state.shape[1]
    query_vec = query_table[query_relation]
    entity_ids = jnp.arange(NENT, dtype=jnp.int32)
    head_match = (entity_ids[:, None] == query_head[None, :]).astype(jnp.float32)
    boundary = (head_match[:, :, None] * query_vec[None, :, :]).reshape(NENT, col_count).astype(jnp.bfloat16)

    def run_layer(state, layer_index):
        mixed_in = boundary.astype(jnp.float32) + propagate(state, rel_vectors[layer_index], edge_tiles)
        update = jnp.einsum("rqd,de->rqe", mixed_in.reshape(NENT, QUERIES, DIM), mix_weight[layer_index], precision=highest) + mix_bias[layer_index]
        result = (state.astype(jnp.float32) + jax.nn.silu(update).reshape(NENT, col_count)).astype(jnp.bfloat16)
        return mixed_in, update, result

    mixed_zero, update_zero, state_one = run_layer(entity_state, 0)
    mixed_one, update_one, state_two = run_layer(state_one, 1)
    grad_out = cotangent.astype(jnp.float32)
    grad_update_one = grad_out.reshape(NENT, QUERIES, DIM) * silu_slope(update_one)
    grad_mixed_one = jnp.einsum("rqe,de->rqd", grad_update_one, mix_weight[1], precision=highest).reshape(NENT, col_count).astype(jnp.bfloat16)
    grad_state_one = grad_out + adjoint(grad_mixed_one, rel_vectors[1], edge_tiles)
    grad_update_zero = grad_state_one.reshape(NENT, QUERIES, DIM) * silu_slope(update_zero)
    weight_zero = jnp.einsum("rqd,rqe->de", mixed_zero.reshape(NENT, QUERIES, DIM), grad_update_zero, precision=highest)
    weight_one = jnp.einsum("rqd,rqe->de", mixed_one.reshape(NENT, QUERIES, DIM), grad_update_one, precision=highest)
    bias_zero = jnp.sum(grad_update_zero, axis=(0, 1))
    bias_one = jnp.sum(grad_update_one, axis=(0, 1))
    return state_two, jnp.stack([weight_zero, weight_one]), jnp.stack([bias_zero, bias_one])
```

```python
import functools

import jax
import jax.numpy as jnp
from jax import lax
from jax.experimental import pallas as pl
from jax.experimental.pallas import tpu as pltpu
from jax.sharding import PartitionSpec as P

DIM = 32
LANES = 128
TILE = 64
F32 = jnp.float32
BF16 = jnp.bfloat16
MESH = pl.DeviceIdType.MESH
VMEM_BYTES = 56 << 20


def split_dot(left, right_high, right_low):
    high = left.astype(BF16)
    low = (left - high.astype(F32)).astype(BF16)
    total = jnp.dot(high, right_high, preferred_element_type=F32)
    total += jnp.dot(low, right_high, preferred_element_type=F32)
    return total + jnp.dot(high, right_low, preferred_element_type=F32)


def split_pair(matrix):
    high = matrix.astype(BF16)
    return high, (matrix - high.astype(F32)).astype(BF16)


def spread_rows(target, first, block):
    rows, cols = block.shape
    count = cols // LANES
    for c in range(count):
        target[pl.ds(first * count + c, rows, stride=count), :] = block[:, c * LANES : (c + 1) * LANES]


def spread_relations(target, rel_ref):
    wide = jnp.concatenate([rel_ref[...]] * (LANES // DIM), axis=1)
    rows = wide.shape[0]
    for c in range(4):
        target[pl.ds(c, rows, stride=4), :] = wide


def block_sums(product):
    rows = lax.broadcasted_iota(jnp.int32, (LANES, LANES), 0) // DIM
    cols = lax.broadcasted_iota(jnp.int32, (LANES, LANES), 1) // DIM
    kept = jnp.where(rows == cols, product, 0.0)
    folded = kept[0:32] + kept[32:64] + kept[64:96] + kept[96:128]
    folded = fold_lanes(folded)
    lane = lax.broadcasted_iota(jnp.int32, (8, LANES), 1) // DIM
    packed = jnp.where(lane == 0, folded[0:8], 0.0)
    for k in range(1, 4):
        packed = jnp.where(lane == k, folded[8 * k : 8 * k + 8], packed)
    return packed


def fold_lanes(values):
    values = values + pltpu.roll(values, 64, 1)
    return values + pltpu.roll(values, 32, 1)


def gather_tile(tile, slots_ref, rels_ref, win_ref, rel_ref, message_ref, slot_total, unroll):
    def block(b, carry):
        base = tile * slot_total + b * unroll
        for u in range(unroll):
            slot = pl.multiple_of(slots_ref[base + u], 4)
            rel = pl.multiple_of(rels_ref[base + u], 4)
            place = pl.multiple_of((b * unroll + u) * 4, 4)
            message_ref[pl.ds(place, 4), :] = win_ref[pl.ds(slot, 4), :] * rel_ref[pl.ds(rel, 4), :]
        return carry

    lax.fori_loop(0, slot_total // unroll, block, 0)


def sum_messages(
    first_row, slots_ref, rels_ref, targets_ref, head_ref, query_ref, win_ref, rel_ref, message_ref, mixed_ref
):
    tiles, unused, slot_total = targets_ref.shape

    def tile_step(tile, carry):
        gather_tile(tile, slots_ref, rels_ref, win_ref, rel_ref, message_ref, slot_total, 32)
        onehot = (targets_ref[tile] == lax.broadcasted_iota(jnp.int32, (TILE, slot_total), 0)).astype(BF16)
        row = pl.multiple_of(tile * TILE, TILE)
        ids = first_row + row + lax.broadcasted_iota(jnp.int32, (TILE, LANES), 0)
        for c in range(4):
            cols = slice(c * LANES, (c + 1) * LANES)
            message = message_ref[pl.ds(c, slot_total, stride=4), :].astype(BF16)
            summed = jnp.dot(onehot, message, preferred_element_type=F32)
            start = jnp.where(ids == head_ref[:, cols], query_ref[:, cols], 0.0)
            mixed_ref[pl.ds(row, TILE), cols] = start + summed
        return carry

    lax.fori_loop(0, tiles, tile_step, 0)


def layer_zero_kernel(
    slots_ref, rels_ref, targets_ref, head_ref, query_ref, rel_in, low_ref, own_ref, high_ref, mirror_ref,
    weight_ref, bias_ref, state_out, mixed_out, slope_out, win_ref, rel_ref, message_ref, mixed_ref,
):
    rows = own_ref.shape[0]
    spread_relations(rel_ref, rel_in)
    for quarter, block in enumerate((low_ref, own_ref, high_ref, mirror_ref)):
        def fill(i, carry, quarter=quarter, block=block):
            at = pl.multiple_of(i * TILE, TILE)
            spread_rows(win_ref, quarter * rows + at, block[pl.ds(at, TILE), :].astype(F32))
            return carry

        lax.fori_loop(0, rows // TILE, fill, 0)
    first_row = lax.axis_index("node") * rows
    sum_messages(
        first_row, slots_ref, rels_ref, targets_ref, head_ref, query_ref, win_ref, rel_ref, message_ref, mixed_ref
    )
    weight_high, weight_low = split_pair(weight_ref[...])

    def finish(i, carry):
        at = pl.ds(pl.multiple_of(i * 256, 256), 256)
        for half in range(2):
            cols = slice(half * 256, half * 256 + 256)
            mixed = mixed_ref[at, cols]
            update = split_dot(mixed, weight_high, weight_low) + bias_ref[...]
            sigma = jax.nn.sigmoid(update)
            state_out[at, cols] = (own_ref[at, cols].astype(F32) + update * sigma).astype(BF16)
            slope_out[at, cols] = sigma * (1.0 + update * (1.0 - sigma))
            mixed_out[at, cols] = mixed.astype(BF16)
        return carry

    lax.fori_loop(0, rows // 256, finish, 0)


def layer_one_kernel(
    slots_ref, rels_ref, places_ref, targets_ref, head_ref, query_ref, rel_in, low_ref, own_ref, high_ref, mirror_ref,
    weight_ref, back_ref, bias_ref, cot_ref, state_out, own_out, low_out, high_out, mirror_out, sums_out,
    win_ref, second_ref, rel_ref, message_ref, mixed_ref, grad_ref,
):
    rows = own_ref.shape[0]
    spread_relations(rel_ref, rel_in)
    for quarter, block in enumerate((low_ref, own_ref, high_ref, mirror_ref)):
        def fill(i, carry, quarter=quarter, block=block):
            at = pl.multiple_of(i * TILE, TILE)
            spread_rows(win_ref, quarter * rows + at, block[pl.ds(at, TILE), :].astype(F32))
            return carry

        lax.fori_loop(0, rows // TILE, fill, 0)
    first_row = lax.axis_index("node") * rows
    sum_messages(
        first_row, slots_ref, rels_ref, targets_ref, head_ref, query_ref, win_ref, rel_ref, message_ref, mixed_ref
    )
    weight_high, weight_low = split_pair(weight_ref[...])
    back_high, back_low = split_pair(back_ref[...])

    def finish(i, carry):
        product, bias_sum = carry
        start = pl.multiple_of(i * 256, 256)
        at = pl.ds(start, 256)
        for half in range(2):
            cols = slice(half * 256, half * 256 + 256)
            mixed = mixed_ref[at, cols]
            update = split_dot(mixed, weight_high, weight_low) + bias_ref[...]
            sigma = jax.nn.sigmoid(update)
            state_out[at, cols] = (own_ref[at, cols].astype(F32) + update * sigma).astype(BF16)
            grad = cot_ref[at, cols].astype(F32) * (sigma * (1.0 + update * (1.0 - sigma)))
            back = split_dot(grad, back_high, back_low).astype(BF16).astype(F32)
            for c in range(2):
                grad_ref[pl.ds(start * 4 + half * 2 + c, 256, stride=4), :] = back[:, c * LANES : (c + 1) * LANES]
                part = slice(c * LANES, (c + 1) * LANES)
                product += lax.dot_general(
                    mixed[:, part].astype(BF16), grad[:, part].astype(BF16),
                    (((0,), (0,)), ((), ())), preferred_element_type=F32,
                )
                bias_sum += jnp.sum(grad[:, part], axis=0, keepdims=True)
        return product, bias_sum

    product, bias_sum = lax.fori_loop(
        0, rows // 256, finish, (jnp.zeros((LANES, LANES), F32), jnp.zeros((1, LANES), F32))
    )
    sums_out[0:8, :] = block_sums(product)
    sums_out[8:16, :] = jnp.broadcast_to(fold_lanes(jnp.broadcast_to(bias_sum, (8, LANES))), (8, LANES))

    def clear(i, carry):
        at = pl.ds(pl.multiple_of(i * 256, 256), 256)
        win_ref[at, :] = jnp.zeros((256, LANES), F32)
        second_ref[at, :] = jnp.zeros((256, LANES), F32)
        return carry

    lax.fori_loop(0, rows * 16 // 256, clear, 0)
    edges = slots_ref.shape[0]
    unroll = 16

    def scatter(b, carry):
        base = b * unroll
        for u in range(unroll):
            total = win_ref if u % 2 == 0 else second_ref
            slot = pl.multiple_of(slots_ref[base + u], 4)
            rel = pl.multiple_of(rels_ref[base + u], 4)
            place = pl.multiple_of(places_ref[base + u], 4)
            term = grad_ref[pl.ds(place, 4), :] * rel_ref[pl.ds(rel, 4), :]
            total[pl.ds(slot, 4), :] = total[pl.ds(slot, 4), :] + term
        return carry

    lax.fori_loop(0, edges // unroll, scatter, 0)
    for quarter, out in enumerate((low_out, own_out, high_out, mirror_out)):
        def collect(i, carry, quarter=quarter, out=out):
            start = pl.multiple_of(i * TILE, TILE)
            for c in range(4):
                at = pl.ds((quarter * rows + start) * 4 + c, TILE, stride=4)
                out[pl.ds(start, TILE), c * LANES : (c + 1) * LANES] = (win_ref[at, :] + second_ref[at, :]).astype(out.dtype)
            return carry

        lax.fori_loop(0, rows // TILE, collect, 0)


def last_kernel(
    cot_ref, own_ref, right_ref, left_ref, mirror_ref, slope_ref, mixed_ref, sums_ref,
    weight_out, bias_out, mine, first_buf, second_buf, first_send, first_recv, second_send, second_recv,
):
    node, query = lax.axis_index("node"), lax.axis_index("query")
    low_node = lax.rem(node, 16)
    half = node // 16
    in_first = half * 4 + query
    barrier = pltpu.get_barrier_semaphore()

    def first_peer(j):
        return {"node": (j // 4) * 16 + low_node, "query": lax.rem(j, 4)}

    def second_peer(j):
        return {"node": half * 16 + j, "query": query}

    for d in range(1, 8):
        pl.semaphore_signal(barrier, inc=1, device_id=first_peer(lax.rem(in_first + d, 8)), device_id_type=MESH)
    for d in range(1, 16):
        pl.semaphore_signal(barrier, inc=1, device_id=second_peer(lax.rem(low_node + d, 16)), device_id_type=MESH)

    rows = cot_ref.shape[0]

    def step(i, carry):
        product, bias_sum = carry
        at = pl.ds(pl.multiple_of(i * 256, 256), 256)
        for c in range(4):
            cols = slice(c * LANES, (c + 1) * LANES)
            state_grad = cot_ref[at, cols].astype(F32) + (
                own_ref[at, cols]
                + right_ref[at, cols].astype(F32)
                + left_ref[at, cols].astype(F32)
                + mirror_ref[at, cols].astype(F32)
            )
            grad = state_grad * slope_ref[at, cols]
            product += lax.dot_general(
                mixed_ref[at, cols], grad.astype(BF16), (((0,), (0,)), ((), ())), preferred_element_type=F32
            )
            bias_sum += jnp.sum(grad, axis=0, keepdims=True)
        return product, bias_sum

    product, bias_sum = lax.fori_loop(
        0, rows // 256, step, (jnp.zeros((LANES, LANES), F32), jnp.zeros((1, LANES), F32))
    )
    bias_zero = fold_lanes(jnp.broadcast_to(bias_sum, (8, LANES)))
    mine[0:8, :] = block_sums(product)
    mine[8:16, :] = sums_ref[0:8, :]
    sub = lax.broadcasted_iota(jnp.int32, (8, LANES), 0)
    mine[16:24, :] = jnp.where(sub == 0, bias_zero, sums_ref[8:16, :])

    pl.semaphore_wait(barrier, 22)

    def stage(buf, send, recv, me, peer, count):
        copies = []
        for d in range(1, count):
            to = lax.rem(me + d, count)
            copy = pltpu.make_async_remote_copy(
                src_ref=mine, dst_ref=buf.at[me], send_sem=send.at[to], recv_sem=recv.at[me],
                device_id=peer(to), device_id_type=MESH,
            )
            copy.start()
            copies.append(copy)
        buf[me] = mine[...]
        for d in range(1, count):
            source = lax.rem(me + d, count)
            pltpu.make_async_remote_copy(
                src_ref=mine, dst_ref=buf.at[source], send_sem=send.at[source], recv_sem=recv.at[source],
                device_id=peer(source), device_id_type=MESH,
            ).wait_recv()
        for copy in copies:
            copy.wait_send()
        total = buf[0]
        for j in range(1, count):
            total = total + buf[j]
        return total

    mine[...] = stage(first_buf, first_send, first_recv, in_first, first_peer, 8)
    total = stage(second_buf, second_send, second_recv, low_node, second_peer, 16)
    for l in range(2):
        packed = total[8 * l : 8 * l + 8, :]
        for k in range(4):
            moved = packed if k == 0 else pltpu.roll(packed, LANES - 32 * k, 1)
            weight_out[l, 8 * k : 8 * k + 8, :] = moved[:, 0:32]
    bias_out[...] = total[16:18, 0:32]


def ring_moves(block, mirror_bit):
    count = lax.axis_size("node")
    forward = [(i, (i + 1) % count) for i in range(count)]
    backward = [((i + 1) % count, i) for i in range(count)]
    low = lax.ppermute(block, "node", forward)
    high = lax.ppermute(block, "node", backward)
    return low, high, across(block, mirror_bit)


def across(block, mirror_bit):
    count = lax.axis_size("node")
    return lax.ppermute(block, "node", [(i, i ^ (1 << mirror_bit)) for i in range(count)])


def block_diagonal(matrix):
    size = 256
    at = lax.iota(jnp.int32, size) // DIM
    return jnp.where(at[:, None] == at[None, :], jnp.tile(matrix, (size // DIM, size // DIM)), 0.0)


def body(
    entity_state, edge_tiles, query_head, query_relation, query_table, rel_vectors, mix_weight, mix_bias, cotangent
):
    rows, cols = entity_state.shape
    tiles, unused, slot_total = edge_tiles.shape
    edges = tiles * slot_total
    mirror_bit = lax.axis_size("node").bit_length() - 2
    rel_rows = rel_vectors.shape[1]
    low, high, mirror = ring_moves(entity_state, mirror_bit)
    slots = (edge_tiles[:, 0, :] * 4).reshape(edges)
    rels = (edge_tiles[:, 2, :] * 4).reshape(edges)
    targets = edge_tiles[:, 1:2, :]
    places = ((edge_tiles[:, 1, :] + TILE * lax.iota(jnp.int32, tiles)[:, None]) * 4).reshape(edges)
    head = jnp.repeat(query_head, DIM)[None, :]
    query_vec = jnp.take(query_table, query_relation, axis=0).astype(BF16).astype(F32).reshape(1, cols)
    bias = jnp.tile(mix_bias, (1, 256 // DIM))
    smem = pl.BlockSpec(memory_space=pltpu.SMEM)
    vmem = pl.BlockSpec(memory_space=pltpu.VMEM)
    params = pltpu.CompilerParams(vmem_limit_bytes=VMEM_BYTES)
    scratch = [
        pltpu.VMEM((rows * 16, LANES), F32),
        pltpu.VMEM((rel_rows * 4, LANES), F32),
        pltpu.VMEM((slot_total * 4, LANES), F32),
        pltpu.VMEM((rows, cols), F32),
    ]
    full = jax.ShapeDtypeStruct((rows, cols), F32)
    half = jax.ShapeDtypeStruct((rows, cols), BF16)
    state_one, mixed_zero, slope_zero = pl.pallas_call(
        layer_zero_kernel,
        out_shape=(half, half, full),
        in_specs=[smem] * 2 + [vmem] * 10,
        out_specs=(vmem,) * 3,
        scratch_shapes=scratch,
        compiler_params=params,
        name="layer_zero",
    )(
        slots, rels, targets, head, query_vec, rel_vectors[0], low, entity_state, high, mirror,
        block_diagonal(mix_weight[0]), bias[0:1],
    )
    low, high, mirror = ring_moves(state_one, mirror_bit)
    state_two, own_terms, low_terms, high_terms, mirror_terms, sums = pl.pallas_call(
        layer_one_kernel,
        out_shape=(half, full, half, half, half, jax.ShapeDtypeStruct((16, LANES), F32)),
        in_specs=[smem] * 3 + [vmem] * 12,
        out_specs=(vmem,) * 6,
        scratch_shapes=[scratch[0]] + scratch + [pltpu.VMEM((rows * 4, LANES), F32)],
        compiler_params=params,
        name="layer_one",
    )(
        slots, rels, places, targets, head, query_vec, rel_vectors[1], low, state_one, high, mirror,
        block_diagonal(mix_weight[1]), block_diagonal(mix_weight[1].T), bias[1:2], cotangent,
    )
    count = lax.axis_size("node")
    from_right = lax.ppermute(low_terms, "node", [((i + 1) % count, i) for i in range(count)])
    from_left = lax.ppermute(high_terms, "node", [(i, (i + 1) % count) for i in range(count)])
    from_mirror = across(mirror_terms, mirror_bit)
    packet = (24, LANES)
    weight_grads, bias_grads = pl.pallas_call(
        last_kernel,
        out_shape=(jax.ShapeDtypeStruct((2, DIM, DIM), F32), jax.ShapeDtypeStruct((2, DIM), F32)),
        in_specs=[vmem] * 8,
        out_specs=(vmem,) * 2,
        scratch_shapes=[
            pltpu.VMEM(packet, F32),
            pltpu.VMEM((8,) + packet, F32),
            pltpu.VMEM((16,) + packet, F32),
            pltpu.SemaphoreType.DMA((8,)),
            pltpu.SemaphoreType.DMA((8,)),
            pltpu.SemaphoreType.DMA((16,)),
            pltpu.SemaphoreType.DMA((16,)),
        ],
        compiler_params=pltpu.CompilerParams(
            vmem_limit_bytes=VMEM_BYTES, collective_id=0, has_side_effects=True
        ),
        name="last_sums",
    )(cotangent, own_terms, from_right, from_left, from_mirror, slope_zero, mixed_zero, sums)
    return state_two, weight_grads, bias_grads


def solution(mesh):
    placed = (
        P("node", "query"),
        P("node", None, None),
        P("query"),
        P("query"),
        P(),
        P(),
        P(),
        P(),
        P("node", "query"),
    )
    return jax.shard_map(
        body, mesh=mesh, in_specs=placed, out_specs=(P("node", "query"), P(), P()), check_vma=False
    )
```

```python
import jax
import jax.numpy as jnp
from jax import lax
from jax.experimental import pallas as pl
from jax.experimental.pallas import tpu as pltpu
from jax.sharding import PartitionSpec as P

DIM = 32
LANES = 128
TILE = 64
CHUNK = 128
CHUNKS = 8
RING = 16
F32 = jnp.float32
BF16 = jnp.bfloat16
MESH = pl.DeviceIdType.MESH
VMEM_BYTES = 58 << 20


def split_pair(matrix):
    high = matrix.astype(BF16)
    return high, (matrix - high.astype(F32)).astype(BF16)


def split_dot(left, right_high, right_low, right_dim=0):
    dims = (((1,), (right_dim,)), ((), ()))
    high, low = split_pair(left)
    total = lax.dot_general(high, right_high, dims, preferred_element_type=F32)
    total += lax.dot_general(low, right_high, dims, preferred_element_type=F32)
    return total + lax.dot_general(high, right_low, dims, preferred_element_type=F32)


def spread_rows(target, first, block):
    rows, cols = block.shape
    flat = target.reshape(target.shape[0] * 4, LANES)
    for c in range(4):
        flat[pl.ds(first * 4 + c, rows, stride=4), :] = block[:, c * LANES : (c + 1) * LANES]


def spread_relations(target, columns_ref):
    count = columns_ref.shape[1]
    flat = target.reshape(target.shape[0] * 4, LANES)
    for start in range(0, count, LANES):
        width = min(LANES, count - start)
        wide = jnp.concatenate([columns_ref[:, start : start + width]] * 4, axis=0).T
        for c in range(4):
            flat[pl.ds(start * 4 + c, width, stride=4), :] = wide


def block_diagonal(matrix):
    row = jnp.concatenate([matrix] * 8, axis=1)
    wide = jnp.concatenate([row] * 8, axis=0)
    rows = lax.broadcasted_iota(jnp.int32, (256, 256), 0) // DIM
    cols = lax.broadcasted_iota(jnp.int32, (256, 256), 1) // DIM
    return jnp.where(rows == cols, wide, 0.0)


def fold_lanes(values):
    values = values + pltpu.roll(values, 64, 1)
    return values + pltpu.roll(values, 32, 1)


def block_sums(product):
    rows = lax.broadcasted_iota(jnp.int32, (LANES, LANES), 0) // DIM
    cols = lax.broadcasted_iota(jnp.int32, (LANES, LANES), 1) // DIM
    kept = jnp.where(rows == cols, product, 0.0)
    folded = fold_lanes(kept[0:32] + kept[32:64] + kept[64:96] + kept[96:128])
    lane = lax.broadcasted_iota(jnp.int32, (8, LANES), 1) // DIM
    packed = jnp.where(lane == 0, folded[0:8], 0.0)
    for k in range(1, 4):
        packed = jnp.where(lane == k, folded[8 * k : 8 * k + 8], packed)
    return packed


def product_of(left, right):
    return lax.dot_general(left, right, (((0,), (0,)), ((), ())), preferred_element_type=F32)


def chunk_rows(k):
    return pl.ds(pl.multiple_of(k * CHUNK, CHUNK), CHUNK)


def ring_targets():
    node = lax.axis_index("node")
    position = lax.rem(node, RING)
    plane = node - position
    after = plane + lax.rem(position + 1, RING)
    before = plane + lax.rem(position + RING - 1, RING)
    across = lax.rem(node + RING, 2 * RING)
    return node, position, (after, before, across)


def sum_chunk(k, first_row, edges_s, edges_v, head_ref, query_ref, win_ref, rel_ref, message_ref, mixed_ref):
    slot_total = edges_v.shape[2]
    unroll = 32

    def tile_step(j, carry):
        tile = 2 * k + j

        def block(b, carry):
            for u in range(unroll):
                at = b * unroll + u
                place = pl.multiple_of(at * 4, 4)
                message_ref[pl.ds(place, 4), :] = win_ref[edges_s[0, tile, at]] * rel_ref[edges_s[2, tile, at]]
            return carry

        lax.fori_loop(0, slot_total // unroll, block, 0)
        targets = edges_v[1, pl.ds(tile, 1), :]
        onehot = (targets == lax.broadcasted_iota(jnp.int32, (TILE, slot_total), 0)).astype(BF16)
        row = pl.multiple_of(j * TILE, TILE)
        ids = first_row + tile * TILE + lax.broadcasted_iota(jnp.int32, (TILE, LANES), 0)
        for c in range(4):
            cols = slice(c * LANES, (c + 1) * LANES)
            message = message_ref[pl.ds(c, slot_total, stride=4), :].astype(BF16)
            summed = jnp.dot(onehot, message, preferred_element_type=F32)
            start = jnp.where(ids == head_ref[:, cols], query_ref[:, cols], 0.0)
            mixed_ref[pl.ds(row, TILE), cols] = start + summed
        return carry

    lax.fori_loop(0, 2, tile_step, 0)


def forward_kernel(
    state_hbm, cot_hbm, edges_s, head_s, chosen_s, edges_v, table_t, rel_t, weight_ref, bias_ref,
    state_out, grad_out, mixed_out, slope_out, sums_out,
    own, middle, cot, inbox, win_a, win_b, rel_ref, table_ref, message_ref, mixed_ref, wide_ref, head_ref, query_ref,
    copy_sem, send_sem, recv_sem,
):
    node, position, targets = ring_targets()
    rows = own.shape[0]
    barrier = pltpu.get_barrier_semaphore()
    for target in targets:
        pl.semaphore_signal(barrier, inc=1, device_id={"node": target}, device_id_type=MESH)
    own_copy = pltpu.make_async_copy(state_hbm, own, copy_sem.at[0])
    cot_copy = pltpu.make_async_copy(cot_hbm, cot, copy_sem.at[1])
    own_copy.start()
    cot_copy.start()
    pl.semaphore_wait(barrier, 3)

    def piece(layer, way, k, source):
        return pltpu.make_async_remote_copy(
            src_ref=source.at[chunk_rows(k), :],
            dst_ref=inbox.at[layer, way, chunk_rows(k), :],
            send_sem=send_sem.at[layer, way, k],
            recv_sem=recv_sem.at[layer, way, k],
            device_id={"node": targets[way]},
            device_id_type=MESH,
        )

    def send_chunk(layer, k, source):
        piece(layer, 2, k, source).start()

        @pl.when(position != RING - 1)
        def _():
            piece(layer, 0, k, source).start()

        @pl.when(position != 0)
        def _():
            piece(layer, 1, k, source).start()

    def relay_chunk(layer, k):
        mirrored = inbox.at[layer, 2]
        piece(layer, 2, k, mirrored).wait_recv()

        @pl.when(position == RING - 1)
        def _():
            piece(layer, 0, k, mirrored).start()

        @pl.when(position == 0)
        def _():
            piece(layer, 1, k, mirrored).start()

    def fill(win, quarter, k, block):
        spread_rows(win, quarter * rows + k * CHUNK, block.astype(F32))

    def take_mirror(layer, win, k):
        relay_chunk(layer, k)
        fill(win, 3, k, inbox[layer, 2, chunk_rows(k), :])

    def take_sides(layer, win, k):
        for way, quarter in ((0, 0), (1, 2)):
            piece(layer, way, k, own).wait_recv()
            fill(win, quarter, k, inbox[layer, way, chunk_rows(k), :])

    def each(count, step):
        def run(i, carry):
            step(i)
            return carry

        lax.fori_loop(0, count, run, 0)

    each(CHUNKS, lambda k: send_chunk(0, k, state_hbm))

    spread_relations(table_ref, table_t)
    spread_relations(rel_ref, rel_t.at[0])
    lane = lax.broadcasted_iota(jnp.int32, (1, LANES), 1) // DIM
    for c in range(4):
        heads = jnp.zeros((1, LANES), jnp.int32)
        vectors = jnp.zeros((1, LANES), F32)
        for k in range(4):
            heads = jnp.where(lane == k, head_s[4 * c + k], heads)
            vectors = jnp.where(lane == k, table_ref[chosen_s[4 * c + k]][0:1], vectors)
        head_ref[:, c * LANES : (c + 1) * LANES] = heads
        query_ref[:, c * LANES : (c + 1) * LANES] = vectors.astype(BF16).astype(F32)
    for layer in range(2):
        high, low = split_pair(block_diagonal(weight_ref[layer]))
        wide_ref[2 * layer] = high
        wide_ref[2 * layer + 1] = low
    bias_zero = jnp.concatenate([bias_ref[0:1, :]] * 8, axis=1)
    bias_one = jnp.concatenate([bias_ref[1:2, :]] * 8, axis=1)
    first_row = node * rows

    own_copy.wait()
    each(CHUNKS, lambda k: fill(win_a, 1, k, own[chunk_rows(k), :]))
    each(CHUNKS, lambda k: take_mirror(0, win_a, k))
    each(CHUNKS, lambda k: take_sides(0, win_a, k))

    def zero_step(k):
        sum_chunk(k, first_row, edges_s, edges_v, head_ref, query_ref, win_a, rel_ref, message_ref, mixed_ref)
        at = chunk_rows(k)
        for half in range(2):
            cols = slice(half * 256, half * 256 + 256)
            mixed = mixed_ref[:, cols]
            update = split_dot(mixed, wide_ref[0], wide_ref[1]) + bias_zero
            sigma = jax.nn.sigmoid(update)
            middle[at, cols] = (own[at, cols].astype(F32) + update * sigma).astype(BF16)
            slope_out[at, cols] = sigma * (1.0 + update * (1.0 - sigma))
            mixed_out[at, cols] = mixed.astype(BF16)
        send_chunk(1, k, middle)
        fill(win_b, 1, k, middle[at, :])

        @pl.when(k >= 2)
        def _():
            take_mirror(1, win_b, k - 2)

    each(CHUNKS, zero_step)
    spread_relations(rel_ref, rel_t.at[1])
    each(2, lambda k: take_mirror(1, win_b, k + CHUNKS - 2))
    each(CHUNKS, lambda k: take_sides(1, win_b, k))
    cot_copy.wait()

    def one_step(k, carry):
        product, bias_sum = carry
        sum_chunk(k, first_row, edges_s, edges_v, head_ref, query_ref, win_b, rel_ref, message_ref, mixed_ref)
        at = chunk_rows(k)
        for half in range(2):
            cols = slice(half * 256, half * 256 + 256)
            mixed = mixed_ref[:, cols]
            update = split_dot(mixed, wide_ref[2], wide_ref[3]) + bias_one
            sigma = jax.nn.sigmoid(update)
            state_out[at, cols] = (middle[at, cols].astype(F32) + update * sigma).astype(BF16)
            grad = cot[at, cols].astype(F32) * (sigma * (1.0 + update * (1.0 - sigma)))
            back = split_dot(grad, wide_ref[2], wide_ref[3], 1).astype(BF16).astype(F32)
            for c in range(2):
                part = slice(c * LANES, (c + 1) * LANES)
                grad_out[pl.ds(k * CHUNK * 4 + half * 2 + c, CHUNK, stride=4), :] = back[:, part]
                product += product_of(mixed[:, part].astype(BF16), grad[:, part].astype(BF16))
                bias_sum += jnp.sum(grad[:, part], axis=0, keepdims=True)
        return product, bias_sum

    product, bias_sum = lax.fori_loop(
        0, CHUNKS, one_step, (jnp.zeros((LANES, LANES), F32), jnp.zeros((1, LANES), F32))
    )
    sums_out[0:8, :] = block_sums(product)
    sums_out[8:16, :] = fold_lanes(jnp.broadcast_to(bias_sum, (8, LANES)))
    for layer in range(2):
        for way in range(3):
            each(CHUNKS, lambda k: piece(layer, way, k, own).wait_send())


def scatter_kernel(
    state_in, edges_s, grad_ref, rel_t, state_out, own_out, low_out, high_out, mirror_out,
    first_ref, second_ref, rel_ref, copy_sem,
):
    state_copy = pltpu.make_async_copy(state_in, state_out, copy_sem)
    state_copy.start()
    rows = own_out.shape[0]
    spread_relations(rel_ref, rel_t.at[1])

    def clear(i, carry):
        at = pl.ds(pl.multiple_of(i * TILE, TILE), TILE)
        first_ref[at] = jnp.zeros((TILE, 4, LANES), F32)
        second_ref[at] = jnp.zeros((TILE, 4, LANES), F32)
        return carry

    lax.fori_loop(0, rows * 4 // TILE, clear, 0)
    tiles, slot_total = edges_s.shape[1:]
    unroll = 16

    def tile_step(tile, carry):
        def scatter(b, carry):
            for u in range(unroll):
                total = first_ref if u % 2 == 0 else second_ref
                at = b * unroll + u
                slot = edges_s[0, tile, at]
                place = pl.multiple_of((edges_s[1, tile, at] + tile * TILE) * 4, 4)
                total[slot] = total[slot] + grad_ref[pl.ds(place, 4), :] * rel_ref[edges_s[2, tile, at]]
            return carry

        lax.fori_loop(0, slot_total // unroll, scatter, 0)
        return carry

    lax.fori_loop(0, tiles, tile_step, 0)
    flat_first = first_ref.reshape(rows * 16, LANES)
    flat_second = second_ref.reshape(rows * 16, LANES)
    for quarter, out in enumerate((low_out, own_out, high_out, mirror_out)):
        def collect(i, carry, quarter=quarter, out=out):
            start = pl.multiple_of(i * TILE, TILE)
            for c in range(4):
                at = pl.ds((quarter * rows + start) * 4 + c, TILE, stride=4)
                out[pl.ds(start, TILE), c * LANES : (c + 1) * LANES] = (flat_first[at, :] + flat_second[at, :]).astype(
                    out.dtype
                )
            return carry

        lax.fori_loop(0, rows // TILE, collect, 0)
    state_copy.wait()


def last_kernel(
    low_ref, high_ref, mirror_ref, cot_ref, own_ref, slope_ref, mixed_ref, sums_ref,
    weight_out, bias_out,
    passed, inbox, mine, first_buf, second_buf, back_send, back_recv, first_send, first_recv, second_send, second_recv,
):
    node, position, (after, before, across) = ring_targets()
    query = lax.axis_index("query")
    half = node // RING
    in_first = half * 4 + query
    targets = (before, after, across)
    barrier = pltpu.get_barrier_semaphore()

    def first_peer(j):
        return {"node": (j // 4) * RING + position, "query": lax.rem(j, 4)}

    def second_peer(j):
        return {"node": half * RING + j, "query": query}

    for d in range(1, 8):
        pl.semaphore_signal(barrier, inc=1, device_id=first_peer(lax.rem(in_first + d, 8)), device_id_type=MESH)
    for d in range(1, RING):
        pl.semaphore_signal(barrier, inc=1, device_id=second_peer(lax.rem(position + d, RING)), device_id_type=MESH)
    pl.semaphore_wait(barrier, 22)

    def piece(way, k, source):
        return pltpu.make_async_remote_copy(
            src_ref=source.at[chunk_rows(k), :],
            dst_ref=inbox.at[way, chunk_rows(k), :],
            send_sem=back_send.at[way, k],
            recv_sem=back_recv.at[way, k],
            device_id={"node": targets[way]},
            device_id_type=MESH,
        )

    def each(count, step):
        def run(i, carry):
            step(i)
            return carry

        lax.fori_loop(0, count, run, 0)

    at_end = jnp.logical_or(position == 0, position == RING - 1)

    def send_sides(k):
        piece(0, k, low_ref).start()
        piece(1, k, high_ref).start()

        @pl.when(jnp.logical_not(at_end))
        def _():
            piece(2, k, mirror_ref).start()

    each(CHUNKS, send_sides)

    def relay(way, k):
        piece(way, k, low_ref).wait_recv()
        at = chunk_rows(k)
        passed[at, :] = (mirror_ref[at, :].astype(F32) + inbox[way, at, :].astype(F32)).astype(BF16)
        piece(2, k, passed).start()

    @pl.when(position == RING - 1)
    def _():
        each(CHUNKS, lambda k: relay(0, k))

    @pl.when(position == 0)
    def _():
        each(CHUNKS, lambda k: relay(1, k))

    def step(k, carry):
        product, bias_sum = carry

        @pl.when(position != RING - 1)
        def _():
            piece(0, k, low_ref).wait_recv()

        @pl.when(position != 0)
        def _():
            piece(1, k, low_ref).wait_recv()

        piece(2, k, low_ref).wait_recv()
        at = chunk_rows(k)
        for c in range(4):
            cols = slice(c * LANES, (c + 1) * LANES)
            from_after = jnp.where(position == RING - 1, 0.0, inbox[0, at, cols].astype(F32))
            from_before = jnp.where(position == 0, 0.0, inbox[1, at, cols].astype(F32))
            state_grad = cot_ref[at, cols].astype(F32) + (
                own_ref[at, cols] + from_after + from_before + inbox[2, at, cols].astype(F32)
            )
            grad = state_grad * slope_ref[at, cols]
            product += product_of(mixed_ref[at, cols], grad.astype(BF16))
            bias_sum += jnp.sum(grad, axis=0, keepdims=True)
        return product, bias_sum

    product, bias_sum = lax.fori_loop(
        0, CHUNKS, step, (jnp.zeros((LANES, LANES), F32), jnp.zeros((1, LANES), F32))
    )
    mine[0:8, :] = block_sums(product)
    mine[8:16, :] = sums_ref[0:8, :]
    sub = lax.broadcasted_iota(jnp.int32, (8, LANES), 0)
    mine[16:24, :] = jnp.where(sub == 0, fold_lanes(jnp.broadcast_to(bias_sum, (8, LANES))), sums_ref[8:16, :])

    def stage(buf, send, recv, me, peer, count):
        copies = []
        for d in range(1, count):
            to = lax.rem(me + d, count)
            copy = pltpu.make_async_remote_copy(
                src_ref=mine, dst_ref=buf.at[me], send_sem=send.at[to], recv_sem=recv.at[me],
                device_id=peer(to), device_id_type=MESH,
            )
            copy.start()
            copies.append(copy)
        buf[me] = mine[...]
        for d in range(1, count):
            source = lax.rem(me + d, count)
            pltpu.make_async_remote_copy(
                src_ref=mine, dst_ref=buf.at[source], send_sem=send.at[source], recv_sem=recv.at[source],
                device_id=peer(source), device_id_type=MESH,
            ).wait_recv()
        for copy in copies:
            copy.wait_send()
        total = buf[0]
        for j in range(1, count):
            total = total + buf[j]
        return total

    mine[...] = stage(first_buf, first_send, first_recv, in_first, first_peer, 8)
    total = stage(second_buf, second_send, second_recv, position, second_peer, RING)
    for l in range(2):
        packed = total[8 * l : 8 * l + 8, :]
        for k in range(4):
            moved = packed if k == 0 else pltpu.roll(packed, LANES - 32 * k, 1)
            weight_out[l, 8 * k : 8 * k + 8, :] = moved[:, 0:32]
    bias_out[...] = total[16:18, 0:32]
    for way in range(3):
        each(CHUNKS, lambda k: piece(way, k, low_ref).wait_send())


def body(
    entity_state, edge_tiles, query_head, query_relation, query_table, rel_vectors, mix_weight, mix_bias, cotangent
):
    rows, cols = entity_state.shape
    slot_total = edge_tiles.shape[2]
    rel_rows = rel_vectors.shape[1]
    edges = edge_tiles.transpose(1, 0, 2)
    table_t = query_table.T
    rel_t = rel_vectors.transpose(0, 2, 1)
    smem = pl.BlockSpec(memory_space=pltpu.SMEM)
    vmem = pl.BlockSpec(memory_space=pltpu.VMEM)
    anywhere = pl.BlockSpec(memory_space=pl.ANY)
    full = jax.ShapeDtypeStruct((rows, cols), F32)
    half = jax.ShapeDtypeStruct((rows, cols), BF16)
    tall = jax.ShapeDtypeStruct((rows * 4, LANES), F32)
    window = pltpu.VMEM((rows * 4, 4, LANES), F32)
    relations = pltpu.VMEM((rel_rows, 4, LANES), F32)
    state_two, grad_mixed, mixed_zero, slope_zero, sums = pl.pallas_call(
        forward_kernel,
        out_shape=(half, tall, half, full, jax.ShapeDtypeStruct((16, LANES), F32)),
        in_specs=[anywhere] * 2 + [smem] * 3 + [vmem] * 5,
        out_specs=(vmem,) * 5,
        scratch_shapes=[
            pltpu.VMEM((rows, cols), BF16),
            pltpu.VMEM((rows, cols), BF16),
            pltpu.VMEM((rows, cols), BF16),
            pltpu.VMEM((2, 3, rows, cols), BF16),
            window,
            window,
            relations,
            relations,
            pltpu.VMEM((slot_total * 4, LANES), F32),
            pltpu.VMEM((CHUNK, cols), F32),
            pltpu.VMEM((4, 256, 256), BF16),
            pltpu.VMEM((1, cols), jnp.int32),
            pltpu.VMEM((1, cols), F32),
            pltpu.SemaphoreType.DMA((2,)),
            pltpu.SemaphoreType.DMA((2, 3, CHUNKS)),
            pltpu.SemaphoreType.DMA((2, 3, CHUNKS)),
        ],
        compiler_params=pltpu.CompilerParams(
            vmem_limit_bytes=VMEM_BYTES, collective_id=0, has_side_effects=True
        ),
        name="two_layers",
    )(
        entity_state, cotangent, edges, query_head, query_relation, edges, table_t, rel_t, mix_weight, mix_bias
    )
    state_out, own_terms, low_terms, high_terms, mirror_terms = pl.pallas_call(
        scatter_kernel,
        out_shape=(half, full, half, half, half),
        in_specs=[anywhere, smem, vmem, vmem],
        out_specs=(anywhere,) + (vmem,) * 4,
        scratch_shapes=[window, window, relations, pltpu.SemaphoreType.DMA],
        compiler_params=pltpu.CompilerParams(vmem_limit_bytes=VMEM_BYTES),
        name="scatter_terms",
    )(state_two, edges, grad_mixed, rel_t)
    packet = (24, LANES)
    weight_grads, bias_grads = pl.pallas_call(
        last_kernel,
        out_shape=(jax.ShapeDtypeStruct((2, DIM, DIM), F32), jax.ShapeDtypeStruct((2, DIM), F32)),
        in_specs=[vmem] * 8,
        out_specs=(vmem,) * 2,
        scratch_shapes=[
            pltpu.VMEM((rows, cols), BF16),
            pltpu.VMEM((3, rows, cols), BF16),
            pltpu.VMEM(packet, F32),
            pltpu.VMEM((8,) + packet, F32),
            pltpu.VMEM((RING,) + packet, F32),
            pltpu.SemaphoreType.DMA((3, CHUNKS)),
            pltpu.SemaphoreType.DMA((3, CHUNKS)),
            pltpu.SemaphoreType.DMA((8,)),
            pltpu.SemaphoreType.DMA((8,)),
            pltpu.SemaphoreType.DMA((RING,)),
            pltpu.SemaphoreType.DMA((RING,)),
        ],
        compiler_params=pltpu.CompilerParams(
            vmem_limit_bytes=VMEM_BYTES, collective_id=1, has_side_effects=True
        ),
        name="last_sums",
    )(low_terms, high_terms, mirror_terms, cotangent, own_terms, slope_zero, mixed_zero, sums)
    return state_out, weight_grads, bias_grads


def solution(mesh):
    placed = (
        P("node", "query"),
        P("node", None, None),
        P("query"),
        P("query"),
        P(),
        P(),
        P(),
        P(),
        P("node", "query"),
    )
    return jax.shard_map(
        body, mesh=mesh, in_specs=placed, out_specs=(P("node", "query"), P(), P()), check_vma=False
    )
```

```python
import jax
import jax.numpy as jnp
from jax import lax
from jax.experimental import pallas as pl
from jax.experimental.pallas import tpu as pltpu
from jax.sharding import PartitionSpec as P

DIM = 32
LANES = 128
TILE = 64
CHUNK = 128
CHUNKS = 8
RING = 16
UNROLL = 32
F32 = jnp.float32
BF16 = jnp.bfloat16
MESH = pl.DeviceIdType.MESH
VMEM_BYTES = 58 << 20


def split_pair(matrix):
    high = matrix.astype(BF16)
    return high, (matrix - high.astype(F32)).astype(BF16)


def half_dot(left, right, right_dim):
    return lax.dot_general(left, right, (((1,), (right_dim,)), ((), ())), preferred_element_type=F32)


def split_dot(left, right_high, right_low, right_dim=0):
    high, low = split_pair(left)
    total = half_dot(high, right_high, right_dim) + half_dot(low, right_high, right_dim)
    return total + half_dot(high, right_low, right_dim)


def product_of(left, right):
    return lax.dot_general(left, right, (((0,), (0,)), ((), ())), preferred_element_type=F32)


def each(count, step):
    def run(i, carry):
        step(i)
        return carry

    lax.fori_loop(0, count, run, 0)


def flat(target):
    return target.reshape(target.shape[0] * 4, LANES)


def spread_rows(target, first, block):
    rows = block.shape[0]
    for c in range(4):
        flat(target)[pl.ds(first * 4 + c, rows, stride=4), :] = block[:, c * LANES : (c + 1) * LANES]


def spread_table(target, columns_ref):
    count = columns_ref.shape[1]
    for start in range(0, count, LANES):
        width = min(LANES, count - start)
        wide = jnp.concatenate([columns_ref[:, start : start + width]] * 4, axis=0).T
        for c in range(4):
            flat(target)[pl.ds(start * 4 + c, width, stride=4), :] = wide


def pad_columns(target, columns_ref):
    count = columns_ref.shape[1]
    whole = count // LANES * LANES
    target[:, 0:whole] = columns_ref[:, 0:whole]
    if whole < count:
        rest = jnp.zeros((columns_ref.shape[0], LANES - count + whole), F32)
        target[:, whole : whole + LANES] = jnp.concatenate([columns_ref[:, whole:count], rest], axis=1)


def relation_rows(target, table_ref, edges_v):
    parts = table_ref.shape[1] // LANES
    tiles, slot_total = edges_v.shape[1:]

    def tile_step(tile):
        row = edges_v[2, pl.ds(tile, 1), :]
        for q in range(slot_total // LANES):
            ids = jnp.broadcast_to(row[:, q * LANES : (q + 1) * LANES], (DIM, LANES))
            lane, part = lax.rem(ids, LANES), ids // LANES
            found = jnp.zeros((DIM, LANES), F32)
            for j in range(parts):
                columns = table_ref[:, j * LANES : (j + 1) * LANES]
                found = jnp.where(part == j, jnp.take_along_axis(columns, lane, axis=1), found)
            at = pl.multiple_of(tile * slot_total + q * LANES, LANES)
            target[pl.ds(at, LANES), :] = jnp.concatenate([found] * 4, axis=0).T

    each(tiles, tile_step)


def block_diagonal(matrix):
    row = jnp.concatenate([matrix] * 8, axis=1)
    wide = jnp.concatenate([row] * 8, axis=0)
    rows = lax.broadcasted_iota(jnp.int32, (256, 256), 0) // DIM
    cols = lax.broadcasted_iota(jnp.int32, (256, 256), 1) // DIM
    return jnp.where(rows == cols, wide, 0.0)


def fold_lanes(values):
    values = values + pltpu.roll(values, 64, 1)
    return values + pltpu.roll(values, 32, 1)


def block_sums(product):
    rows = lax.broadcasted_iota(jnp.int32, (LANES, LANES), 0) // DIM
    cols = lax.broadcasted_iota(jnp.int32, (LANES, LANES), 1) // DIM
    kept = jnp.where(rows == cols, product, 0.0)
    folded = fold_lanes(kept[0:32] + kept[32:64] + kept[64:96] + kept[96:128])
    lane = lax.broadcasted_iota(jnp.int32, (8, LANES), 1) // DIM
    packed = jnp.where(lane == 0, folded[0:8], 0.0)
    for k in range(1, 4):
        packed = jnp.where(lane == k, folded[8 * k : 8 * k + 8], packed)
    return packed


def chunk_rows(k):
    return pl.ds(pl.multiple_of(k * CHUNK, CHUNK), CHUNK)


def slot_base(tile, block):
    return (tile // 8 * 4 + block // 4) * 1024 + lax.rem(tile, 8) * LANES + lax.rem(block, 4) * UNROLL


def target_onehot(edges_v, tile):
    targets = edges_v[1, pl.ds(tile, 1), :]
    return (targets == lax.broadcasted_iota(jnp.int32, (TILE, targets.shape[1]), 0)).astype(BF16)


def ring_targets():
    node = lax.axis_index("node")
    position = lax.rem(node, RING)
    plane = node - position
    after = plane + lax.rem(position + 1, RING)
    before = plane + lax.rem(position + RING - 1, RING)
    across = lax.rem(node + RING, 2 * RING)
    return node, position, (after, before, across)


def sum_chunk(k, first_row, slots_s, edges_v, head_ref, query_ref, win_ref, rel_ref, message_ref, mixed_ref):
    slot_total = edges_v.shape[2]

    def tile_step(j):
        tile = 2 * k + j

        def block(b):
            base = slot_base(tile, b)
            for u in range(UNROLL):
                place = pl.multiple_of((b * UNROLL + u) * 4, 4)
                message_ref[pl.ds(place, 4), :] = win_ref[slots_s[base + u]]

        each(slot_total // UNROLL, block)
        onehot = target_onehot(edges_v, tile)
        row = pl.multiple_of(j * TILE, TILE)
        ids = first_row + tile * TILE + lax.broadcasted_iota(jnp.int32, (TILE, LANES), 0)
        scale = rel_ref[pl.ds(pl.multiple_of(tile * slot_total, slot_total), slot_total), :]
        for half in range(2):
            message = jnp.concatenate(
                [
                    (message_ref[pl.ds(2 * half + c, slot_total, stride=4), :] * scale).astype(BF16)
                    for c in range(2)
                ],
                axis=1,
            )
            summed = jnp.dot(onehot, message, preferred_element_type=F32)
            for c in range(2):
                cols = slice((2 * half + c) * LANES, (2 * half + c + 1) * LANES)
                start = jnp.where(ids == head_ref[:, cols], query_ref[:, cols], 0.0)
                mixed_ref[pl.ds(row, TILE), cols] = start + summed[:, c * LANES : (c + 1) * LANES]

    each(2, tile_step)


def forward_kernel(
    state_hbm, cot_hbm, slots_s, head_s, chosen_s, edges_v, table_t, rel_t, weight_ref, bias_ref,
    state_out, grad_out, mixed_out, slope_out, sums_out,
    own, middle, mixed_own, cot, inbox, win_a, win_b, rel_a, rel_b, padded, table_ref, message_ref, mixed_ref,
    wide_ref, head_ref, query_ref, copy_sem, send_sem, recv_sem,
):
    node, position, targets = ring_targets()
    rows = own.shape[0]
    barrier = pltpu.get_barrier_semaphore()
    for target in targets:
        pl.semaphore_signal(barrier, inc=1, device_id={"node": target}, device_id_type=MESH)
    own_copy = pltpu.make_async_copy(state_hbm, own, copy_sem.at[0])
    cot_copy = pltpu.make_async_copy(cot_hbm, cot, copy_sem.at[1])
    own_copy.start()
    cot_copy.start()
    pl.semaphore_wait(barrier, 3)

    def piece(trip, way, k, source):
        return pltpu.make_async_remote_copy(
            src_ref=source.at[chunk_rows(k), :],
            dst_ref=inbox.at[trip, way, chunk_rows(k), :],
            send_sem=send_sem.at[trip, way, k],
            recv_sem=recv_sem.at[trip, way, k],
            device_id={"node": targets[way]},
            device_id_type=MESH,
        )

    def send_chunk(trip, k, source):
        piece(trip, 2, k, source).start()

        @pl.when(position != RING - 1)
        def _():
            piece(trip, 0, k, source).start()

        @pl.when(position != 0)
        def _():
            piece(trip, 1, k, source).start()

    def relay_chunk(trip, k):
        mirrored = inbox.at[trip, 2]
        piece(trip, 2, k, mirrored).wait_recv()

        @pl.when(position == RING - 1)
        def _():
            piece(trip, 0, k, mirrored).start()

        @pl.when(position == 0)
        def _():
            piece(trip, 1, k, mirrored).start()

    def fill(win, quarter, k, block):
        spread_rows(win, quarter * rows + k * CHUNK, block.astype(F32))

    each(CHUNKS, lambda k: send_chunk(0, k, state_hbm))

    spread_table(table_ref, table_t)
    for layer, target in enumerate((rel_a, rel_b)):
        pad_columns(padded, rel_t.at[layer])
        relation_rows(target, padded, edges_v)
    lane = lax.broadcasted_iota(jnp.int32, (1, LANES), 1) // DIM
    for c in range(4):
        heads = jnp.zeros((1, LANES), jnp.int32)
        vectors = jnp.zeros((1, LANES), F32)
        for k in range(4):
            heads = jnp.where(lane == k, head_s[4 * c + k], heads)
            vectors = jnp.where(lane == k, table_ref[chosen_s[4 * c + k]][0:1], vectors)
        head_ref[:, c * LANES : (c + 1) * LANES] = heads
        query_ref[:, c * LANES : (c + 1) * LANES] = vectors.astype(BF16).astype(F32)
    for layer in range(2):
        high, low = split_pair(block_diagonal(weight_ref[layer]))
        wide_ref[2 * layer] = high
        wide_ref[2 * layer + 1] = low
    bias_zero = jnp.concatenate([bias_ref[0:1, :]] * 8, axis=1)
    bias_one = jnp.concatenate([bias_ref[1:2, :]] * 8, axis=1)
    first_row = node * rows

    own_copy.wait()
    each(CHUNKS, lambda k: fill(win_a, 1, k, own[chunk_rows(k), :]))

    def take_first_mirror(k):
        relay_chunk(0, k)
        fill(win_a, 3, k, inbox[0, 2, chunk_rows(k), :])

    def take_first_sides(k):
        for way, quarter in ((0, 0), (1, 2)):
            piece(0, way, k, own).wait_recv()
            fill(win_a, quarter, k, inbox[0, way, chunk_rows(k), :])

    each(CHUNKS, take_first_mirror)
    each(CHUNKS, take_first_sides)

    def next_state(state, update, quarter, k, half):
        sigma = jax.nn.sigmoid(update)
        place = pl.ds(pl.multiple_of(quarter * rows + k * CHUNK, CHUNK), CHUNK)
        slope_out[place, half * 256 : half * 256 + 256] = (sigma * (1.0 + update * (1.0 - sigma))).astype(BF16)
        result = (state.astype(F32) + update * sigma).astype(BF16)
        for c in range(2):
            flat(win_b)[pl.ds((quarter * rows + k * CHUNK) * 4 + half * 2 + c, CHUNK, stride=4), :] = result[
                :, c * LANES : (c + 1) * LANES
            ].astype(F32)
        return result

    def remote_state(way, quarter, k):
        at = chunk_rows(k)
        place = pl.ds(pl.multiple_of(quarter * rows + k * CHUNK, CHUNK), CHUNK)
        for half in range(2):
            cols = slice(half * 256, half * 256 + 256)
            mixed = inbox[1, way, at, cols]
            mixed_out[place, cols] = mixed
            update = half_dot(mixed, wide_ref[0], 0) + half_dot(mixed, wide_ref[1], 0) + bias_zero
            next_state(inbox[0, way, at, cols], update, quarter, k, half)

    def take_second_mirror(k):
        relay_chunk(1, k)
        remote_state(2, 3, k)

    def take_second_sides(k):
        for way, quarter in ((0, 0), (1, 2)):
            piece(1, way, k, own).wait_recv()
            remote_state(way, quarter, k)

    def zero_step(k):
        sum_chunk(k, first_row, slots_s, edges_v, head_ref, query_ref, win_a, rel_a, message_ref, mixed_ref)
        at = chunk_rows(k)
        mixed_own[at, :] = mixed_ref[...].astype(BF16)
        send_chunk(1, k, mixed_own)
        for half in range(2):
            cols = slice(half * 256, half * 256 + 256)
            update = split_dot(mixed_ref[:, cols], wide_ref[0], wide_ref[1]) + bias_zero
            middle[at, cols] = next_state(own[at, cols], update, 1, k, half)
        mixed_out[pl.ds(pl.multiple_of(rows + k * CHUNK, CHUNK), CHUNK), :] = mixed_own[at, :]

        @pl.when(k >= 3)
        def _():
            take_second_mirror(k - 3)

        @pl.when(k >= 5)
        def _():
            take_second_sides(k - 5)

    each(CHUNKS, zero_step)
    each(3, lambda k: take_second_mirror(k + CHUNKS - 3))
    each(5, lambda k: take_second_sides(k + CHUNKS - 5))
    cot_copy.wait()

    def one_step(k, carry):
        product, bias_sum = carry
        sum_chunk(k, first_row, slots_s, edges_v, head_ref, query_ref, win_b, rel_b, message_ref, mixed_ref)
        at = chunk_rows(k)
        for half in range(2):
            cols = slice(half * 256, half * 256 + 256)
            mixed = mixed_ref[:, cols]
            update = split_dot(mixed, wide_ref[2], wide_ref[3]) + bias_one
            sigma = jax.nn.sigmoid(update)
            state_out[at, cols] = (middle[at, cols].astype(F32) + update * sigma).astype(BF16)
            grad = cot[at, cols].astype(F32) * (sigma * (1.0 + update * (1.0 - sigma)))
            grad_out[at, cols] = split_dot(grad, wide_ref[2], wide_ref[3], 1).astype(BF16)
            for c in range(2):
                part = slice(c * LANES, (c + 1) * LANES)
                product += product_of(mixed[:, part].astype(BF16), grad[:, part].astype(BF16))
                bias_sum += jnp.sum(grad[:, part], axis=0, keepdims=True)
        return product, bias_sum

    product, bias_sum = lax.fori_loop(
        0, CHUNKS, one_step, (jnp.zeros((LANES, LANES), F32), jnp.zeros((1, LANES), F32))
    )
    sums_out[0:8, :] = block_sums(product)
    sums_out[8:16, :] = fold_lanes(jnp.broadcast_to(bias_sum, (8, LANES)))
    for trip in range(2):
        for way in range(3):
            each(CHUNKS, lambda k: piece(trip, way, k, own).wait_send())


def scatter_kernel(
    state_in, slots_s, edges_v, grad_ref, rel_t, mixed_ref, slope_ref, cot_ref, sums_in, state_out, sums_out,
    first_ref, second_ref, rel_ref, padded, term_ref, copy_sem,
):
    state_copy = pltpu.make_async_copy(state_in, state_out, copy_sem)
    state_copy.start()
    rows = cot_ref.shape[0]
    tiles, slot_total = edges_v.shape[1:]
    pad_columns(padded, rel_t.at[1])
    relation_rows(rel_ref, padded, edges_v)
    flat_first, flat_second = flat(first_ref), flat(second_ref)

    def clear(i):
        at = pl.ds(pl.multiple_of(i * 256, 256), 256)
        flat_first[at, :] = jnp.zeros((256, LANES), F32)
        flat_second[at, :] = jnp.zeros((256, LANES), F32)

    each(rows * 16 // 256, clear)

    def tile_step(tile):
        onehot = target_onehot(edges_v, tile)
        scale = rel_ref[pl.ds(pl.multiple_of(tile * slot_total, slot_total), slot_total), :]
        grads = grad_ref[pl.ds(pl.multiple_of(tile * TILE, TILE), TILE), :]
        for half in range(2):
            picked = product_of(onehot, grads[:, half * 256 : half * 256 + 256])
            for c in range(2):
                term_ref[pl.ds(2 * half + c, slot_total, stride=4), :] = picked[:, c * LANES : (c + 1) * LANES] * scale

        def block(b):
            base = slot_base(tile, b)
            for u in range(UNROLL):
                total = first_ref if u % 2 == 0 else second_ref
                slot = slots_s[base + u]
                place = pl.multiple_of((b * UNROLL + u) * 4, 4)
                total[slot] = total[slot] + term_ref[pl.ds(place, 4), :]

        each(slot_total // UNROLL, block)

    each(tiles, tile_step)

    def collect(i, carry):
        product, bias_sum = carry
        start = pl.multiple_of(i * CHUNK, CHUNK)
        at = pl.ds(start, CHUNK)
        own_rows = pl.ds(pl.multiple_of(lax.rem(i, CHUNKS) * CHUNK, CHUNK), CHUNK)
        mine = i // CHUNKS == 1
        for c in range(4):
            cols = slice(c * LANES, (c + 1) * LANES)
            place = pl.ds(start * 4 + c, CHUNK, stride=4)
            terms = flat_first[place, :] + flat_second[place, :]
            terms += jnp.where(mine, cot_ref[own_rows, cols].astype(F32), 0.0)
            grad = terms * slope_ref[at, cols].astype(F32)
            product += product_of(mixed_ref[at, cols], grad.astype(BF16))
            bias_sum += jnp.sum(grad, axis=0, keepdims=True)
        return product, bias_sum

    product, bias_sum = lax.fori_loop(
        0, 4 * CHUNKS, collect, (jnp.zeros((LANES, LANES), F32), jnp.zeros((1, LANES), F32))
    )
    sums_out[0:8, :] = block_sums(product)
    sums_out[8:16, :] = sums_in[0:8, :]
    sub = lax.broadcasted_iota(jnp.int32, (8, LANES), 0)
    sums_out[16:24, :] = jnp.where(sub == 0, fold_lanes(jnp.broadcast_to(bias_sum, (8, LANES))), sums_in[8:16, :])
    state_copy.wait()


def total_kernel(
    sums_ref, weight_out, bias_out, mine, first_buf, second_buf, first_send, first_recv, second_send, second_recv
):
    node = lax.axis_index("node")
    query = lax.axis_index("query")
    position = lax.rem(node, RING)
    half = node // RING
    in_first = half * 4 + query
    barrier = pltpu.get_barrier_semaphore()

    def first_peer(j):
        return {"node": (j // 4) * RING + position, "query": lax.rem(j, 4)}

    def second_peer(j):
        return {"node": half * RING + j, "query": query}

    for d in range(1, 8):
        pl.semaphore_signal(barrier, inc=1, device_id=first_peer(lax.rem(in_first + d, 8)), device_id_type=MESH)
    for d in range(1, RING):
        pl.semaphore_signal(barrier, inc=1, device_id=second_peer(lax.rem(position + d, RING)), device_id_type=MESH)
    pl.semaphore_wait(barrier, 22)

    def stage(source, buf, send, recv, me, peer, count):
        def piece(slot, to):
            return pltpu.make_async_remote_copy(
                src_ref=source, dst_ref=buf.at[slot], send_sem=send.at[to], recv_sem=recv.at[slot],
                device_id=peer(to), device_id_type=MESH,
            )

        others = [lax.rem(me + d, count) for d in range(1, count)]
        for to in others:
            piece(me, to).start()
        buf[me] = source[...]
        for other in others:
            piece(other, other).wait_recv()
        total = buf[0]
        for j in range(1, count):
            total = total + buf[j]
        return total, lambda: [piece(me, to).wait_send() for to in others]

    total, finish_first = stage(sums_ref, first_buf, first_send, first_recv, in_first, first_peer, 8)
    mine[...] = total
    total, finish_second = stage(mine, second_buf, second_send, second_recv, position, second_peer, RING)
    for l in range(2):
        packed = total[8 * l : 8 * l + 8, :]
        for k in range(4):
            moved = packed if k == 0 else pltpu.roll(packed, LANES - 32 * k, 1)
            weight_out[l, 8 * k : 8 * k + 8, :] = moved[:, 0:32]
    bias_out[...] = total[16:18, 0:32]
    finish_first()
    finish_second()


def body(
    entity_state, edge_tiles, query_head, query_relation, query_table, rel_vectors, mix_weight, mix_bias, cotangent
):
    rows, cols = entity_state.shape
    tiles, unused, slot_total = edge_tiles.shape
    edge_count = tiles * slot_total
    rel_rows = rel_vectors.shape[1]
    padded_rows = -(-rel_rows // LANES) * LANES
    edges = edge_tiles.transpose(1, 0, 2)
    slots = edges.reshape(3, tiles // 8, 8, slot_total // LANES, LANES).transpose(0, 1, 3, 2, 4).reshape(3 * edge_count)
    table_t = query_table.T
    rel_t = rel_vectors.transpose(0, 2, 1)
    smem = pl.BlockSpec(memory_space=pltpu.SMEM)
    vmem = pl.BlockSpec(memory_space=pltpu.VMEM)
    anywhere = pl.BlockSpec(memory_space=pl.ANY)
    half = jax.ShapeDtypeStruct((rows, cols), BF16)
    wide = jax.ShapeDtypeStruct((4 * rows, cols), BF16)
    packet = (24, LANES)
    block = pltpu.VMEM((rows, cols), BF16)
    window = pltpu.VMEM((rows * 4, 4, LANES), F32)
    edge_rows = pltpu.VMEM((edge_count, LANES), F32)
    padded = pltpu.VMEM((DIM, padded_rows), F32)
    message = pltpu.VMEM((slot_total * 4, LANES), F32)
    state_two, grad_mixed, mixed_zero, slope_zero, sums = pl.pallas_call(
        forward_kernel,
        out_shape=(half, half, wide, wide, jax.ShapeDtypeStruct((16, LANES), F32)),
        in_specs=[anywhere] * 2 + [smem] * 3 + [vmem] * 5,
        out_specs=(vmem,) * 5,
        scratch_shapes=[
            block,
            block,
            block,
            block,
            pltpu.VMEM((2, 3, rows, cols), BF16),
            window,
            window,
            edge_rows,
            edge_rows,
            padded,
            pltpu.VMEM((rel_rows, 4, LANES), F32),
            message,
            pltpu.VMEM((CHUNK, cols), F32),
            pltpu.VMEM((4, 256, 256), BF16),
            pltpu.VMEM((1, cols), jnp.int32),
            pltpu.VMEM((1, cols), F32),
            pltpu.SemaphoreType.DMA((2,)),
            pltpu.SemaphoreType.DMA((2, 3, CHUNKS)),
            pltpu.SemaphoreType.DMA((2, 3, CHUNKS)),
        ],
        compiler_params=pltpu.CompilerParams(
            vmem_limit_bytes=VMEM_BYTES, collective_id=0, has_side_effects=True
        ),
        name="two_layers",
    )(
        entity_state, cotangent, slots, query_head, query_relation, edges, table_t, rel_t, mix_weight, mix_bias
    )
    state_out, sums = pl.pallas_call(
        scatter_kernel,
        out_shape=(half, jax.ShapeDtypeStruct(packet, F32)),
        in_specs=[anywhere, smem] + [vmem] * 7,
        out_specs=(anywhere, vmem),
        scratch_shapes=[window, window, edge_rows, padded, message, pltpu.SemaphoreType.DMA],
        compiler_params=pltpu.CompilerParams(vmem_limit_bytes=VMEM_BYTES),
        name="scatter_terms",
    )(state_two, slots, edges, grad_mixed, rel_t, mixed_zero, slope_zero, cotangent, sums)
    weight_grads, bias_grads = pl.pallas_call(
        total_kernel,
        out_shape=(jax.ShapeDtypeStruct((2, DIM, DIM), F32), jax.ShapeDtypeStruct((2, DIM), F32)),
        in_specs=[vmem],
        out_specs=(vmem,) * 2,
        scratch_shapes=[
            pltpu.VMEM(packet, F32),
            pltpu.VMEM((8,) + packet, F32),
            pltpu.VMEM((RING,) + packet, F32),
            pltpu.SemaphoreType.DMA((8,)),
            pltpu.SemaphoreType.DMA((8,)),
            pltpu.SemaphoreType.DMA((RING,)),
            pltpu.SemaphoreType.DMA((RING,)),
        ],
        compiler_params=pltpu.CompilerParams(collective_id=1, has_side_effects=True),
        name="total_sums",
    )(sums)
    return state_out, weight_grads, bias_grads


def solution(mesh):
    placed = (
        P("node", "query"),
        P("node", None, None),
        P("query"),
        P("query"),
        P(),
        P(),
        P(),
        P(),
        P("node", "query"),
    )
    return jax.shard_map(
        body, mesh=mesh, in_specs=placed, out_specs=(P("node", "query"), P(), P()), check_vma=False
    )
```

```python
import jax
import jax.numpy as jnp
from jax import lax
from jax.experimental import pallas as pl
from jax.experimental.pallas import tpu as pltpu
from jax.sharding import PartitionSpec as P

DIM = 32
LANES = 128
TILE = 64
CHUNK = 128
CHUNKS = 8
RING = 16
WINDOW = 3
SUMS = 4
F32 = jnp.float32
BF16 = jnp.bfloat16
MESH = pl.DeviceIdType.MESH
VMEM_BYTES = 58 << 20


def split_pair(matrix):
    high = matrix.astype(BF16)
    return high, (matrix - high.astype(F32)).astype(BF16)


def half_dot(left, right, right_dim):
    return lax.dot_general(left, right, (((1,), (right_dim,)), ((), ())), preferred_element_type=F32)


def split_dot(left, right_high, right_low, right_dim=0):
    high, low = split_pair(left)
    total = half_dot(high, right_high, right_dim) + half_dot(low, right_high, right_dim)
    return total + half_dot(high, right_low, right_dim)


def product_of(left, right):
    return lax.dot_general(left, right, (((0,), (0,)), ((), ())), preferred_element_type=F32)


def each(count, step):
    def run(i, carry):
        step(i)
        return carry

    lax.fori_loop(0, count, run, 0)


def flat(target):
    return target.reshape(target.shape[0] * 4, LANES)


def spread_rows(target, first, block):
    rows = block.shape[0]
    for c in range(4):
        flat(target)[pl.ds(first * 4 + c, rows, stride=4), :] = block[:, c * LANES : (c + 1) * LANES]


def spread_table(target, columns_ref):
    count = columns_ref.shape[1]
    for start in range(0, count, LANES):
        width = min(LANES, count - start)
        wide = jnp.concatenate([columns_ref[:, start : start + width]] * 4, axis=0).T
        for c in range(4):
            flat(target)[pl.ds(start * 4 + c, width, stride=4), :] = wide


def pad_columns(target, columns_ref):
    count = columns_ref.shape[1]
    whole = count // LANES * LANES
    target[:, 0:whole] = columns_ref[:, 0:whole]
    if whole < count:
        rest = jnp.zeros((columns_ref.shape[0], LANES - count + whole), F32)
        target[:, whole : whole + LANES] = jnp.concatenate([columns_ref[:, whole:count], rest], axis=1)


def relation_rows(target, table_ref, edges_v):
    parts = table_ref.shape[1] // LANES
    tiles, slot_total = edges_v.shape[1:]

    def tile_step(tile):
        row = edges_v[2, pl.ds(tile, 1), :]
        for q in range(slot_total // LANES):
            ids = jnp.broadcast_to(row[:, q * LANES : (q + 1) * LANES], (DIM, LANES))
            lane, part = lax.rem(ids, LANES), ids // LANES
            found = jnp.zeros((DIM, LANES), F32)
            for j in range(parts):
                columns = table_ref[:, j * LANES : (j + 1) * LANES]
                found = jnp.where(part == j, jnp.take_along_axis(columns, lane, axis=1), found)
            at = pl.multiple_of(tile * slot_total + q * LANES, LANES)
            target[pl.ds(at, LANES), :] = jnp.concatenate([found] * 4, axis=0).T

    each(tiles, tile_step)


def block_diagonal(matrix):
    row = jnp.concatenate([matrix] * 8, axis=1)
    wide = jnp.concatenate([row] * 8, axis=0)
    rows = lax.broadcasted_iota(jnp.int32, (256, 256), 0) // DIM
    cols = lax.broadcasted_iota(jnp.int32, (256, 256), 1) // DIM
    return jnp.where(rows == cols, wide, 0.0)


def fold_lanes(values):
    values = values + pltpu.roll(values, 64, 1)
    return values + pltpu.roll(values, 32, 1)


def block_sums(product):
    rows = lax.broadcasted_iota(jnp.int32, (LANES, LANES), 0) // DIM
    cols = lax.broadcasted_iota(jnp.int32, (LANES, LANES), 1) // DIM
    kept = jnp.where(rows == cols, product, 0.0)
    folded = fold_lanes(kept[0:32] + kept[32:64] + kept[64:96] + kept[96:128])
    lane = lax.broadcasted_iota(jnp.int32, (8, LANES), 1) // DIM
    packed = jnp.where(lane == 0, folded[0:8], 0.0)
    for k in range(1, 4):
        packed = jnp.where(lane == k, folded[8 * k : 8 * k + 8], packed)
    return packed


def chunk_rows(k):
    return pl.ds(pl.multiple_of(k * CHUNK, CHUNK), CHUNK)


def slot_base(tile):
    return tile // 8 * 4096 + lax.rem(tile, 8) * LANES


def slot_step(edge):
    return edge // LANES * 1024 + edge % LANES


def target_onehot(edges_v, tile):
    targets = edges_v[1, pl.ds(tile, 1), :]
    return (targets == lax.broadcasted_iota(jnp.int32, (TILE, targets.shape[1]), 0)).astype(BF16)


def ring_targets():
    node = lax.axis_index("node")
    position = lax.rem(node, RING)
    plane = node - position
    after = plane + lax.rem(position + 1, RING)
    before = plane + lax.rem(position + RING - 1, RING)
    across = lax.rem(node + RING, 2 * RING)
    return node, position, (after, before, across)


def sum_chunk(k, first_row, slots_s, edges_v, head_ref, query_ref, win_ref, rel_ref, message_ref, mixed_ref):
    slot_total = edges_v.shape[2]

    def tile_step(j):
        tile = 2 * k + j

        base = slot_base(tile)
        for edge in range(slot_total):
            message_ref[4 * edge : 4 * edge + 4, :] = win_ref[slots_s[base + slot_step(edge)]]
        onehot = target_onehot(edges_v, tile)
        row = pl.multiple_of(j * TILE, TILE)
        ids = first_row + tile * TILE + lax.broadcasted_iota(jnp.int32, (TILE, LANES), 0)
        scale = rel_ref[pl.ds(pl.multiple_of(tile * slot_total, slot_total), slot_total), :]
        message = jnp.concatenate(
            [(message_ref[pl.ds(c, slot_total, stride=4), :] * scale).astype(BF16) for c in range(4)], axis=1
        )
        summed = jnp.dot(onehot, message, preferred_element_type=F32)
        for c in range(4):
            cols = slice(c * LANES, (c + 1) * LANES)
            start = jnp.where(ids == head_ref[:, cols], query_ref[:, cols], 0.0)
            mixed_ref[pl.ds(row, TILE), cols] = start + summed[:, cols]

    each(2, tile_step)


def forward_kernel(
    state_hbm, cot_hbm, slots_s, head_s, chosen_s, edges_v, table_t, rel_t, weight_ref, bias_ref,
    state_out, grad_out, mixed_out, slope_out, rel_out, sums_out, places_out,
    own, middle, mixed_own, cot, state_ref, grad_ref, slope_ref, inbox, win_a, win_b, rel_a, rel_b, padded, table_ref,
    message_ref, mixed_ref, wide_ref, head_ref, query_ref, copy_sem, send_sem, recv_sem,
):
    node, position, targets = ring_targets()
    at_end = jnp.logical_or(position == 0, position == RING - 1)
    rows = own.shape[0]
    barrier = pltpu.get_barrier_semaphore()
    for target in targets:
        pl.semaphore_signal(barrier, inc=1, device_id={"node": target}, device_id_type=MESH)
    own_copy = pltpu.make_async_copy(state_hbm, own, copy_sem.at[0])
    cot_copy = pltpu.make_async_copy(cot_hbm, cot, copy_sem.at[1])
    own_copy.start()
    cot_copy.start()
    pl.semaphore_wait(barrier, 3)

    def piece(trip, way, k, source):
        return pltpu.make_async_remote_copy(
            src_ref=source.at[chunk_rows(k), :],
            dst_ref=inbox.at[trip, way, chunk_rows(k), :],
            send_sem=send_sem.at[trip, way, k],
            recv_sem=recv_sem.at[trip, way, k],
            device_id={"node": targets[way]},
            device_id_type=MESH,
        )

    def send_sides(trip, k, source):
        @pl.when(position != RING - 1)
        def _():
            piece(trip, 0, k, source).start()

        @pl.when(position != 0)
        def _():
            piece(trip, 1, k, source).start()

    def relay_chunk(trip, k):
        mirrored = inbox.at[trip, 2]
        piece(trip, 2, k, mirrored).wait_recv()

        @pl.when(position == RING - 1)
        def _():
            piece(trip, 0, k, mirrored).start()

        @pl.when(position == 0)
        def _():
            piece(trip, 1, k, mirrored).start()

    def fill(win, quarter, k, block):
        spread_rows(win, quarter * rows + k * CHUNK, block.astype(F32))

    def start_first(k):
        send_sides(0, k, state_hbm)

        @pl.when(jnp.logical_or(jnp.logical_not(at_end), k < WINDOW))
        def _():
            piece(0, 2, k, state_hbm).start()

    each(CHUNKS, start_first)

    spread_table(table_ref, table_t)
    for layer, target in enumerate((rel_a, rel_b)):
        pad_columns(padded, rel_t.at[layer])
        relation_rows(target, padded, edges_v)
    rel_copy = pltpu.make_async_copy(rel_b, rel_out, copy_sem.at[2])
    rel_copy.start()
    places_out[...] = edges_v[0] * 4
    lane = lax.broadcasted_iota(jnp.int32, (1, LANES), 1) // DIM
    for c in range(4):
        heads = jnp.zeros((1, LANES), jnp.int32)
        vectors = jnp.zeros((1, LANES), F32)
        for k in range(4):
            heads = jnp.where(lane == k, head_s[4 * c + k], heads)
            vectors = jnp.where(lane == k, table_ref[chosen_s[4 * c + k]][0:1], vectors)
        head_ref[:, c * LANES : (c + 1) * LANES] = heads
        query_ref[:, c * LANES : (c + 1) * LANES] = vectors.astype(BF16).astype(F32)
    for layer in range(2):
        high, low = split_pair(block_diagonal(weight_ref[layer]))
        wide_ref[2 * layer] = high
        wide_ref[2 * layer + 1] = low
    bias_zero = jnp.concatenate([bias_ref[0:1, :]] * 8, axis=1)
    bias_one = jnp.concatenate([bias_ref[1:2, :]] * 8, axis=1)
    first_row = node * rows

    own_copy.wait()
    each(CHUNKS, lambda k: fill(win_a, 1, k, own[chunk_rows(k), :]))

    def take_first_mirror(k):
        relay_chunk(0, k)

        @pl.when(jnp.logical_and(at_end, k + WINDOW < CHUNKS))
        def _():
            piece(0, 2, k + WINDOW, state_hbm).start()

        fill(win_a, 3, k, inbox[0, 2, chunk_rows(k), :])

    def take_first_sides(k):
        for way, quarter in ((0, 0), (1, 2)):
            piece(0, way, k, own).wait_recv()
            fill(win_a, quarter, k, inbox[0, way, chunk_rows(k), :])

    each(CHUNKS, take_first_mirror)
    each(CHUNKS, take_first_sides)

    def next_state(state, update, quarter, k, half):
        sigma = jax.nn.sigmoid(update)
        place = pl.ds(pl.multiple_of(quarter * rows + k * CHUNK, CHUNK), CHUNK)
        slope_ref[place, half * 256 : half * 256 + 256] = (sigma * (1.0 + update * (1.0 - sigma))).astype(BF16)
        result = (state.astype(F32) + update * sigma).astype(BF16)
        for c in range(2):
            flat(win_b)[pl.ds((quarter * rows + k * CHUNK) * 4 + half * 2 + c, CHUNK, stride=4), :] = result[
                :, c * LANES : (c + 1) * LANES
            ].astype(F32)
        return result

    def remote_state(way, quarter, k):
        at = chunk_rows(k)
        for half in range(2):
            cols = slice(half * 256, half * 256 + 256)
            mixed = inbox[1, way, at, cols]
            update = half_dot(mixed, wide_ref[0], 0) + half_dot(mixed, wide_ref[1], 0) + bias_zero
            next_state(inbox[0, way, at, cols], update, quarter, k, half)

    def take_second_mirror(k):
        relay_chunk(1, k)
        remote_state(2, 3, k)

    def take_second_sides(k):
        for way, quarter in ((0, 0), (1, 2)):
            piece(1, way, k, own).wait_recv()
            remote_state(way, quarter, k)

    def zero_step(k):
        sum_chunk(k, first_row, slots_s, edges_v, head_ref, query_ref, win_a, rel_a, message_ref, mixed_ref)
        at = chunk_rows(k)
        mixed_own[at, :] = mixed_ref[...].astype(BF16)
        piece(1, 2, k, mixed_own).start()
        send_sides(1, k, mixed_own)
        for half in range(2):
            cols = slice(half * 256, half * 256 + 256)
            update = split_dot(mixed_ref[:, cols], wide_ref[0], wide_ref[1]) + bias_zero
            middle[at, cols] = next_state(own[at, cols], update, 1, k, half)
        @pl.when(k >= 3)
        def _():
            take_second_mirror(k - 3)

        @pl.when(k >= 5)
        def _():
            take_second_sides(k - 5)

    each(CHUNKS, zero_step)
    each(3, lambda k: take_second_mirror(k + CHUNKS - 3))
    each(5, lambda k: take_second_sides(k + CHUNKS - 5))
    cot_copy.wait()
    window_copies = [pltpu.make_async_copy(slope_ref, slope_out, copy_sem.at[3])]
    for quarter, source in enumerate((inbox.at[1, 0], mixed_own, inbox.at[1, 1], inbox.at[1, 2])):
        window_copies.append(
            pltpu.make_async_copy(source, mixed_out.at[pl.ds(quarter * rows, rows), :], copy_sem.at[4 + quarter])
        )
    for copy in window_copies:
        copy.start()

    def result_copies(k):
        at = chunk_rows(k)
        return (
            pltpu.make_async_copy(state_ref.at[at, :], state_out.at[at, :], copy_sem.at[8 + 2 * k]),
            pltpu.make_async_copy(grad_ref.at[at, :], grad_out.at[at, :], copy_sem.at[9 + 2 * k]),
        )

    def one_step(k, carry):
        product, bias_sum = carry
        sum_chunk(k, first_row, slots_s, edges_v, head_ref, query_ref, win_b, rel_b, message_ref, mixed_ref)
        at = chunk_rows(k)
        for half in range(2):
            cols = slice(half * 256, half * 256 + 256)
            mixed = mixed_ref[:, cols]
            update = split_dot(mixed, wide_ref[2], wide_ref[3]) + bias_one
            sigma = jax.nn.sigmoid(update)
            state_ref[at, cols] = (middle[at, cols].astype(F32) + update * sigma).astype(BF16)
            grad = cot[at, cols].astype(F32) * (sigma * (1.0 + update * (1.0 - sigma)))
            grad_ref[at, cols] = split_dot(grad, wide_ref[2], wide_ref[3], 1).astype(BF16)
            for c in range(2):
                part = slice(c * LANES, (c + 1) * LANES)
                product += product_of(mixed[:, part].astype(BF16), grad[:, part].astype(BF16))
                bias_sum += jnp.sum(grad[:, part], axis=0, keepdims=True)
        for copy in result_copies(k):
            copy.start()
        return product, bias_sum

    product, bias_sum = lax.fori_loop(
        0, CHUNKS, one_step, (jnp.zeros((LANES, LANES), F32), jnp.zeros((1, LANES), F32))
    )
    sums_out[0:8, :] = block_sums(product)
    sums_out[8:16, :] = fold_lanes(jnp.broadcast_to(bias_sum, (8, LANES)))
    for trip in range(2):
        for way in range(3):
            each(CHUNKS, lambda k: piece(trip, way, k, own).wait_send())
    rel_copy.wait()
    for copy in window_copies:
        copy.wait()
    each(CHUNKS, lambda k: [copy.wait() for copy in result_copies(k)])


def scatter_kernel(
    state_in, mixed_in, slope_in, rel_in, places_s, edges_v, grad_ref, cot_ref, sums_in, state_out, sums_out,
    first_ref, second_ref, third_ref, fourth_ref, rel_ref, mixed_ref, slope_ref, term_ref, copy_sem,
):
    copies = [
        pltpu.make_async_copy(source, target, copy_sem.at[i])
        for i, (source, target) in enumerate(
            ((rel_in, rel_ref), (state_in, state_out), (mixed_in, mixed_ref), (slope_in, slope_ref))
        )
    ]
    for copy in copies:
        copy.start()
    totals = (first_ref, second_ref, third_ref, fourth_ref)
    tiles, slot_total = edges_v.shape[1:]
    half_total = slot_total // 2

    def clear(i):
        at = pl.ds(pl.multiple_of(i * 256, 256), 256)
        for total in totals:
            total[at, :] = jnp.zeros((256, LANES), F32)

    each(first_ref.shape[0] // 256, clear)
    copies[0].wait()

    def make_terms(tile, half):
        edges = slice(half * half_total, half * half_total + half_total)
        onehot = target_onehot(edges_v, tile)[:, edges]
        start = pl.multiple_of(tile * slot_total + half * half_total, half_total)
        scale = rel_ref[pl.ds(start, half_total), :]
        picked = product_of(onehot, grad_ref[pl.ds(pl.multiple_of(tile * TILE, TILE), TILE), :])
        for c in range(4):
            place = pl.ds(4 * half * half_total + c, half_total, stride=4)
            term_ref[place, :] = picked[:, c * LANES : (c + 1) * LANES] * scale

    def add_terms(tile, half):
        base = slot_base(tile)
        for edge in range(half * half_total, (half + 1) * half_total):
            total = totals[edge % SUMS]
            place = pl.ds(pl.multiple_of(places_s[base + slot_step(edge)], 4), 4)
            total[place, :] = total[place, :] + term_ref[4 * edge : 4 * edge + 4, :]

    make_terms(0, 0)

    def tile_step(tile):
        add_terms(tile, 0)
        make_terms(tile, 1)
        add_terms(tile, 1)
        make_terms(jnp.minimum(tile + 1, tiles - 1), 0)

    each(tiles, tile_step)
    for copy in copies[1:]:
        copy.wait()

    def collect(i, carry):
        product, bias_sum = carry
        start = pl.multiple_of(i * CHUNK, CHUNK)
        at = pl.ds(start, CHUNK)
        own_rows = pl.ds(pl.multiple_of(lax.rem(i, CHUNKS) * CHUNK, CHUNK), CHUNK)
        mine = i // CHUNKS == 1
        for c in range(4):
            cols = slice(c * LANES, (c + 1) * LANES)
            place = pl.ds(start * 4 + c, CHUNK, stride=4)
            terms = (first_ref[place, :] + second_ref[place, :]) + (third_ref[place, :] + fourth_ref[place, :])
            terms += jnp.where(mine, cot_ref[own_rows, cols].astype(F32), 0.0)
            grad = terms * slope_ref[at, cols].astype(F32)
            product += product_of(mixed_ref[at, cols], grad.astype(BF16))
            bias_sum += jnp.sum(grad, axis=0, keepdims=True)
        return product, bias_sum

    product, bias_sum = lax.fori_loop(
        0, 4 * CHUNKS, collect, (jnp.zeros((LANES, LANES), F32), jnp.zeros((1, LANES), F32))
    )
    sums_out[0:8, :] = block_sums(product)
    sums_out[8:16, :] = sums_in[0:8, :]
    sub = lax.broadcasted_iota(jnp.int32, (8, LANES), 0)
    sums_out[16:24, :] = jnp.where(sub == 0, fold_lanes(jnp.broadcast_to(bias_sum, (8, LANES))), sums_in[8:16, :])


def total_kernel(
    sums_ref, weight_out, bias_out, mine, first_buf, second_buf, first_send, first_recv, second_send, second_recv
):
    node = lax.axis_index("node")
    query = lax.axis_index("query")
    position = lax.rem(node, RING)
    half = node // RING
    in_first = half * 4 + query
    barrier = pltpu.get_barrier_semaphore()

    def first_peer(j):
        return {"node": (j // 4) * RING + position, "query": lax.rem(j, 4)}

    def second_peer(j):
        return {"node": half * RING + j, "query": query}

    for d in range(1, 8):
        pl.semaphore_signal(barrier, inc=1, device_id=first_peer(lax.rem(in_first + d, 8)), device_id_type=MESH)
    for d in range(1, RING):
        pl.semaphore_signal(barrier, inc=1, device_id=second_peer(lax.rem(position + d, RING)), device_id_type=MESH)
    pl.semaphore_wait(barrier, 22)

    def stage(source, buf, send, recv, me, peer, count):
        def piece(slot, to):
            return pltpu.make_async_remote_copy(
                src_ref=source, dst_ref=buf.at[slot], send_sem=send.at[to], recv_sem=recv.at[slot],
                device_id=peer(to), device_id_type=MESH,
            )

        others = [lax.rem(me + d, count) for d in range(1, count)]
        for to in others:
            piece(me, to).start()
        buf[me] = source[...]
        for other in others:
            piece(other, other).wait_recv()
        total = buf[0]
        for j in range(1, count):
            total = total + buf[j]
        return total, lambda: [piece(me, to).wait_send() for to in others]

    total, finish_first = stage(sums_ref, first_buf, first_send, first_recv, in_first, first_peer, 8)
    mine[...] = total
    total, finish_second = stage(mine, second_buf, second_send, second_recv, position, second_peer, RING)
    for l in range(2):
        packed = total[8 * l : 8 * l + 8, :]
        for k in range(4):
            moved = packed if k == 0 else pltpu.roll(packed, LANES - 32 * k, 1)
            weight_out[l, 8 * k : 8 * k + 8, :] = moved[:, 0:32]
    bias_out[...] = total[16:18, 0:32]
    finish_first()
    finish_second()


def in_memory_order(table):
    cols = table.shape[-1]
    return table.reshape(-1, 8, cols // LANES, LANES).transpose(0, 2, 1, 3).reshape(table.size)


def body(
    entity_state, edge_tiles, query_head, query_relation, query_table, rel_vectors, mix_weight, mix_bias, cotangent
):
    rows, cols = entity_state.shape
    tiles, unused, slot_total = edge_tiles.shape
    edge_count = tiles * slot_total
    rel_rows = rel_vectors.shape[1]
    padded_rows = -(-rel_rows // LANES) * LANES
    edges = edge_tiles.transpose(1, 0, 2)
    slots = in_memory_order(edges)
    table_t = query_table.T
    rel_t = rel_vectors.transpose(0, 2, 1)
    smem = pl.BlockSpec(memory_space=pltpu.SMEM)
    vmem = pl.BlockSpec(memory_space=pltpu.VMEM)
    anywhere = pl.BlockSpec(memory_space=pl.ANY)
    half = jax.ShapeDtypeStruct((rows, cols), BF16)
    wide = jax.ShapeDtypeStruct((4 * rows, cols), BF16)
    packet = (24, LANES)
    block = pltpu.VMEM((rows, cols), BF16)
    window = pltpu.VMEM((rows * 4, 4, LANES), F32)
    edge_rows = pltpu.VMEM((edge_count, LANES), F32)
    padded = pltpu.VMEM((DIM, padded_rows), F32)
    message = pltpu.VMEM((slot_total * 4, LANES), F32)
    state_two, grad_mixed, mixed_zero, slope_zero, rel_one, sums, places = pl.pallas_call(
        forward_kernel,
        out_shape=(
            half,
            half,
            wide,
            wide,
            jax.ShapeDtypeStruct((edge_count, LANES), F32),
            jax.ShapeDtypeStruct((16, LANES), F32),
            jax.ShapeDtypeStruct((tiles, slot_total), jnp.int32),
        ),
        in_specs=[anywhere] * 2 + [smem] * 3 + [vmem] * 5,
        out_specs=(anywhere,) * 5 + (vmem,) * 2,
        scratch_shapes=[block] * 6
        + [
            pltpu.VMEM((4 * rows, cols), BF16),
            pltpu.VMEM((2, 3, rows, cols), BF16),
            window,
            window,
            edge_rows,
            edge_rows,
            padded,
            pltpu.VMEM((rel_rows, 4, LANES), F32),
            message,
            pltpu.VMEM((CHUNK, cols), F32),
            pltpu.VMEM((4, 256, 256), BF16),
            pltpu.VMEM((1, cols), jnp.int32),
            pltpu.VMEM((1, cols), F32),
            pltpu.SemaphoreType.DMA((8 + 2 * CHUNKS,)),
            pltpu.SemaphoreType.DMA((2, 3, CHUNKS)),
            pltpu.SemaphoreType.DMA((2, 3, CHUNKS)),
        ],
        compiler_params=pltpu.CompilerParams(
            vmem_limit_bytes=VMEM_BYTES, collective_id=0, has_side_effects=True
        ),
        name="two_layers",
    )(
        entity_state, cotangent, slots, query_head, query_relation, edges, table_t, rel_t, mix_weight, mix_bias
    )
    state_out, sums = pl.pallas_call(
        scatter_kernel,
        out_shape=(half, jax.ShapeDtypeStruct(packet, F32)),
        in_specs=[anywhere] * 4 + [smem] + [vmem] * 4,
        out_specs=(anywhere, vmem),
        scratch_shapes=[pltpu.VMEM((rows * 16, LANES), F32)] * SUMS
        + [
            edge_rows,
            pltpu.VMEM((4 * rows, cols), BF16),
            pltpu.VMEM((4 * rows, cols), BF16),
            message,
            pltpu.SemaphoreType.DMA((4,)),
        ],
        compiler_params=pltpu.CompilerParams(vmem_limit_bytes=VMEM_BYTES),
        name="scatter_terms",
    )(state_two, mixed_zero, slope_zero, rel_one, in_memory_order(places), edges, grad_mixed, cotangent, sums)
    weight_grads, bias_grads = pl.pallas_call(
        total_kernel,
        out_shape=(jax.ShapeDtypeStruct((2, DIM, DIM), F32), jax.ShapeDtypeStruct((2, DIM), F32)),
        in_specs=[vmem],
        out_specs=(vmem,) * 2,
        scratch_shapes=[
            pltpu.VMEM(packet, F32),
            pltpu.VMEM((8,) + packet, F32),
            pltpu.VMEM((RING,) + packet, F32),
            pltpu.SemaphoreType.DMA((8,)),
            pltpu.SemaphoreType.DMA((8,)),
            pltpu.SemaphoreType.DMA((RING,)),
            pltpu.SemaphoreType.DMA((RING,)),
        ],
        compiler_params=pltpu.CompilerParams(collective_id=1, has_side_effects=True),
        name="total_sums",
    )(sums)
    return state_out, weight_grads, bias_grads


def solution(mesh):
    placed = (
        P("node", "query"),
        P("node", None, None),
        P("query"),
        P("query"),
        P(),
        P(),
        P(),
        P(),
        P("node", "query"),
    )
    return jax.shard_map(
        body, mesh=mesh, in_specs=placed, out_specs=(P("node", "query"), P(), P()), check_vma=False
    )
```

```python
import functools

import jax
import jax.numpy as jnp
from jax import lax
from jax.experimental import pallas as pl
from jax.experimental.pallas import tpu as pltpu
from jax.sharding import PartitionSpec as P

DIM = 32
LANES = 128
TILE = 64
CHUNK = 128
CHUNKS = 8
RING = 16
WINDOW = 3
SUMS = 4
COLLECT = 512
F32 = jnp.float32
BF16 = jnp.bfloat16
MESH = pl.DeviceIdType.MESH
VMEM_BYTES = 58 << 20


def split_pair(matrix):
    high = matrix.astype(BF16)
    return high, (matrix - high.astype(F32)).astype(BF16)


def half_dot(left, right, right_dim):
    return lax.dot_general(left, right, (((1,), (right_dim,)), ((), ())), preferred_element_type=F32)


def split_dot(left, right_high, right_low, right_dim=0):
    high, low = split_pair(left)
    total = half_dot(high, right_high, right_dim) + half_dot(low, right_high, right_dim)
    return total + half_dot(high, right_low, right_dim)


def product_of(left, right):
    return lax.dot_general(left, right, (((0,), (0,)), ((), ())), preferred_element_type=F32)


def each(count, step):
    def run(i, carry):
        step(i)
        return carry

    lax.fori_loop(0, count, run, 0)


def flat(target):
    return target.reshape(target.shape[0] * 4, LANES)


def spread_rows(target, first, block):
    rows = block.shape[0]
    for c in range(4):
        flat(target)[pl.ds(first * 4 + c, rows, stride=4), :] = block[:, c * LANES : (c + 1) * LANES]


def spread_table(target, columns_ref):
    count = columns_ref.shape[1]
    for start in range(0, count, LANES):
        width = min(LANES, count - start)
        wide = jnp.concatenate([columns_ref[:, start : start + width]] * 4, axis=0).T
        for c in range(4):
            flat(target)[pl.ds(start * 4 + c, width, stride=4), :] = wide


def pad_columns(target, columns_ref):
    count = columns_ref.shape[1]
    whole = count // LANES * LANES
    target[:, 0:whole] = columns_ref[:, 0:whole]
    if whole < count:
        rest = jnp.zeros((columns_ref.shape[0], LANES - count + whole), F32)
        target[:, whole : whole + LANES] = jnp.concatenate([columns_ref[:, whole:count], rest], axis=1)


def relation_rows(target, table_ref, edges_v, tile):
    slot_total = edges_v.shape[2]
    row = edges_v[2, pl.ds(tile, 1), :]
    for q in range(slot_total // LANES):
        ids = jnp.broadcast_to(row[:, q * LANES : (q + 1) * LANES], (DIM, LANES))
        lane, part = ids & (LANES - 1), ids >> 7
        found = jnp.zeros((DIM, LANES), F32)
        for j in range(table_ref.shape[1] // LANES):
            columns = table_ref[:, j * LANES : (j + 1) * LANES]
            found = jnp.where(part == j, jnp.take_along_axis(columns, lane, axis=1), found)
        at = pl.multiple_of(tile * slot_total + q * LANES, LANES)
        target[pl.ds(at, LANES), :] = jnp.concatenate([found] * 4, axis=0).T


def block_diagonal(matrix):
    row = jnp.concatenate([matrix] * 8, axis=1)
    wide = jnp.concatenate([row] * 8, axis=0)
    rows = lax.broadcasted_iota(jnp.int32, (256, 256), 0) // DIM
    cols = lax.broadcasted_iota(jnp.int32, (256, 256), 1) // DIM
    return jnp.where(rows == cols, wide, 0.0)


def fold_lanes(values):
    values = values + pltpu.roll(values, 64, 1)
    return values + pltpu.roll(values, 32, 1)


def block_sums(product):
    rows = lax.broadcasted_iota(jnp.int32, (LANES, LANES), 0) // DIM
    cols = lax.broadcasted_iota(jnp.int32, (LANES, LANES), 1) // DIM
    kept = jnp.where(rows == cols, product, 0.0)
    folded = fold_lanes(kept[0:32] + kept[32:64] + kept[64:96] + kept[96:128])
    lane = lax.broadcasted_iota(jnp.int32, (8, LANES), 1) // DIM
    packed = jnp.where(lane == 0, folded[0:8], 0.0)
    for k in range(1, 4):
        packed = jnp.where(lane == k, folded[8 * k : 8 * k + 8], packed)
    return packed


def chunk_rows(k):
    return pl.ds(pl.multiple_of(k * CHUNK, CHUNK), CHUNK)


def slot_base(tile):
    return tile // 8 * 4096 + lax.rem(tile, 8) * LANES


def slot_step(edge):
    return edge // LANES * 1024 + edge % LANES


def target_onehot(edges_v, tile):
    targets = edges_v[1, pl.ds(tile, 1), :]
    return (targets == lax.broadcasted_iota(jnp.int32, (TILE, targets.shape[1]), 0)).astype(BF16)


def ring_targets():
    node = lax.axis_index("node")
    position = lax.rem(node, RING)
    plane = node - position
    after = plane + lax.rem(position + 1, RING)
    before = plane + lax.rem(position + RING - 1, RING)
    across = lax.rem(node + RING, 2 * RING)
    return node, position, (after, before, across)


def sum_chunk(k, first_row, slots_s, edges_v, head_ref, query_ref, win_ref, rel_ref, message_ref, mixed_ref):
    slot_total = edges_v.shape[2]

    def tile_step(j):
        tile = 2 * k + j

        base = slot_base(tile)
        for edge in range(slot_total):
            message_ref[4 * edge : 4 * edge + 4, :] = win_ref[slots_s[base + slot_step(edge)]]
        onehot = target_onehot(edges_v, tile)
        row = pl.multiple_of(j * TILE, TILE)
        ids = first_row + tile * TILE + lax.broadcasted_iota(jnp.int32, (TILE, LANES), 0)
        scale = rel_ref[pl.ds(pl.multiple_of(tile * slot_total, slot_total), slot_total), :]
        message = jnp.concatenate(
            [(message_ref[pl.ds(c, slot_total, stride=4), :] * scale).astype(BF16) for c in range(4)], axis=1
        )
        summed = jnp.dot(onehot, message, preferred_element_type=F32)
        for c in range(4):
            cols = slice(c * LANES, (c + 1) * LANES)
            start = jnp.where(ids == head_ref[:, cols], query_ref[:, cols], 0.0)
            mixed_ref[pl.ds(row, TILE), cols] = start + summed[:, cols]

    each(2, tile_step)


def forward_kernel(
    state_hbm, cot_hbm, slots_s, head_s, chosen_s, edges_v, table_t, rel_t, weight_ref, bias_ref,
    state_out, grad_out, mixed_out, slope_out, rel_out, sums_out, places_out,
    own, middle, mixed_own, cot, state_ref, grad_ref, slope_ref, inbox, win_a, win_b, rel_a, rel_b, padded, table_ref,
    message_ref, mixed_ref, wide_ref, head_ref, query_ref, copy_sem, send_sem, recv_sem,
):
    node, position, targets = ring_targets()
    at_end = jnp.logical_or(position == 0, position == RING - 1)
    rows = own.shape[0]
    barrier = pltpu.get_barrier_semaphore()
    for target in targets:
        pl.semaphore_signal(barrier, inc=1, device_id={"node": target}, device_id_type=MESH)
    own_copy = pltpu.make_async_copy(state_hbm, own, copy_sem.at[0])
    cot_copy = pltpu.make_async_copy(cot_hbm, cot, copy_sem.at[1])
    own_copy.start()
    cot_copy.start()
    pl.semaphore_wait(barrier, 3)

    def piece(trip, way, k, source):
        return pltpu.make_async_remote_copy(
            src_ref=source.at[chunk_rows(k), :],
            dst_ref=inbox.at[trip, way, chunk_rows(k), :],
            send_sem=send_sem.at[trip, way, k],
            recv_sem=recv_sem.at[trip, way, k],
            device_id={"node": targets[way]},
            device_id_type=MESH,
        )

    def send_sides(trip, k, source):
        @pl.when(position != RING - 1)
        def _():
            piece(trip, 0, k, source).start()

        @pl.when(position != 0)
        def _():
            piece(trip, 1, k, source).start()

    def relay_chunk(trip, k):
        mirrored = inbox.at[trip, 2]
        piece(trip, 2, k, mirrored).wait_recv()

        @pl.when(position == RING - 1)
        def _():
            piece(trip, 0, k, mirrored).start()

        @pl.when(position == 0)
        def _():
            piece(trip, 1, k, mirrored).start()

    def fill(win, quarter, k, block):
        spread_rows(win, quarter * rows + k * CHUNK, block.astype(F32))

    def start_first(k):
        send_sides(0, k, state_hbm)

        @pl.when(jnp.logical_or(jnp.logical_not(at_end), k < WINDOW))
        def _():
            piece(0, 2, k, state_hbm).start()

    each(CHUNKS, start_first)

    spread_table(table_ref, table_t)
    for layer in range(2):
        pad_columns(padded.at[layer], rel_t.at[layer])
    places_out[...] = edges_v[0] * 4
    lane = lax.broadcasted_iota(jnp.int32, (1, LANES), 1) // DIM
    for c in range(4):
        heads = jnp.zeros((1, LANES), jnp.int32)
        vectors = jnp.zeros((1, LANES), F32)
        for k in range(4):
            heads = jnp.where(lane == k, head_s[4 * c + k], heads)
            vectors = jnp.where(lane == k, table_ref[chosen_s[4 * c + k]][0:1], vectors)
        head_ref[:, c * LANES : (c + 1) * LANES] = heads
        query_ref[:, c * LANES : (c + 1) * LANES] = vectors.astype(BF16).astype(F32)
    for layer in range(2):
        high, low = split_pair(block_diagonal(weight_ref[layer]))
        wide_ref[2 * layer] = high
        wide_ref[2 * layer + 1] = low
    bias_zero = jnp.concatenate([bias_ref[0:1, :]] * 8, axis=1)
    bias_one = jnp.concatenate([bias_ref[1:2, :]] * 8, axis=1)
    first_row = node * rows

    own_copy.wait()
    each(CHUNKS, lambda k: fill(win_a, 1, k, own[chunk_rows(k), :]))

    def relations_of(layer, target, k):
        relation_rows(target, padded.at[layer], edges_v, 2 * k)
        relation_rows(target, padded.at[layer], edges_v, 2 * k + 1)

    def take_first_mirror(k):
        relations_of(0, rel_a, k)
        relations_of(1, rel_b, k)
        relay_chunk(0, k)

        @pl.when(jnp.logical_and(at_end, k + WINDOW < CHUNKS))
        def _():
            piece(0, 2, k + WINDOW, state_hbm).start()

        fill(win_a, 3, k, inbox[0, 2, chunk_rows(k), :])

    def take_first_sides(k):
        for way, quarter in ((0, 0), (1, 2)):
            piece(0, way, k, own).wait_recv()
            fill(win_a, quarter, k, inbox[0, way, chunk_rows(k), :])

    each(CHUNKS, take_first_mirror)
    rel_copy = pltpu.make_async_copy(rel_b, rel_out, copy_sem.at[2])
    rel_copy.start()
    each(CHUNKS, take_first_sides)

    def next_state(state, update, quarter, k, half):
        sigma = jax.nn.sigmoid(update)
        place = pl.ds(pl.multiple_of(quarter * rows + k * CHUNK, CHUNK), CHUNK)
        slope_ref[place, half * 256 : half * 256 + 256] = (sigma * (1.0 + update * (1.0 - sigma))).astype(BF16)
        result = (state.astype(F32) + update * sigma).astype(BF16)
        for c in range(2):
            flat(win_b)[pl.ds((quarter * rows + k * CHUNK) * 4 + half * 2 + c, CHUNK, stride=4), :] = result[
                :, c * LANES : (c + 1) * LANES
            ].astype(F32)
        return result

    def remote_state(way, quarter, k):
        at = chunk_rows(k)
        for half in range(2):
            cols = slice(half * 256, half * 256 + 256)
            mixed = inbox[1, way, at, cols]
            update = half_dot(mixed, wide_ref[0], 0) + half_dot(mixed, wide_ref[1], 0) + bias_zero
            next_state(inbox[0, way, at, cols], update, quarter, k, half)

    def take_second_mirror(k):
        relay_chunk(1, k)
        remote_state(2, 3, k)

    def take_second_sides(k):
        for way, quarter in ((0, 0), (1, 2)):
            piece(1, way, k, own).wait_recv()
            remote_state(way, quarter, k)

    def zero_step(k):
        sum_chunk(k, first_row, slots_s, edges_v, head_ref, query_ref, win_a, rel_a, message_ref, mixed_ref)
        at = chunk_rows(k)
        mixed_own[at, :] = mixed_ref[...].astype(BF16)
        piece(1, 2, k, mixed_own).start()
        send_sides(1, k, mixed_own)
        for half in range(2):
            cols = slice(half * 256, half * 256 + 256)
            update = split_dot(mixed_ref[:, cols], wide_ref[0], wide_ref[1]) + bias_zero
            middle[at, cols] = next_state(own[at, cols], update, 1, k, half)
        @pl.when(k >= 2)
        def _():
            take_second_mirror(k - 2)

        @pl.when(k >= 5)
        def _():
            take_second_sides(k - 5)

    each(CHUNKS, zero_step)
    each(2, lambda k: take_second_mirror(k + CHUNKS - 2))
    each(5, lambda k: take_second_sides(k + CHUNKS - 5))
    cot_copy.wait()
    window_copies = [pltpu.make_async_copy(slope_ref, slope_out, copy_sem.at[3])]
    for quarter, source in enumerate((inbox.at[1, 0], mixed_own, inbox.at[1, 1], inbox.at[1, 2])):
        window_copies.append(
            pltpu.make_async_copy(source, mixed_out.at[pl.ds(quarter * rows, rows), :], copy_sem.at[4 + quarter])
        )
    for copy in window_copies:
        copy.start()

    def result_copies(k):
        at = chunk_rows(k)
        return (
            pltpu.make_async_copy(state_ref.at[at, :], state_out.at[at, :], copy_sem.at[8 + 2 * k]),
            pltpu.make_async_copy(grad_ref.at[at, :], grad_out.at[at, :], copy_sem.at[9 + 2 * k]),
        )

    def one_step(k, carry):
        product, bias_sum = carry
        sum_chunk(k, first_row, slots_s, edges_v, head_ref, query_ref, win_b, rel_b, message_ref, mixed_ref)
        at = chunk_rows(k)
        for half in range(2):
            cols = slice(half * 256, half * 256 + 256)
            mixed = mixed_ref[:, cols]
            update = split_dot(mixed, wide_ref[2], wide_ref[3]) + bias_one
            sigma = jax.nn.sigmoid(update)
            state_ref[at, cols] = (middle[at, cols].astype(F32) + update * sigma).astype(BF16)
            grad = cot[at, cols].astype(F32) * (sigma * (1.0 + update * (1.0 - sigma)))
            grad_ref[at, cols] = split_dot(grad, wide_ref[2], wide_ref[3], 1).astype(BF16)
            for c in range(2):
                part = slice(c * LANES, (c + 1) * LANES)
                product += product_of(mixed[:, part].astype(BF16), grad[:, part].astype(BF16))
                bias_sum += jnp.sum(grad[:, part], axis=0, keepdims=True)
        for copy in result_copies(k):
            copy.start()
        return product, bias_sum

    product, bias_sum = lax.fori_loop(
        0, CHUNKS, one_step, (jnp.zeros((LANES, LANES), F32), jnp.zeros((1, LANES), F32))
    )
    sums_out[0:8, :] = block_sums(product)
    sums_out[8:16, :] = fold_lanes(jnp.broadcast_to(bias_sum, (8, LANES)))
    for trip in range(2):
        for way in range(3):
            each(CHUNKS, lambda k: piece(trip, way, k, own).wait_send())
    rel_copy.wait()
    for copy in window_copies:
        copy.wait()
    each(CHUNKS, lambda k: [copy.wait() for copy in result_copies(k)])


def scatter_kernel(
    state_in, mixed_in, slope_in, rel_in, cot_in, places_s, edges_v, grad_ref, sums_in, state_out, sums_out,
    first_ref, second_ref, third_ref, fourth_ref, rel_ref, mixed_ref, slope_ref, cot_ref, state_ref, term_ref, copy_sem,
):
    copies = [
        pltpu.make_async_copy(source, target, copy_sem.at[i])
        for i, (source, target) in enumerate(
            ((state_in, state_ref), (mixed_in, mixed_ref), (slope_in, slope_ref), (cot_in, cot_ref))
        )
    ]
    part_rows = rel_ref.shape[0] // 4

    def rel_part(i):
        at = pl.ds(pl.multiple_of(i * part_rows, part_rows), part_rows)
        return pltpu.make_async_copy(rel_in.at[at, :], rel_ref.at[at, :], copy_sem.at[5 + i])

    rel_part(0).start()
    totals = (first_ref, second_ref, third_ref, fourth_ref)
    tiles, slot_total = edges_v.shape[1:]
    half_total = slot_total // 2

    def clear(i):
        at = pl.ds(pl.multiple_of(i * 256, 256), 256)
        for total in totals:
            total[at, :] = jnp.zeros((256, LANES), F32)

    each(first_ref.shape[0] // 256, clear)
    rel_part(0).wait()
    for i in range(1, 4):
        rel_part(i).start()
    for copy in copies:
        copy.start()
    state_copy = pltpu.make_async_copy(state_ref, state_out, copy_sem.at[4])

    def make_terms(tile, half):
        edges = slice(half * half_total, half * half_total + half_total)
        onehot = target_onehot(edges_v, tile)[:, edges]
        start = pl.multiple_of(tile * slot_total + half * half_total, half_total)
        scale = rel_ref[pl.ds(start, half_total), :]
        picked = product_of(onehot, grad_ref[pl.ds(pl.multiple_of(tile * TILE, TILE), TILE), :])
        for c in range(4):
            place = pl.ds(4 * half * half_total + c, half_total, stride=4)
            term_ref[place, :] = picked[:, c * LANES : (c + 1) * LANES] * scale

    def add_terms(tile, half):
        base = slot_base(tile)
        for edge in range(half * half_total, (half + 1) * half_total):
            total = totals[edge % SUMS]
            place = pl.ds(pl.multiple_of(places_s[base + slot_step(edge)], 4), 4)
            total[place, :] = total[place, :] + term_ref[4 * edge : 4 * edge + 4, :]

    make_terms(0, 0)

    def tile_step(tile):
        @pl.when(jnp.logical_and(tile & 3 == 3, tile < tiles - 1))
        def _():
            rel_part(tile // 4 + 1).wait()

        add_terms(tile, 0)
        make_terms(tile, 1)
        add_terms(tile, 1)
        make_terms(jnp.minimum(tile + 1, tiles - 1), 0)

    each(tiles, tile_step)
    for copy in copies:
        copy.wait()
    state_copy.start()

    rows = cot_ref.shape[0]

    def collect(quarter, i, carry):
        product, bias_sum = carry
        start = quarter * rows + pl.multiple_of(i * COLLECT, COLLECT)
        at = pl.ds(start, COLLECT)
        grads, mixed = [], []
        for c in range(4):
            cols = slice(c * LANES, (c + 1) * LANES)
            place = pl.ds(start * 4 + c, COLLECT, stride=4)
            terms = (first_ref[place, :] + second_ref[place, :]) + (third_ref[place, :] + fourth_ref[place, :])
            if quarter == 1:
                own_rows = pl.ds(pl.multiple_of(i * COLLECT, COLLECT), COLLECT)
                terms += cot_ref[own_rows, cols].astype(F32)
            grad = terms * slope_ref[at, cols].astype(F32)
            bias_sum += jnp.sum(grad, axis=0, keepdims=True)
            grads.append(grad.astype(BF16))
            mixed.append(mixed_ref[at, cols])
        product += product_of(jnp.concatenate(mixed, axis=0), jnp.concatenate(grads, axis=0))
        return product, bias_sum

    sums = (jnp.zeros((LANES, LANES), F32), jnp.zeros((1, LANES), F32))
    for quarter in range(4):
        sums = lax.fori_loop(0, rows // COLLECT, functools.partial(collect, quarter), sums)
    product, bias_sum = sums
    sums_out[0:8, :] = block_sums(product)
    sums_out[8:16, :] = sums_in[0:8, :]
    sub = lax.broadcasted_iota(jnp.int32, (8, LANES), 0)
    sums_out[16:24, :] = jnp.where(sub == 0, fold_lanes(jnp.broadcast_to(bias_sum, (8, LANES))), sums_in[8:16, :])
    state_copy.wait()


def total_kernel(
    sums_ref, weight_out, bias_out, mine, first_buf, second_buf, first_send, first_recv, second_send, second_recv
):
    node = lax.axis_index("node")
    query = lax.axis_index("query")
    position = lax.rem(node, RING)
    half = node // RING
    in_first = half * 4 + query
    barrier = pltpu.get_barrier_semaphore()

    def first_peer(j):
        return {"node": (j // 4) * RING + position, "query": lax.rem(j, 4)}

    def second_peer(j):
        return {"node": half * RING + j, "query": query}

    for d in range(1, 8):
        pl.semaphore_signal(barrier, inc=1, device_id=first_peer(lax.rem(in_first + d, 8)), device_id_type=MESH)
    for d in range(1, RING):
        pl.semaphore_signal(barrier, inc=1, device_id=second_peer(lax.rem(position + d, RING)), device_id_type=MESH)
    pl.semaphore_wait(barrier, 22)

    def stage(source, buf, send, recv, me, peer, count):
        def piece(slot, to):
            return pltpu.make_async_remote_copy(
                src_ref=source, dst_ref=buf.at[slot], send_sem=send.at[to], recv_sem=recv.at[slot],
                device_id=peer(to), device_id_type=MESH,
            )

        others = [lax.rem(me + d, count) for d in range(1, count)]
        for to in others:
            piece(me, to).start()
        buf[me] = source[...]
        for other in others:
            piece(other, other).wait_recv()
        total = buf[0]
        for j in range(1, count):
            total = total + buf[j]
        return total, lambda: [piece(me, to).wait_send() for to in others]

    total, finish_first = stage(sums_ref, first_buf, first_send, first_recv, in_first, first_peer, 8)
    mine[...] = total
    total, finish_second = stage(mine, second_buf, second_send, second_recv, position, second_peer, RING)
    for l in range(2):
        packed = total[8 * l : 8 * l + 8, :]
        for k in range(4):
            moved = packed if k == 0 else pltpu.roll(packed, LANES - 32 * k, 1)
            weight_out[l, 8 * k : 8 * k + 8, :] = moved[:, 0:32]
    bias_out[...] = total[16:18, 0:32]
    finish_first()
    finish_second()


def in_memory_order(table):
    cols = table.shape[-1]
    return table.reshape(-1, 8, cols // LANES, LANES).transpose(0, 2, 1, 3).reshape(table.size)


def body(
    entity_state, edge_tiles, query_head, query_relation, query_table, rel_vectors, mix_weight, mix_bias, cotangent
):
    rows, cols = entity_state.shape
    tiles, unused, slot_total = edge_tiles.shape
    edge_count = tiles * slot_total
    rel_rows = rel_vectors.shape[1]
    padded_rows = -(-rel_rows // LANES) * LANES
    edges = edge_tiles.transpose(1, 0, 2)
    slots = in_memory_order(edges)
    table_t = query_table.T
    rel_t = rel_vectors.transpose(0, 2, 1)
    smem = pl.BlockSpec(memory_space=pltpu.SMEM)
    vmem = pl.BlockSpec(memory_space=pltpu.VMEM)
    anywhere = pl.BlockSpec(memory_space=pl.ANY)
    half = jax.ShapeDtypeStruct((rows, cols), BF16)
    wide = jax.ShapeDtypeStruct((4 * rows, cols), BF16)
    packet = (24, LANES)
    block = pltpu.VMEM((rows, cols), BF16)
    window = pltpu.VMEM((rows * 4, 4, LANES), F32)
    edge_rows = pltpu.VMEM((edge_count, LANES), F32)
    padded = pltpu.VMEM((2, DIM, padded_rows), F32)
    message = pltpu.VMEM((slot_total * 4, LANES), F32)
    state_two, grad_mixed, mixed_zero, slope_zero, rel_one, sums, places = pl.pallas_call(
        forward_kernel,
        out_shape=(
            half,
            half,
            wide,
            wide,
            jax.ShapeDtypeStruct((edge_count, LANES), F32),
            jax.ShapeDtypeStruct((16, LANES), F32),
            jax.ShapeDtypeStruct((tiles, slot_total), jnp.int32),
        ),
        in_specs=[anywhere] * 2 + [smem] * 3 + [vmem] * 5,
        out_specs=(anywhere,) * 5 + (vmem,) * 2,
        scratch_shapes=[block] * 6
        + [
            pltpu.VMEM((4 * rows, cols), BF16),
            pltpu.VMEM((2, 3, rows, cols), BF16),
            window,
            window,
            edge_rows,
            edge_rows,
            padded,
            pltpu.VMEM((rel_rows, 4, LANES), F32),
            message,
            pltpu.VMEM((CHUNK, cols), F32),
            pltpu.VMEM((4, 256, 256), BF16),
            pltpu.VMEM((1, cols), jnp.int32),
            pltpu.VMEM((1, cols), F32),
            pltpu.SemaphoreType.DMA((8 + 2 * CHUNKS,)),
            pltpu.SemaphoreType.DMA((2, 3, CHUNKS)),
            pltpu.SemaphoreType.DMA((2, 3, CHUNKS)),
        ],
        compiler_params=pltpu.CompilerParams(
            vmem_limit_bytes=VMEM_BYTES, collective_id=0, has_side_effects=True
        ),
        name="two_layers",
    )(
        entity_state, cotangent, slots, query_head, query_relation, edges, table_t, rel_t, mix_weight, mix_bias
    )
    state_out, sums = pl.pallas_call(
        scatter_kernel,
        out_shape=(half, jax.ShapeDtypeStruct(packet, F32)),
        in_specs=[anywhere] * 5 + [smem] + [vmem] * 3,
        out_specs=(anywhere, vmem),
        scratch_shapes=[pltpu.VMEM((rows * 16, LANES), F32)] * SUMS
        + [
            edge_rows,
            pltpu.VMEM((4 * rows, cols), BF16),
            pltpu.VMEM((4 * rows, cols), BF16),
            block,
            block,
            message,
            pltpu.SemaphoreType.DMA((9,)),
        ],
        compiler_params=pltpu.CompilerParams(vmem_limit_bytes=VMEM_BYTES),
        name="scatter_terms",
    )(state_two, mixed_zero, slope_zero, rel_one, cotangent, in_memory_order(places), edges, grad_mixed, sums)
    weight_grads, bias_grads = pl.pallas_call(
        total_kernel,
        out_shape=(jax.ShapeDtypeStruct((2, DIM, DIM), F32), jax.ShapeDtypeStruct((2, DIM), F32)),
        in_specs=[vmem],
        out_specs=(vmem,) * 2,
        scratch_shapes=[
            pltpu.VMEM(packet, F32),
            pltpu.VMEM((8,) + packet, F32),
            pltpu.VMEM((RING,) + packet, F32),
            pltpu.SemaphoreType.DMA((8,)),
            pltpu.SemaphoreType.DMA((8,)),
            pltpu.SemaphoreType.DMA((RING,)),
            pltpu.SemaphoreType.DMA((RING,)),
        ],
        compiler_params=pltpu.CompilerParams(collective_id=1, has_side_effects=True),
        name="total_sums",
    )(sums)
    return state_out, weight_grads, bias_grads


def solution(mesh):
    placed = (
        P("node", "query"),
        P("node", None, None),
        P("query"),
        P("query"),
        P(),
        P(),
        P(),
        P(),
        P("node", "query"),
    )
    return jax.shard_map(
        body, mesh=mesh, in_specs=placed, out_specs=(P("node", "query"), P(), P()), check_vma=False
    )
```

```python
import functools

import jax
import jax.numpy as jnp
from jax import lax
from jax.experimental import pallas as pl
from jax.experimental.pallas import tpu as pltpu
from jax.sharding import PartitionSpec as P

DIM = 32
LANES = 128
TILE = 64
CHUNK = 128
CHUNKS = 8
RING = 16
WINDOW = 3
SUMS = 4
COLLECT = 512
F32 = jnp.float32
BF16 = jnp.bfloat16
MESH = pl.DeviceIdType.MESH
VMEM_BYTES = 58 << 20


def split_pair(matrix):
    high = matrix.astype(BF16)
    return high, (matrix - high.astype(F32)).astype(BF16)


def half_dot(left, right, right_dim):
    return lax.dot_general(left, right, (((1,), (right_dim,)), ((), ())), preferred_element_type=F32)


def split_dot(left, right_high, right_low, right_dim=0):
    high, low = split_pair(left)
    total = half_dot(high, right_high, right_dim) + half_dot(low, right_high, right_dim)
    return total + half_dot(high, right_low, right_dim)


def product_of(left, right):
    return lax.dot_general(left, right, (((0,), (0,)), ((), ())), preferred_element_type=F32)


def each(count, step):
    def run(i, carry):
        step(i)
        return carry

    lax.fori_loop(0, count, run, 0)


def flat(target):
    return target.reshape(target.shape[0] * 4, LANES)


def spread_rows(target, first, block):
    rows = block.shape[0]
    for c in range(4):
        flat(target)[pl.ds(first * 4 + c, rows, stride=4), :] = block[:, c * LANES : (c + 1) * LANES]


def spread_table(target, columns_ref):
    count = columns_ref.shape[1]
    for start in range(0, count, LANES):
        width = min(LANES, count - start)
        wide = jnp.concatenate([columns_ref[:, start : start + width]] * 4, axis=0).T
        for c in range(4):
            flat(target)[pl.ds(start * 4 + c, width, stride=4), :] = wide


def pad_columns(target, columns_ref):
    count = columns_ref.shape[1]
    whole = count // LANES * LANES
    target[:, 0:whole] = columns_ref[:, 0:whole]
    if whole < count:
        rest = jnp.zeros((columns_ref.shape[0], LANES - count + whole), F32)
        target[:, whole : whole + LANES] = jnp.concatenate([columns_ref[:, whole:count], rest], axis=1)


def relation_rows(target, table_ref, edges_v, tile):
    slot_total = edges_v.shape[2]
    row = edges_v[2, pl.ds(tile, 1), :]
    for q in range(slot_total // LANES):
        ids = jnp.broadcast_to(row[:, q * LANES : (q + 1) * LANES], (DIM, LANES))
        lane, part = ids & (LANES - 1), ids >> 7
        found = jnp.zeros((DIM, LANES), F32)
        for j in range(table_ref.shape[1] // LANES):
            columns = table_ref[:, j * LANES : (j + 1) * LANES]
            found = jnp.where(part == j, jnp.take_along_axis(columns, lane, axis=1), found)
        at = pl.multiple_of(tile * slot_total + q * LANES, LANES)
        target[pl.ds(at, LANES), :] = jnp.concatenate([found] * 4, axis=0).T


def block_diagonal(matrix):
    row = jnp.concatenate([matrix] * 8, axis=1)
    wide = jnp.concatenate([row] * 8, axis=0)
    rows = lax.broadcasted_iota(jnp.int32, (256, 256), 0) // DIM
    cols = lax.broadcasted_iota(jnp.int32, (256, 256), 1) // DIM
    return jnp.where(rows == cols, wide, 0.0)


def fold_lanes(values):
    values = values + pltpu.roll(values, 64, 1)
    return values + pltpu.roll(values, 32, 1)


def block_sums(product):
    rows = lax.broadcasted_iota(jnp.int32, (LANES, LANES), 0) // DIM
    cols = lax.broadcasted_iota(jnp.int32, (LANES, LANES), 1) // DIM
    kept = jnp.where(rows == cols, product, 0.0)
    folded = fold_lanes(kept[0:32] + kept[32:64] + kept[64:96] + kept[96:128])
    lane = lax.broadcasted_iota(jnp.int32, (8, LANES), 1) // DIM
    packed = jnp.where(lane == 0, folded[0:8], 0.0)
    for k in range(1, 4):
        packed = jnp.where(lane == k, folded[8 * k : 8 * k + 8], packed)
    return packed


def chunk_rows(k):
    return pl.ds(pl.multiple_of(k * CHUNK, CHUNK), CHUNK)


def slot_base(tile):
    return tile // 8 * 4096 + lax.rem(tile, 8) * LANES


def slot_step(edge):
    return edge // LANES * 1024 + edge % LANES


def target_onehot(edges_v, tile):
    targets = edges_v[1, pl.ds(tile, 1), :]
    return (targets == lax.broadcasted_iota(jnp.int32, (TILE, targets.shape[1]), 0)).astype(BF16)


def ring_targets():
    node = lax.axis_index("node")
    position = lax.rem(node, RING)
    plane = node - position
    after = plane + lax.rem(position + 1, RING)
    before = plane + lax.rem(position + RING - 1, RING)
    across = lax.rem(node + RING, 2 * RING)
    return node, position, (after, before, across)


def sum_chunk(k, first_row, slots_s, edges_v, head_ref, query_ref, win_ref, rel_ref, message_ref, mixed_ref):
    slot_total = edges_v.shape[2]

    def tile_step(j):
        tile = 2 * k + j

        base = slot_base(tile)
        for edge in range(slot_total):
            message_ref[4 * edge : 4 * edge + 4, :] = win_ref[slots_s[base + slot_step(edge)]]
        onehot = target_onehot(edges_v, tile)
        row = pl.multiple_of(j * TILE, TILE)
        ids = first_row + tile * TILE + lax.broadcasted_iota(jnp.int32, (TILE, LANES), 0)
        scale = rel_ref[pl.ds(pl.multiple_of(tile * slot_total, slot_total), slot_total), :]
        message = jnp.concatenate(
            [(message_ref[pl.ds(c, slot_total, stride=4), :] * scale).astype(BF16) for c in range(4)], axis=1
        )
        summed = jnp.dot(onehot, message, preferred_element_type=F32)
        for c in range(4):
            cols = slice(c * LANES, (c + 1) * LANES)
            start = jnp.where(ids == head_ref[:, cols], query_ref[:, cols], 0.0)
            mixed_ref[pl.ds(row, TILE), cols] = start + summed[:, cols]

    each(2, tile_step)


def forward_kernel(
    state_hbm, cot_hbm, slots_hbm, edges_hbm, table_hbm, rel_hbm, head_s, chosen_s, weight_ref, bias_ref,
    state_out, grad_out, mixed_out, slope_out, rel_out, sums_out, places_out,
    own, middle, mixed_own, cot, state_ref, grad_ref, slope_ref, inbox, win_a, win_b, rel_a, rel_b, padded, table_ref,
    message_ref, mixed_ref, wide_ref, head_ref, query_ref, slots_s, edges_v, table_t, rel_t, copy_sem, send_sem, recv_sem,
):
    node, position, targets = ring_targets()
    at_end = jnp.logical_or(position == 0, position == RING - 1)
    rows = own.shape[0]
    barrier = pltpu.get_barrier_semaphore()
    for target in targets:
        pl.semaphore_signal(barrier, inc=1, device_id={"node": target}, device_id_type=MESH)
    first = 8 + 2 * CHUNKS
    operand_copies = [
        pltpu.make_async_copy(source, target, copy_sem.at[first + i])
        for i, (source, target) in enumerate(
            (
                (table_hbm, table_t),
                (rel_hbm, rel_t),
                (edges_hbm, edges_v),
                (slots_hbm.at[pl.ds(0, slots_s.shape[0])], slots_s),
            )
        )
    ]
    own_copy = pltpu.make_async_copy(state_hbm, own, copy_sem.at[0])
    cot_copy = pltpu.make_async_copy(cot_hbm, cot, copy_sem.at[1])
    pl.semaphore_wait(barrier, 3)

    def piece(trip, way, k, source):
        return pltpu.make_async_remote_copy(
            src_ref=source.at[chunk_rows(k), :],
            dst_ref=inbox.at[trip, way, chunk_rows(k), :],
            send_sem=send_sem.at[trip, way, k],
            recv_sem=recv_sem.at[trip, way, k],
            device_id={"node": targets[way]},
            device_id_type=MESH,
        )

    def send_sides(trip, k, source):
        @pl.when(position != RING - 1)
        def _():
            piece(trip, 0, k, source).start()

        @pl.when(position != 0)
        def _():
            piece(trip, 1, k, source).start()

    def relay_chunk(trip, k):
        mirrored = inbox.at[trip, 2]
        piece(trip, 2, k, mirrored).wait_recv()

        @pl.when(position == RING - 1)
        def _():
            piece(trip, 0, k, mirrored).start()

        @pl.when(position == 0)
        def _():
            piece(trip, 1, k, mirrored).start()

    def fill(win, quarter, k, block):
        spread_rows(win, quarter * rows + k * CHUNK, block.astype(F32))

    def start_first(k):
        send_sides(0, k, state_hbm)

        @pl.when(jnp.logical_or(jnp.logical_not(at_end), k < WINDOW))
        def _():
            piece(0, 2, k, state_hbm).start()

    each(CHUNKS, start_first)
    for copy in operand_copies:
        copy.start()
    own_copy.start()
    cot_copy.start()
    for copy in operand_copies:
        copy.wait()

    spread_table(table_ref, table_t)
    for layer in range(2):
        pad_columns(padded.at[layer], rel_t.at[layer])
    places_out[...] = edges_v[0] * 4
    lane = lax.broadcasted_iota(jnp.int32, (1, LANES), 1) // DIM
    for c in range(4):
        heads = jnp.zeros((1, LANES), jnp.int32)
        vectors = jnp.zeros((1, LANES), F32)
        for k in range(4):
            heads = jnp.where(lane == k, head_s[4 * c + k], heads)
            vectors = jnp.where(lane == k, table_ref[chosen_s[4 * c + k]][0:1], vectors)
        head_ref[:, c * LANES : (c + 1) * LANES] = heads
        query_ref[:, c * LANES : (c + 1) * LANES] = vectors.astype(BF16).astype(F32)
    for layer in range(2):
        high, low = split_pair(block_diagonal(weight_ref[layer]))
        wide_ref[2 * layer] = high
        wide_ref[2 * layer + 1] = low
    bias_zero = jnp.concatenate([bias_ref[0:1, :]] * 8, axis=1)
    bias_one = jnp.concatenate([bias_ref[1:2, :]] * 8, axis=1)
    first_row = node * rows

    own_copy.wait()
    each(CHUNKS, lambda k: fill(win_a, 1, k, own[chunk_rows(k), :]))

    def relations_of(layer, target, k):
        relation_rows(target, padded.at[layer], edges_v, 2 * k)
        relation_rows(target, padded.at[layer], edges_v, 2 * k + 1)

    def take_first_mirror(k):
        relations_of(0, rel_a, k)
        relations_of(1, rel_b, k)
        relay_chunk(0, k)

        @pl.when(jnp.logical_and(at_end, k + WINDOW < CHUNKS))
        def _():
            piece(0, 2, k + WINDOW, state_hbm).start()

        fill(win_a, 3, k, inbox[0, 2, chunk_rows(k), :])

    def take_first_sides(k):
        for way, quarter in ((0, 0), (1, 2)):
            piece(0, way, k, own).wait_recv()
            fill(win_a, quarter, k, inbox[0, way, chunk_rows(k), :])

    each(CHUNKS, take_first_mirror)
    rel_copy = pltpu.make_async_copy(rel_b, rel_out, copy_sem.at[2])
    rel_copy.start()
    each(CHUNKS, take_first_sides)

    def next_state(state, update, quarter, k, half):
        sigma = jax.nn.sigmoid(update)
        place = pl.ds(pl.multiple_of(quarter * rows + k * CHUNK, CHUNK), CHUNK)
        slope_ref[place, half * 256 : half * 256 + 256] = (sigma * (1.0 + update * (1.0 - sigma))).astype(BF16)
        result = (state.astype(F32) + update * sigma).astype(BF16)
        for c in range(2):
            flat(win_b)[pl.ds((quarter * rows + k * CHUNK) * 4 + half * 2 + c, CHUNK, stride=4), :] = result[
                :, c * LANES : (c + 1) * LANES
            ].astype(F32)
        return result

    def remote_state(way, quarter, k):
        at = chunk_rows(k)
        for half in range(2):
            cols = slice(half * 256, half * 256 + 256)
            mixed = inbox[1, way, at, cols]
            update = half_dot(mixed, wide_ref[0], 0) + half_dot(mixed, wide_ref[1], 0) + bias_zero
            next_state(inbox[0, way, at, cols], update, quarter, k, half)

    def take_second_mirror(k):
        relay_chunk(1, k)
        remote_state(2, 3, k)

    def take_second_sides(k):
        for way, quarter in ((0, 0), (1, 2)):
            piece(1, way, k, own).wait_recv()
            remote_state(way, quarter, k)

    def zero_step(k):
        sum_chunk(k, first_row, slots_s, edges_v, head_ref, query_ref, win_a, rel_a, message_ref, mixed_ref)
        at = chunk_rows(k)
        mixed_own[at, :] = mixed_ref[...].astype(BF16)
        piece(1, 2, k, mixed_own).start()
        send_sides(1, k, mixed_own)
        for half in range(2):
            cols = slice(half * 256, half * 256 + 256)
            update = split_dot(mixed_ref[:, cols], wide_ref[0], wide_ref[1]) + bias_zero
            middle[at, cols] = next_state(own[at, cols], update, 1, k, half)
        @pl.when(k >= 2)
        def _():
            take_second_mirror(k - 2)

        @pl.when(k >= 5)
        def _():
            take_second_sides(k - 5)

    each(CHUNKS, zero_step)
    take_second_sides(CHUNKS - 5)
    take_second_mirror(CHUNKS - 2)
    take_second_sides(CHUNKS - 4)
    take_second_mirror(CHUNKS - 1)
    each(3, lambda k: take_second_sides(k + CHUNKS - 3))
    cot_copy.wait()
    window_copies = [pltpu.make_async_copy(slope_ref, slope_out, copy_sem.at[3])]
    for quarter, source in enumerate((inbox.at[1, 0], mixed_own, inbox.at[1, 1], inbox.at[1, 2])):
        window_copies.append(
            pltpu.make_async_copy(source, mixed_out.at[pl.ds(quarter * rows, rows), :], copy_sem.at[4 + quarter])
        )
    for copy in window_copies:
        copy.start()

    def result_copies(k):
        at = chunk_rows(k)
        return (
            pltpu.make_async_copy(state_ref.at[at, :], state_out.at[at, :], copy_sem.at[8 + 2 * k]),
            pltpu.make_async_copy(grad_ref.at[at, :], grad_out.at[at, :], copy_sem.at[9 + 2 * k]),
        )

    def one_step(k, carry):
        product, bias_sum = carry
        sum_chunk(k, first_row, slots_s, edges_v, head_ref, query_ref, win_b, rel_b, message_ref, mixed_ref)
        at = chunk_rows(k)
        for half in range(2):
            cols = slice(half * 256, half * 256 + 256)
            mixed = mixed_ref[:, cols]
            update = split_dot(mixed, wide_ref[2], wide_ref[3]) + bias_one
            sigma = jax.nn.sigmoid(update)
            state_ref[at, cols] = (middle[at, cols].astype(F32) + update * sigma).astype(BF16)
            grad = cot[at, cols].astype(F32) * (sigma * (1.0 + update * (1.0 - sigma)))
            grad_ref[at, cols] = split_dot(grad, wide_ref[2], wide_ref[3], 1).astype(BF16)
            for c in range(2):
                part = slice(c * LANES, (c + 1) * LANES)
                product += product_of(mixed[:, part].astype(BF16), grad[:, part].astype(BF16))
                bias_sum += jnp.sum(grad[:, part], axis=0, keepdims=True)
        for copy in result_copies(k):
            copy.start()
        return product, bias_sum

    product, bias_sum = lax.fori_loop(
        0, CHUNKS, one_step, (jnp.zeros((LANES, LANES), F32), jnp.zeros((1, LANES), F32))
    )
    sums_out[0:8, :] = block_sums(product)
    sums_out[8:16, :] = fold_lanes(jnp.broadcast_to(bias_sum, (8, LANES)))
    for trip in range(2):
        for way in range(3):
            each(CHUNKS, lambda k: piece(trip, way, k, own).wait_send())
    rel_copy.wait()
    for copy in window_copies:
        copy.wait()
    each(CHUNKS, lambda k: [copy.wait() for copy in result_copies(k)])


def scatter_kernel(
    state_in, mixed_in, slope_in, rel_in, cot_in, places_in, edges_in, grad_in, sums_in, state_out, sums_out,
    first_ref, second_ref, third_ref, fourth_ref, rel_ref, mixed_ref, slope_ref, cot_ref, state_ref, term_ref,
    places_s, edges_v, grad_ref, copy_sem,
):
    copies = [
        pltpu.make_async_copy(source, target, copy_sem.at[i])
        for i, (source, target) in enumerate(
            ((state_in, state_ref), (mixed_in, mixed_ref), (slope_in, slope_ref), (cot_in, cot_ref))
        )
    ]
    part_rows = rel_ref.shape[0] // 4

    def rel_part(i):
        at = pl.ds(pl.multiple_of(i * part_rows, part_rows), part_rows)
        return pltpu.make_async_copy(rel_in.at[at, :], rel_ref.at[at, :], copy_sem.at[5 + i])

    early = [
        pltpu.make_async_copy(source, target, copy_sem.at[9 + i])
        for i, (source, target) in enumerate(((places_in, places_s), (edges_in, edges_v), (grad_in, grad_ref)))
    ]
    for copy in early:
        copy.start()
    rel_part(0).start()
    totals = (first_ref, second_ref, third_ref, fourth_ref)
    tiles, slot_total = edges_v.shape[1:]
    half_total = slot_total // 2

    def clear(i):
        at = pl.ds(pl.multiple_of(i * 256, 256), 256)
        for total in totals:
            total[at, :] = jnp.zeros((256, LANES), F32)

    each(first_ref.shape[0] // 256, clear)
    for copy in early:
        copy.wait()
    rel_part(0).wait()
    for i in range(1, 4):
        rel_part(i).start()
    for copy in copies:
        copy.start()
    state_copy = pltpu.make_async_copy(state_ref, state_out, copy_sem.at[4])

    def make_terms(tile, half):
        edges = slice(half * half_total, half * half_total + half_total)
        onehot = target_onehot(edges_v, tile)[:, edges]
        start = pl.multiple_of(tile * slot_total + half * half_total, half_total)
        scale = rel_ref[pl.ds(start, half_total), :]
        picked = product_of(onehot, grad_ref[pl.ds(pl.multiple_of(tile * TILE, TILE), TILE), :])
        for c in range(4):
            place = pl.ds(4 * half * half_total + c, half_total, stride=4)
            term_ref[place, :] = picked[:, c * LANES : (c + 1) * LANES] * scale

    def add_terms(tile, half):
        base = slot_base(tile)
        for edge in range(half * half_total, (half + 1) * half_total):
            total = totals[edge % SUMS]
            place = pl.ds(pl.multiple_of(places_s[base + slot_step(edge)], 4), 4)
            total[place, :] = total[place, :] + term_ref[4 * edge : 4 * edge + 4, :]

    make_terms(0, 0)

    def tile_step(tile):
        @pl.when(jnp.logical_and(tile & 3 == 3, tile < tiles - 1))
        def _():
            rel_part(tile // 4 + 1).wait()

        add_terms(tile, 0)
        make_terms(tile, 1)
        add_terms(tile, 1)
        make_terms(jnp.minimum(tile + 1, tiles - 1), 0)

    each(tiles, tile_step)
    for copy in copies:
        copy.wait()
    state_copy.start()

    rows = cot_ref.shape[0]

    def collect(quarter, i, carry):
        product, bias_sum = carry
        start = quarter * rows + pl.multiple_of(i * COLLECT, COLLECT)
        at = pl.ds(start, COLLECT)
        grads, mixed = [], []
        for c in range(4):
            cols = slice(c * LANES, (c + 1) * LANES)
            place = pl.ds(start * 4 + c, COLLECT, stride=4)
            terms = (first_ref[place, :] + second_ref[place, :]) + (third_ref[place, :] + fourth_ref[place, :])
            if quarter == 1:
                own_rows = pl.ds(pl.multiple_of(i * COLLECT, COLLECT), COLLECT)
                terms += cot_ref[own_rows, cols].astype(F32)
            grad = terms * slope_ref[at, cols].astype(F32)
            bias_sum += jnp.sum(grad, axis=0, keepdims=True)
            grads.append(grad.astype(BF16))
            mixed.append(mixed_ref[at, cols])
        product += product_of(jnp.concatenate(mixed, axis=0), jnp.concatenate(grads, axis=0))
        return product, bias_sum

    sums = (jnp.zeros((LANES, LANES), F32), jnp.zeros((1, LANES), F32))
    for quarter in range(4):
        sums = lax.fori_loop(0, rows // COLLECT, functools.partial(collect, quarter), sums)
    product, bias_sum = sums
    sums_out[0:8, :] = block_sums(product)
    sums_out[8:16, :] = sums_in[0:8, :]
    sub = lax.broadcasted_iota(jnp.int32, (8, LANES), 0)
    sums_out[16:24, :] = jnp.where(sub == 0, fold_lanes(jnp.broadcast_to(bias_sum, (8, LANES))), sums_in[8:16, :])
    state_copy.wait()


def total_kernel(
    sums_ref, total_out, mine, first_buf, second_buf, first_send, first_recv, second_send, second_recv
):
    node = lax.axis_index("node")
    query = lax.axis_index("query")
    position = lax.rem(node, RING)
    half = node // RING
    in_first = half * 4 + query
    barrier = pltpu.get_barrier_semaphore()

    def first_peer(j):
        return {"node": (j // 4) * RING + position, "query": lax.rem(j, 4)}

    def second_peer(j):
        return {"node": half * RING + j, "query": query}

    for d in range(1, 8):
        pl.semaphore_signal(barrier, inc=1, device_id=first_peer(lax.rem(in_first + d, 8)), device_id_type=MESH)
    for d in range(1, RING):
        pl.semaphore_signal(barrier, inc=1, device_id=second_peer(lax.rem(position + d, RING)), device_id_type=MESH)
    pl.semaphore_wait(barrier, 22)

    def stage(source, buf, send, recv, me, peer, count):
        def piece(slot, to):
            return pltpu.make_async_remote_copy(
                src_ref=source, dst_ref=buf.at[slot], send_sem=send.at[to], recv_sem=recv.at[slot],
                device_id=peer(to), device_id_type=MESH,
            )

        others = [lax.rem(me + d, count) for d in range(1, count)]
        for to in others:
            piece(me, to).start()
        buf[me] = source[...]
        for other in others:
            piece(other, other).wait_recv()
        total = buf[0]
        for j in range(1, count):
            total = total + buf[j]
        return total, lambda: [piece(me, to).wait_send() for to in others]

    total, finish_first = stage(sums_ref, first_buf, first_send, first_recv, in_first, first_peer, 8)
    mine[...] = total
    total, finish_second = stage(mine, second_buf, second_send, second_recv, position, second_peer, RING)
    total_out[...] = total
    finish_first()
    finish_second()


def unpack_kernel(total_ref, weight_out, bias_out):
    total = total_ref[...]
    for l in range(2):
        packed = total[8 * l : 8 * l + 8, :]
        for k in range(4):
            moved = packed if k == 0 else pltpu.roll(packed, LANES - 32 * k, 1)
            weight_out[l, 8 * k : 8 * k + 8, :] = moved[:, 0:32]
    bias_out[...] = total[16:18, 0:32]


def in_memory_order(table):
    cols = table.shape[-1]
    return table.reshape(-1, 8, cols // LANES, LANES).transpose(0, 2, 1, 3).reshape(table.size)


def body(
    entity_state, edge_tiles, query_head, query_relation, query_table, rel_vectors, mix_weight, mix_bias, cotangent
):
    rows, cols = entity_state.shape
    tiles, unused, slot_total = edge_tiles.shape
    edge_count = tiles * slot_total
    rel_rows = rel_vectors.shape[1]
    padded_rows = -(-rel_rows // LANES) * LANES
    edges = edge_tiles.transpose(1, 0, 2)
    slots = in_memory_order(edges)
    table_t = query_table.T
    rel_t = rel_vectors.transpose(0, 2, 1)
    smem = pl.BlockSpec(memory_space=pltpu.SMEM)
    vmem = pl.BlockSpec(memory_space=pltpu.VMEM)
    anywhere = pl.BlockSpec(memory_space=pl.ANY)
    half = jax.ShapeDtypeStruct((rows, cols), BF16)
    wide = jax.ShapeDtypeStruct((4 * rows, cols), BF16)
    packet = (24, LANES)
    block = pltpu.VMEM((rows, cols), BF16)
    window = pltpu.VMEM((rows * 4, 4, LANES), F32)
    edge_rows = pltpu.VMEM((edge_count, LANES), F32)
    padded = pltpu.VMEM((2, DIM, padded_rows), F32)
    message = pltpu.VMEM((slot_total * 4, LANES), F32)
    state_two, grad_mixed, mixed_zero, slope_zero, rel_one, sums, places = pl.pallas_call(
        forward_kernel,
        out_shape=(
            half,
            half,
            wide,
            wide,
            jax.ShapeDtypeStruct((edge_count, LANES), F32),
            jax.ShapeDtypeStruct((16, LANES), F32),
            jax.ShapeDtypeStruct((tiles, slot_total), jnp.int32),
        ),
        in_specs=[anywhere] * 6 + [smem] * 2 + [vmem] * 2,
        out_specs=(anywhere,) * 5 + (vmem,) * 2,
        scratch_shapes=[block] * 6
        + [
            pltpu.VMEM((4 * rows, cols), BF16),
            pltpu.VMEM((2, 3, rows, cols), BF16),
            window,
            window,
            edge_rows,
            edge_rows,
            padded,
            pltpu.VMEM((rel_rows, 4, LANES), F32),
            message,
            pltpu.VMEM((CHUNK, cols), F32),
            pltpu.VMEM((4, 256, 256), BF16),
            pltpu.VMEM((1, cols), jnp.int32),
            pltpu.VMEM((1, cols), F32),
            pltpu.SMEM((edge_count,), jnp.int32),
            pltpu.VMEM(edges.shape, jnp.int32),
            pltpu.VMEM(table_t.shape, F32),
            pltpu.VMEM(rel_t.shape, F32),
            pltpu.SemaphoreType.DMA((12 + 2 * CHUNKS,)),
            pltpu.SemaphoreType.DMA((2, 3, CHUNKS)),
            pltpu.SemaphoreType.DMA((2, 3, CHUNKS)),
        ],
        compiler_params=pltpu.CompilerParams(
            vmem_limit_bytes=VMEM_BYTES, collective_id=0, has_side_effects=True
        ),
        name="two_layers",
    )(
        entity_state, cotangent, slots, edges, table_t, rel_t, query_head, query_relation, mix_weight, mix_bias
    )
    state_out, sums = pl.pallas_call(
        scatter_kernel,
        out_shape=(half, jax.ShapeDtypeStruct(packet, F32)),
        in_specs=[anywhere] * 8 + [vmem],
        out_specs=(anywhere, vmem),
        scratch_shapes=[pltpu.VMEM((rows * 16, LANES), F32)] * SUMS
        + [
            edge_rows,
            pltpu.VMEM((4 * rows, cols), BF16),
            pltpu.VMEM((4 * rows, cols), BF16),
            block,
            block,
            message,
            pltpu.SMEM((edge_count,), jnp.int32),
            pltpu.VMEM(edges.shape, jnp.int32),
            block,
            pltpu.SemaphoreType.DMA((12,)),
        ],
        compiler_params=pltpu.CompilerParams(vmem_limit_bytes=VMEM_BYTES),
        name="scatter_terms",
    )(state_two, mixed_zero, slope_zero, rel_one, cotangent, in_memory_order(places), edges, grad_mixed, sums)
    total = pl.pallas_call(
        total_kernel,
        out_shape=jax.ShapeDtypeStruct(packet, F32),
        in_specs=[vmem],
        out_specs=vmem,
        scratch_shapes=[
            pltpu.VMEM(packet, F32),
            pltpu.VMEM((8,) + packet, F32),
            pltpu.VMEM((RING,) + packet, F32),
            pltpu.SemaphoreType.DMA((8,)),
            pltpu.SemaphoreType.DMA((8,)),
            pltpu.SemaphoreType.DMA((RING,)),
            pltpu.SemaphoreType.DMA((RING,)),
        ],
        compiler_params=pltpu.CompilerParams(collective_id=1, has_side_effects=True),
        name="total_sums",
    )(sums)
    weight_grads, bias_grads = pl.pallas_call(
        unpack_kernel,
        out_shape=(jax.ShapeDtypeStruct((2, DIM, DIM), F32), jax.ShapeDtypeStruct((2, DIM), F32)),
        in_specs=[vmem],
        out_specs=(vmem,) * 2,
        name="unpack_sums",
    )(total)
    return state_out, weight_grads, bias_grads


def solution(mesh):
    placed = (
        P("node", "query"),
        P("node", None, None),
        P("query"),
        P("query"),
        P(),
        P(),
        P(),
        P(),
        P("node", "query"),
    )
    return jax.shard_map(
        body, mesh=mesh, in_specs=placed, out_specs=(P("node", "query"), P(), P()), check_vma=False
    )
```

```python
import functools

import jax
import jax.numpy as jnp
from jax import lax
from jax.experimental import pallas as pl
from jax.experimental.pallas import tpu as pltpu
from jax.sharding import PartitionSpec as P

DIM = 32
LANES = 128
TILE = 64
CHUNK = 128
CHUNKS = 8
RING = 16
WINDOW = 3
SUMS = 4
COLLECT = 512
F32 = jnp.float32
BF16 = jnp.bfloat16
MESH = pl.DeviceIdType.MESH
VMEM_BYTES = 58 << 20


def split_pair(matrix):
    high = matrix.astype(BF16)
    return high, (matrix - high.astype(F32)).astype(BF16)


def half_dot(left, right, right_dim):
    return lax.dot_general(left, right, (((1,), (right_dim,)), ((), ())), preferred_element_type=F32)


def split_dot(left, right_high, right_low, right_dim=0):
    high, low = split_pair(left)
    total = half_dot(high, right_high, right_dim) + half_dot(low, right_high, right_dim)
    return total + half_dot(high, right_low, right_dim)


def product_of(left, right):
    return lax.dot_general(left, right, (((0,), (0,)), ((), ())), preferred_element_type=F32)


def each(count, step):
    def run(i, carry):
        step(i)
        return carry

    lax.fori_loop(0, count, run, 0)


def flat(target):
    return target.reshape(target.shape[0] * 4, LANES)


def spread_rows(target, first, block):
    rows = block.shape[0]
    for c in range(4):
        flat(target)[pl.ds(first * 4 + c, rows, stride=4), :] = block[:, c * LANES : (c + 1) * LANES]


def spread_table(target, columns_ref):
    count = columns_ref.shape[1]
    for start in range(0, count, LANES):
        width = min(LANES, count - start)
        wide = jnp.concatenate([columns_ref[:, start : start + width]] * 4, axis=0).T
        for c in range(4):
            flat(target)[pl.ds(start * 4 + c, width, stride=4), :] = wide


def pad_columns(target, columns_ref):
    count = columns_ref.shape[1]
    whole = count // LANES * LANES
    target[:, 0:whole] = columns_ref[:, 0:whole]
    if whole < count:
        rest = jnp.zeros((columns_ref.shape[0], LANES - count + whole), F32)
        target[:, whole : whole + LANES] = jnp.concatenate([columns_ref[:, whole:count], rest], axis=1)


def relation_rows(target, table_ref, edges_v, tile):
    slot_total = edges_v.shape[2]
    row = edges_v[2, pl.ds(tile, 1), :]
    for q in range(slot_total // LANES):
        ids = jnp.broadcast_to(row[:, q * LANES : (q + 1) * LANES], (DIM, LANES))
        lane, part = ids & (LANES - 1), ids >> 7
        found = jnp.zeros((DIM, LANES), F32)
        for j in range(table_ref.shape[1] // LANES):
            columns = table_ref[:, j * LANES : (j + 1) * LANES]
            found = jnp.where(part == j, jnp.take_along_axis(columns, lane, axis=1), found)
        at = pl.multiple_of(tile * slot_total + q * LANES, LANES)
        target[pl.ds(at, LANES), :] = jnp.concatenate([found] * 4, axis=0).T


def block_diagonal(matrix):
    row = jnp.concatenate([matrix] * 8, axis=1)
    wide = jnp.concatenate([row] * 8, axis=0)
    rows = lax.broadcasted_iota(jnp.int32, (256, 256), 0) // DIM
    cols = lax.broadcasted_iota(jnp.int32, (256, 256), 1) // DIM
    return jnp.where(rows == cols, wide, 0.0)


def fold_lanes(values):
    values = values + pltpu.roll(values, 64, 1)
    return values + pltpu.roll(values, 32, 1)


def block_sums(product):
    rows = lax.broadcasted_iota(jnp.int32, (LANES, LANES), 0) // DIM
    cols = lax.broadcasted_iota(jnp.int32, (LANES, LANES), 1) // DIM
    kept = jnp.where(rows == cols, product, 0.0)
    folded = fold_lanes(kept[0:32] + kept[32:64] + kept[64:96] + kept[96:128])
    lane = lax.broadcasted_iota(jnp.int32, (8, LANES), 1) // DIM
    packed = jnp.where(lane == 0, folded[0:8], 0.0)
    for k in range(1, 4):
        packed = jnp.where(lane == k, folded[8 * k : 8 * k + 8], packed)
    return packed


def chunk_rows(k):
    return pl.ds(pl.multiple_of(k * CHUNK, CHUNK), CHUNK)


def slot_base(tile):
    return tile // 8 * 4096 + lax.rem(tile, 8) * LANES


def slot_step(edge):
    return edge // LANES * 1024 + edge % LANES


def target_onehot(edges_v, tile):
    targets = edges_v[1, pl.ds(tile, 1), :]
    return (targets == lax.broadcasted_iota(jnp.int32, (TILE, targets.shape[1]), 0)).astype(BF16)


def ring_targets():
    node = lax.axis_index("node")
    position = lax.rem(node, RING)
    plane = node - position
    after = plane + lax.rem(position + 1, RING)
    before = plane + lax.rem(position + RING - 1, RING)
    across = lax.rem(node + RING, 2 * RING)
    return node, position, (after, before, across)


def sum_chunk(k, first_row, slots_s, edges_v, head_ref, query_ref, win_ref, rel_ref, message_ref, mixed_ref):
    slot_total = edges_v.shape[2]

    def gather(j):
        base = slot_base(2 * k + j)
        for edge in range(slot_total):
            message_ref[j, 4 * edge : 4 * edge + 4, :] = win_ref[slots_s[base + slot_step(edge)]]

    def tile_step(j):
        tile = 2 * k + j

        onehot = target_onehot(edges_v, tile)
        row = j * TILE
        ids = first_row + tile * TILE + lax.broadcasted_iota(jnp.int32, (TILE, LANES), 0)
        scale = rel_ref[pl.ds(pl.multiple_of(tile * slot_total, slot_total), slot_total), :]
        message = jnp.concatenate(
            [(message_ref[j, pl.ds(c, slot_total, stride=4), :] * scale).astype(BF16) for c in range(4)], axis=1
        )
        summed = jnp.dot(onehot, message, preferred_element_type=F32)
        for c in range(4):
            cols = slice(c * LANES, (c + 1) * LANES)
            start = jnp.where(ids == head_ref[:, cols], query_ref[:, cols], 0.0)
            mixed_ref[pl.ds(row, TILE), cols] = start + summed[:, cols]

    for j in range(2):
        gather(j)
    for j in range(2):
        tile_step(j)


def forward_kernel(
    state_hbm, cot_hbm, slots_hbm, edges_hbm, table_hbm, rel_hbm, head_s, chosen_s, weight_ref, bias_ref,
    state_out, grad_out, mixed_out, slope_out, rel_out, sums_out, places_out,
    own, middle, mixed_own, cot, state_ref, grad_ref, slope_ref, inbox, win_a, win_b, rel_a, rel_b, padded, table_ref,
    message_ref, mixed_ref, wide_ref, head_ref, query_ref, slots_s, edges_v, table_t, rel_t, copy_sem, send_sem, recv_sem,
):
    node, position, targets = ring_targets()
    at_end = jnp.logical_or(position == 0, position == RING - 1)
    rows = own.shape[0]
    barrier = pltpu.get_barrier_semaphore()
    for target in targets:
        pl.semaphore_signal(barrier, inc=1, device_id={"node": target}, device_id_type=MESH)
    first = 8 + 2 * CHUNKS
    operand_copies = [
        pltpu.make_async_copy(source, target, copy_sem.at[first + i])
        for i, (source, target) in enumerate(
            (
                (table_hbm, table_t),
                (rel_hbm, rel_t),
                (edges_hbm, edges_v),
                (slots_hbm.at[pl.ds(0, slots_s.shape[0])], slots_s),
            )
        )
    ]
    own_copy = pltpu.make_async_copy(state_hbm, own, copy_sem.at[0])
    cot_copy = pltpu.make_async_copy(cot_hbm, cot, copy_sem.at[1])
    pl.semaphore_wait(barrier, 3)

    def piece(trip, way, k, source):
        return pltpu.make_async_remote_copy(
            src_ref=source.at[chunk_rows(k), :],
            dst_ref=inbox.at[trip, way, chunk_rows(k), :],
            send_sem=send_sem.at[trip, way, k],
            recv_sem=recv_sem.at[trip, way, k],
            device_id={"node": targets[way]},
            device_id_type=MESH,
        )

    def send_sides(trip, k, source):
        @pl.when(position != RING - 1)
        def _():
            piece(trip, 0, k, source).start()

        @pl.when(position != 0)
        def _():
            piece(trip, 1, k, source).start()

    def relay_chunk(trip, k):
        mirrored = inbox.at[trip, 2]
        piece(trip, 2, k, mirrored).wait_recv()

        @pl.when(position == RING - 1)
        def _():
            piece(trip, 0, k, mirrored).start()

        @pl.when(position == 0)
        def _():
            piece(trip, 1, k, mirrored).start()

    def fill(win, quarter, k, block):
        spread_rows(win, quarter * rows + k * CHUNK, block.astype(F32))

    def start_first(k):
        send_sides(0, k, state_hbm)

        @pl.when(jnp.logical_or(jnp.logical_not(at_end), k < WINDOW))
        def _():
            piece(0, 2, k, state_hbm).start()

    each(CHUNKS, start_first)
    for copy in operand_copies:
        copy.start()
    own_copy.start()
    cot_copy.start()
    for copy in operand_copies:
        copy.wait()

    spread_table(table_ref, table_t)
    for layer in range(2):
        pad_columns(padded.at[layer], rel_t.at[layer])
    places_out[...] = edges_v[0] * 4
    lane = lax.broadcasted_iota(jnp.int32, (1, LANES), 1) // DIM
    for c in range(4):
        heads = jnp.zeros((1, LANES), jnp.int32)
        vectors = jnp.zeros((1, LANES), F32)
        for k in range(4):
            heads = jnp.where(lane == k, head_s[4 * c + k], heads)
            vectors = jnp.where(lane == k, table_ref[chosen_s[4 * c + k]][0:1], vectors)
        head_ref[:, c * LANES : (c + 1) * LANES] = heads
        query_ref[:, c * LANES : (c + 1) * LANES] = vectors.astype(BF16).astype(F32)
    for layer in range(2):
        high, low = split_pair(block_diagonal(weight_ref[layer]))
        wide_ref[2 * layer] = high
        wide_ref[2 * layer + 1] = low
    bias_zero = jnp.concatenate([bias_ref[0:1, :]] * 8, axis=1)
    bias_one = jnp.concatenate([bias_ref[1:2, :]] * 8, axis=1)
    first_row = node * rows

    own_copy.wait()
    each(CHUNKS, lambda k: fill(win_a, 1, k, own[chunk_rows(k), :]))

    def relations_of(layer, target, k):
        relation_rows(target, padded.at[layer], edges_v, 2 * k)
        relation_rows(target, padded.at[layer], edges_v, 2 * k + 1)

    def take_first_mirror(k):
        relations_of(0, rel_a, k)
        relations_of(1, rel_b, k)
        relay_chunk(0, k)

        @pl.when(jnp.logical_and(at_end, k + WINDOW < CHUNKS))
        def _():
            piece(0, 2, k + WINDOW, state_hbm).start()

        fill(win_a, 3, k, inbox[0, 2, chunk_rows(k), :])

    def take_first_sides(k):
        for way, quarter in ((0, 0), (1, 2)):
            piece(0, way, k, own).wait_recv()
            fill(win_a, quarter, k, inbox[0, way, chunk_rows(k), :])

    each(CHUNKS, take_first_mirror)
    rel_copy = pltpu.make_async_copy(rel_b, rel_out, copy_sem.at[2])
    rel_copy.start()
    each(CHUNKS, take_first_sides)

    def next_state(state, update, quarter, k, half):
        sigma = jax.nn.sigmoid(update)
        place = pl.ds(pl.multiple_of(quarter * rows + k * CHUNK, CHUNK), CHUNK)
        slope_ref[place, half * 256 : half * 256 + 256] = (sigma * (1.0 + update * (1.0 - sigma))).astype(BF16)
        result = (state.astype(F32) + update * sigma).astype(BF16)
        for c in range(2):
            flat(win_b)[pl.ds((quarter * rows + k * CHUNK) * 4 + half * 2 + c, CHUNK, stride=4), :] = result[
                :, c * LANES : (c + 1) * LANES
            ].astype(F32)
        return result

    def remote_state(way, quarter, k):
        at = chunk_rows(k)
        for half in range(2):
            cols = slice(half * 256, half * 256 + 256)
            mixed = inbox[1, way, at, cols]
            update = half_dot(mixed, wide_ref[0], 0) + half_dot(mixed, wide_ref[1], 0) + bias_zero
            next_state(inbox[0, way, at, cols], update, quarter, k, half)

    def take_second_mirror(k):
        relay_chunk(1, k)
        remote_state(2, 3, k)

    def take_second_sides(k):
        for way, quarter in ((0, 0), (1, 2)):
            piece(1, way, k, own).wait_recv()
            remote_state(way, quarter, k)

    def zero_step(k):
        sum_chunk(k, first_row, slots_s, edges_v, head_ref, query_ref, win_a, rel_a, message_ref, mixed_ref)
        at = chunk_rows(k)
        mixed_own[at, :] = mixed_ref[...].astype(BF16)
        piece(1, 2, k, mixed_own).start()
        send_sides(1, k, mixed_own)
        for half in range(2):
            cols = slice(half * 256, half * 256 + 256)
            update = split_dot(mixed_ref[:, cols], wide_ref[0], wide_ref[1]) + bias_zero
            middle[at, cols] = next_state(own[at, cols], update, 1, k, half)
        @pl.when(k >= 2)
        def _():
            take_second_mirror(k - 2)

        @pl.when(k >= 5)
        def _():
            take_second_sides(k - 5)

    each(CHUNKS, zero_step)
    take_second_sides(CHUNKS - 5)
    take_second_mirror(CHUNKS - 2)
    take_second_sides(CHUNKS - 4)
    take_second_mirror(CHUNKS - 1)
    each(3, lambda k: take_second_sides(k + CHUNKS - 3))
    cot_copy.wait()
    window_copies = [pltpu.make_async_copy(slope_ref, slope_out, copy_sem.at[3])]
    for quarter, source in enumerate((inbox.at[1, 0], mixed_own, inbox.at[1, 1], inbox.at[1, 2])):
        window_copies.append(
            pltpu.make_async_copy(source, mixed_out.at[pl.ds(quarter * rows, rows), :], copy_sem.at[4 + quarter])
        )
    for copy in window_copies:
        copy.start()

    def result_copies(k):
        at = chunk_rows(k)
        return (
            pltpu.make_async_copy(state_ref.at[at, :], state_out.at[at, :], copy_sem.at[8 + 2 * k]),
            pltpu.make_async_copy(grad_ref.at[at, :], grad_out.at[at, :], copy_sem.at[9 + 2 * k]),
        )

    def one_step(k, carry):
        product, bias_sum = carry
        sum_chunk(k, first_row, slots_s, edges_v, head_ref, query_ref, win_b, rel_b, message_ref, mixed_ref)
        at = chunk_rows(k)
        for half in range(2):
            cols = slice(half * 256, half * 256 + 256)
            mixed = mixed_ref[:, cols]
            update = split_dot(mixed, wide_ref[2], wide_ref[3]) + bias_one
            sigma = jax.nn.sigmoid(update)
            state_ref[at, cols] = (middle[at, cols].astype(F32) + update * sigma).astype(BF16)
            grad = cot[at, cols].astype(F32) * (sigma * (1.0 + update * (1.0 - sigma)))
            grad_ref[at, cols] = split_dot(grad, wide_ref[2], wide_ref[3], 1).astype(BF16)
            for c in range(2):
                part = slice(c * LANES, (c + 1) * LANES)
                product += product_of(mixed[:, part].astype(BF16), grad[:, part].astype(BF16))
                bias_sum += jnp.sum(grad[:, part], axis=0, keepdims=True)
        for copy in result_copies(k):
            copy.start()
        return product, bias_sum

    product, bias_sum = lax.fori_loop(
        0, CHUNKS, one_step, (jnp.zeros((LANES, LANES), F32), jnp.zeros((1, LANES), F32))
    )
    sums_out[0:8, :] = block_sums(product)
    sums_out[8:16, :] = fold_lanes(jnp.broadcast_to(bias_sum, (8, LANES)))
    for trip in range(2):
        for way in range(3):
            each(CHUNKS, lambda k: piece(trip, way, k, own).wait_send())
    rel_copy.wait()
    for copy in window_copies:
        copy.wait()
    each(CHUNKS, lambda k: [copy.wait() for copy in result_copies(k)])


def scatter_kernel(
    state_in, mixed_in, slope_in, rel_in, cot_in, places_in, edges_in, grad_in, sums_in, state_out, sums_out,
    first_ref, second_ref, third_ref, fourth_ref, rel_ref, mixed_ref, slope_ref, cot_ref, state_ref, term_ref,
    places_s, edges_v, grad_ref, copy_sem,
):
    copies = [
        pltpu.make_async_copy(source, target, copy_sem.at[i])
        for i, (source, target) in enumerate(
            ((state_in, state_ref), (mixed_in, mixed_ref), (slope_in, slope_ref), (cot_in, cot_ref))
        )
    ]
    part_rows = rel_ref.shape[0] // 4

    def rel_part(i):
        at = pl.ds(pl.multiple_of(i * part_rows, part_rows), part_rows)
        return pltpu.make_async_copy(rel_in.at[at, :], rel_ref.at[at, :], copy_sem.at[5 + i])

    early = [
        pltpu.make_async_copy(source, target, copy_sem.at[9 + i])
        for i, (source, target) in enumerate(((places_in, places_s), (edges_in, edges_v), (grad_in, grad_ref)))
    ]
    for copy in early:
        copy.start()
    rel_part(0).start()
    totals = (first_ref, second_ref, third_ref, fourth_ref)
    tiles, slot_total = edges_v.shape[1:]
    half_total = slot_total // 2

    def clear(i):
        at = pl.ds(pl.multiple_of(i * 256, 256), 256)
        for total in totals:
            total[at, :] = jnp.zeros((256, LANES), F32)

    each(first_ref.shape[0] // 256, clear)
    for copy in early:
        copy.wait()
    rel_part(0).wait()
    for i in range(1, 4):
        rel_part(i).start()
    for copy in copies:
        copy.start()
    state_copy = pltpu.make_async_copy(state_ref, state_out, copy_sem.at[4])

    def make_terms(tile, half):
        edges = slice(half * half_total, half * half_total + half_total)
        onehot = target_onehot(edges_v, tile)[:, edges]
        start = pl.multiple_of(tile * slot_total + half * half_total, half_total)
        scale = rel_ref[pl.ds(start, half_total), :]
        picked = product_of(onehot, grad_ref[pl.ds(pl.multiple_of(tile * TILE, TILE), TILE), :])
        for c in range(4):
            place = pl.ds(4 * half * half_total + c, half_total, stride=4)
            term_ref[place, :] = picked[:, c * LANES : (c + 1) * LANES] * scale

    def add_terms(tile, half):
        base = slot_base(tile)
        for edge in range(half * half_total, (half + 1) * half_total):
            total = totals[edge % SUMS]
            place = pl.ds(pl.multiple_of(places_s[base + slot_step(edge)], 4), 4)
            total[place, :] = total[place, :] + term_ref[4 * edge : 4 * edge + 4, :]

    make_terms(0, 0)

    def tile_step(tile):
        @pl.when(jnp.logical_and(tile & 3 == 3, tile < tiles - 1))
        def _():
            rel_part(tile // 4 + 1).wait()

        add_terms(tile, 0)
        make_terms(tile, 1)
        add_terms(tile, 1)
        make_terms(jnp.minimum(tile + 1, tiles - 1), 0)

    each(tiles, tile_step)
    for copy in copies:
        copy.wait()
    state_copy.start()

    rows = cot_ref.shape[0]

    def collect(quarter, i, carry):
        product, bias_sum = carry
        start = quarter * rows + pl.multiple_of(i * COLLECT, COLLECT)
        at = pl.ds(start, COLLECT)
        grads, mixed = [], []
        for c in range(4):
            cols = slice(c * LANES, (c + 1) * LANES)
            place = pl.ds(start * 4 + c, COLLECT, stride=4)
            terms = (first_ref[place, :] + second_ref[place, :]) + (third_ref[place, :] + fourth_ref[place, :])
            if quarter == 1:
                own_rows = pl.ds(pl.multiple_of(i * COLLECT, COLLECT), COLLECT)
                terms += cot_ref[own_rows, cols].astype(F32)
            grad = terms * slope_ref[at, cols].astype(F32)
            bias_sum += jnp.sum(grad, axis=0, keepdims=True)
            grads.append(grad.astype(BF16))
            mixed.append(mixed_ref[at, cols])
        product += product_of(jnp.concatenate(mixed, axis=0), jnp.concatenate(grads, axis=0))
        return product, bias_sum

    sums = (jnp.zeros((LANES, LANES), F32), jnp.zeros((1, LANES), F32))
    for quarter in range(4):
        sums = lax.fori_loop(0, rows // COLLECT, functools.partial(collect, quarter), sums)
    product, bias_sum = sums
    sums_out[0:8, :] = block_sums(product)
    sums_out[8:16, :] = sums_in[0:8, :]
    sub = lax.broadcasted_iota(jnp.int32, (8, LANES), 0)
    sums_out[16:24, :] = jnp.where(sub == 0, fold_lanes(jnp.broadcast_to(bias_sum, (8, LANES))), sums_in[8:16, :])
    state_copy.wait()


def total_kernel(
    sums_ref, total_out, mine, first_buf, second_buf, first_send, first_recv, second_send, second_recv
):
    node = lax.axis_index("node")
    query = lax.axis_index("query")
    position = lax.rem(node, RING)
    half = node // RING
    in_first = half * 4 + query
    barrier = pltpu.get_barrier_semaphore()

    def first_peer(j):
        return {"node": (j // 4) * RING + position, "query": lax.rem(j, 4)}

    def second_peer(j):
        return {"node": half * RING + j, "query": query}

    for d in range(1, 8):
        pl.semaphore_signal(barrier, inc=1, device_id=first_peer(lax.rem(in_first + d, 8)), device_id_type=MESH)
    for d in range(1, RING):
        pl.semaphore_signal(barrier, inc=1, device_id=second_peer(lax.rem(position + d, RING)), device_id_type=MESH)
    pl.semaphore_wait(barrier, 22)

    def stage(source, buf, send, recv, me, peer, count):
        def piece(slot, to):
            return pltpu.make_async_remote_copy(
                src_ref=source, dst_ref=buf.at[slot], send_sem=send.at[to], recv_sem=recv.at[slot],
                device_id=peer(to), device_id_type=MESH,
            )

        others = [lax.rem(me + d, count) for d in range(1, count)]
        for to in others:
            piece(me, to).start()
        buf[me] = source[...]
        for other in others:
            piece(other, other).wait_recv()
        total = buf[0]
        for j in range(1, count):
            total = total + buf[j]
        return total, lambda: [piece(me, to).wait_send() for to in others]

    total, finish_first = stage(sums_ref, first_buf, first_send, first_recv, in_first, first_peer, 8)
    mine[...] = total
    total, finish_second = stage(mine, second_buf, second_send, second_recv, position, second_peer, RING)
    total_out[...] = total
    finish_first()
    finish_second()


def unpack_kernel(total_ref, weight_out, bias_out):
    total = total_ref[...]
    for l in range(2):
        packed = total[8 * l : 8 * l + 8, :]
        for k in range(4):
            moved = packed if k == 0 else pltpu.roll(packed, LANES - 32 * k, 1)
            weight_out[l, 8 * k : 8 * k + 8, :] = moved[:, 0:32]
    bias_out[...] = total[16:18, 0:32]


def in_memory_order(table):
    cols = table.shape[-1]
    return table.reshape(-1, 8, cols // LANES, LANES).transpose(0, 2, 1, 3).reshape(table.size)


def body(
    entity_state, edge_tiles, query_head, query_relation, query_table, rel_vectors, mix_weight, mix_bias, cotangent
):
    rows, cols = entity_state.shape
    tiles, unused, slot_total = edge_tiles.shape
    edge_count = tiles * slot_total
    rel_rows = rel_vectors.shape[1]
    padded_rows = -(-rel_rows // LANES) * LANES
    edges = edge_tiles.transpose(1, 0, 2)
    slots = in_memory_order(edges)
    table_t = query_table.T
    rel_t = rel_vectors.transpose(0, 2, 1)
    smem = pl.BlockSpec(memory_space=pltpu.SMEM)
    vmem = pl.BlockSpec(memory_space=pltpu.VMEM)
    anywhere = pl.BlockSpec(memory_space=pl.ANY)
    half = jax.ShapeDtypeStruct((rows, cols), BF16)
    wide = jax.ShapeDtypeStruct((4 * rows, cols), BF16)
    packet = (24, LANES)
    block = pltpu.VMEM((rows, cols), BF16)
    window = pltpu.VMEM((rows * 4, 4, LANES), F32)
    edge_rows = pltpu.VMEM((edge_count, LANES), F32)
    padded = pltpu.VMEM((2, DIM, padded_rows), F32)
    message = pltpu.VMEM((slot_total * 4, LANES), F32)
    state_two, grad_mixed, mixed_zero, slope_zero, rel_one, sums, places = pl.pallas_call(
        forward_kernel,
        out_shape=(
            half,
            half,
            wide,
            wide,
            jax.ShapeDtypeStruct((edge_count, LANES), F32),
            jax.ShapeDtypeStruct((16, LANES), F32),
            jax.ShapeDtypeStruct((tiles, slot_total), jnp.int32),
        ),
        in_specs=[anywhere] * 6 + [smem] * 2 + [vmem] * 2,
        out_specs=(anywhere,) * 5 + (vmem,) * 2,
        scratch_shapes=[block] * 6
        + [
            pltpu.VMEM((4 * rows, cols), BF16),
            pltpu.VMEM((2, 3, rows, cols), BF16),
            window,
            window,
            edge_rows,
            edge_rows,
            padded,
            pltpu.VMEM((rel_rows, 4, LANES), F32),
            pltpu.VMEM((2, slot_total * 4, LANES), F32),
            pltpu.VMEM((CHUNK, cols), F32),
            pltpu.VMEM((4, 256, 256), BF16),
            pltpu.VMEM((1, cols), jnp.int32),
            pltpu.VMEM((1, cols), F32),
            pltpu.SMEM((edge_count,), jnp.int32),
            pltpu.VMEM(edges.shape, jnp.int32),
            pltpu.VMEM(table_t.shape, F32),
            pltpu.VMEM(rel_t.shape, F32),
            pltpu.SemaphoreType.DMA((12 + 2 * CHUNKS,)),
            pltpu.SemaphoreType.DMA((2, 3, CHUNKS)),
            pltpu.SemaphoreType.DMA((2, 3, CHUNKS)),
        ],
        compiler_params=pltpu.CompilerParams(
            vmem_limit_bytes=VMEM_BYTES, collective_id=0, has_side_effects=True
        ),
        name="two_layers",
    )(
        entity_state, cotangent, slots, edges, table_t, rel_t, query_head, query_relation, mix_weight, mix_bias
    )
    state_out, sums = pl.pallas_call(
        scatter_kernel,
        out_shape=(half, jax.ShapeDtypeStruct(packet, F32)),
        in_specs=[anywhere] * 8 + [vmem],
        out_specs=(anywhere, vmem),
        scratch_shapes=[pltpu.VMEM((rows * 16, LANES), F32)] * SUMS
        + [
            edge_rows,
            pltpu.VMEM((4 * rows, cols), BF16),
            pltpu.VMEM((4 * rows, cols), BF16),
            block,
            block,
            message,
            pltpu.SMEM((edge_count,), jnp.int32),
            pltpu.VMEM(edges.shape, jnp.int32),
            block,
            pltpu.SemaphoreType.DMA((12,)),
        ],
        compiler_params=pltpu.CompilerParams(vmem_limit_bytes=VMEM_BYTES),
        name="scatter_terms",
    )(state_two, mixed_zero, slope_zero, rel_one, cotangent, in_memory_order(places), edges, grad_mixed, sums)
    total = pl.pallas_call(
        total_kernel,
        out_shape=jax.ShapeDtypeStruct(packet, F32),
        in_specs=[vmem],
        out_specs=vmem,
        scratch_shapes=[
            pltpu.VMEM(packet, F32),
            pltpu.VMEM((8,) + packet, F32),
            pltpu.VMEM((RING,) + packet, F32),
            pltpu.SemaphoreType.DMA((8,)),
            pltpu.SemaphoreType.DMA((8,)),
            pltpu.SemaphoreType.DMA((RING,)),
            pltpu.SemaphoreType.DMA((RING,)),
        ],
        compiler_params=pltpu.CompilerParams(collective_id=1, has_side_effects=True),
        name="total_sums",
    )(sums)
    weight_grads, bias_grads = pl.pallas_call(
        unpack_kernel,
        out_shape=(jax.ShapeDtypeStruct((2, DIM, DIM), F32), jax.ShapeDtypeStruct((2, DIM), F32)),
        in_specs=[vmem],
        out_specs=(vmem,) * 2,
        name="unpack_sums",
    )(total)
    return state_out, weight_grads, bias_grads


def solution(mesh):
    placed = (
        P("node", "query"),
        P("node", None, None),
        P("query"),
        P("query"),
        P(),
        P(),
        P(),
        P(),
        P("node", "query"),
    )
    return jax.shard_map(
        body, mesh=mesh, in_specs=placed, out_specs=(P("node", "query"), P(), P()), check_vma=False
    )
```

```python
import functools

import jax
import jax.numpy as jnp
from jax import lax
from jax.experimental import pallas as pl
from jax.experimental.pallas import tpu as pltpu
from jax.sharding import PartitionSpec as P

DIM = 32
LANES = 128
TILE = 64
CHUNK = 128
CHUNKS = 8
RING = 16
WINDOW = 3
PIECE = 64
PIECES = CHUNK // PIECE
SUMS = 4
COLLECT = 1024
F32 = jnp.float32
BF16 = jnp.bfloat16
MESH = pl.DeviceIdType.MESH
VMEM_BYTES = 58 << 20


def split_pair(matrix):
    high = matrix.astype(BF16)
    return high, (matrix - high.astype(F32)).astype(BF16)


def half_dot(left, right, right_dim):
    return lax.dot_general(left, right, (((1,), (right_dim,)), ((), ())), preferred_element_type=F32)


def split_dot(left, right_high, right_low, right_dim=0):
    high, low = split_pair(left)
    total = half_dot(high, right_high, right_dim) + half_dot(low, right_high, right_dim)
    return total + half_dot(high, right_low, right_dim)


def product_of(left, right):
    return lax.dot_general(left, right, (((0,), (0,)), ((), ())), preferred_element_type=F32)


def each(count, step):
    def run(i, carry):
        step(i)
        return carry

    lax.fori_loop(0, count, run, 0)


def flat(target):
    return target.reshape(target.shape[0] * 4, LANES)


def spread_rows(target, first, block):
    rows = block.shape[0]
    for c in range(4):
        flat(target)[pl.ds(first * 4 + c, rows, stride=4), :] = block[:, c * LANES : (c + 1) * LANES]


def spread_table(target, columns_ref):
    count = columns_ref.shape[1]
    for start in range(0, count, LANES):
        width = min(LANES, count - start)
        wide = jnp.concatenate([columns_ref[:, start : start + width]] * 4, axis=0).T
        for c in range(4):
            flat(target)[pl.ds(start * 4 + c, width, stride=4), :] = wide


def pad_columns(target, columns_ref):
    count = columns_ref.shape[1]
    whole = count // LANES * LANES
    target[:, 0:whole] = columns_ref[:, 0:whole]
    if whole < count:
        rest = jnp.zeros((columns_ref.shape[0], LANES - count + whole), F32)
        target[:, whole : whole + LANES] = jnp.concatenate([columns_ref[:, whole:count], rest], axis=1)


def relation_rows(target, table_ref, edges_v, tile):
    slot_total = edges_v.shape[2]
    row = edges_v[2, pl.ds(tile, 1), :]
    for q in range(slot_total // LANES):
        ids = jnp.broadcast_to(row[:, q * LANES : (q + 1) * LANES], (DIM, LANES))
        lane, part = ids & (LANES - 1), ids >> 7
        found = jnp.zeros((DIM, LANES), F32)
        for j in range(table_ref.shape[1] // LANES):
            columns = table_ref[:, j * LANES : (j + 1) * LANES]
            found = jnp.where(part == j, jnp.take_along_axis(columns, lane, axis=1), found)
        at = pl.multiple_of(tile * slot_total + q * LANES, LANES)
        target[pl.ds(at, LANES), :] = jnp.concatenate([found] * 4, axis=0).T


def block_diagonal(matrix):
    row = jnp.concatenate([matrix] * 8, axis=1)
    wide = jnp.concatenate([row] * 8, axis=0)
    rows = lax.broadcasted_iota(jnp.int32, (256, 256), 0) // DIM
    cols = lax.broadcasted_iota(jnp.int32, (256, 256), 1) // DIM
    return jnp.where(rows == cols, wide, 0.0)


def fold_lanes(values):
    values = values + pltpu.roll(values, 64, 1)
    return values + pltpu.roll(values, 32, 1)


def block_sums(product):
    rows = lax.broadcasted_iota(jnp.int32, (LANES, LANES), 0) // DIM
    cols = lax.broadcasted_iota(jnp.int32, (LANES, LANES), 1) // DIM
    kept = jnp.where(rows == cols, product, 0.0)
    folded = fold_lanes(kept[0:32] + kept[32:64] + kept[64:96] + kept[96:128])
    lane = lax.broadcasted_iota(jnp.int32, (8, LANES), 1) // DIM
    packed = jnp.where(lane == 0, folded[0:8], 0.0)
    for k in range(1, 4):
        packed = jnp.where(lane == k, folded[8 * k : 8 * k + 8], packed)
    return packed


def chunk_rows(k):
    return pl.ds(pl.multiple_of(k * CHUNK, CHUNK), CHUNK)


def slot_base(tile):
    return tile // 8 * 4096 + lax.rem(tile, 8) * LANES


def slot_step(edge):
    return edge // LANES * 1024 + edge % LANES


def target_onehot(edges_v, tile):
    targets = edges_v[1, pl.ds(tile, 1), :]
    return (targets == lax.broadcasted_iota(jnp.int32, (TILE, targets.shape[1]), 0)).astype(BF16)


def ring_targets():
    node = lax.axis_index("node")
    position = lax.rem(node, RING)
    plane = node - position
    after = plane + lax.rem(position + 1, RING)
    before = plane + lax.rem(position + RING - 1, RING)
    across = lax.rem(node + RING, 2 * RING)
    return node, position, (after, before, across)


def sum_chunk(k, first_row, slots_s, edges_v, head_ref, query_ref, win_ref, rel_ref, message_ref, mixed_ref):
    slot_total = edges_v.shape[2]

    def gather(j):
        base = slot_base(2 * k + j)
        for edge in range(slot_total):
            message_ref[j, 4 * edge : 4 * edge + 4, :] = win_ref[slots_s[base + slot_step(edge)]]

    def tile_step(j):
        tile = 2 * k + j

        onehot = target_onehot(edges_v, tile)
        row = j * TILE
        ids = first_row + tile * TILE + lax.broadcasted_iota(jnp.int32, (TILE, LANES), 0)
        scale = rel_ref[pl.ds(pl.multiple_of(tile * slot_total, slot_total), slot_total), :]
        message = jnp.concatenate(
            [(message_ref[j, pl.ds(c, slot_total, stride=4), :] * scale).astype(BF16) for c in range(4)], axis=1
        )
        summed = jnp.dot(onehot, message, preferred_element_type=F32)
        for c in range(4):
            cols = slice(c * LANES, (c + 1) * LANES)
            start = jnp.where(ids == head_ref[:, cols], query_ref[:, cols], 0.0)
            mixed_ref[pl.ds(row, TILE), cols] = start + summed[:, cols]

    for j in range(2):
        gather(j)
    for j in range(2):
        tile_step(j)


def forward_kernel(
    state_hbm, cot_hbm, slots_hbm, edges_hbm, table_hbm, rel_hbm, head_s, chosen_s, weight_ref, bias_ref,
    state_out, grad_out, mixed_out, slope_out, rel_out, sums_out, places_out,
    own, middle, mixed_own, cot, state_ref, grad_ref, slope_ref, inbox, win_a, win_b, rel_a, rel_b, padded, table_ref,
    message_ref, mixed_ref, wide_ref, head_ref, query_ref, slots_s, edges_v, table_t, rel_t, copy_sem, send_sem, recv_sem,
):
    node, position, targets = ring_targets()
    at_end = jnp.logical_or(position == 0, position == RING - 1)
    rows = own.shape[0]
    barrier = pltpu.get_barrier_semaphore()
    for target in targets:
        pl.semaphore_signal(barrier, inc=1, device_id={"node": target}, device_id_type=MESH)
    first = 8 + 2 * CHUNKS
    operand_copies = [
        pltpu.make_async_copy(source, target, copy_sem.at[first + i])
        for i, (source, target) in enumerate(
            (
                (table_hbm, table_t),
                (rel_hbm, rel_t),
                (edges_hbm, edges_v),
                (slots_hbm.at[pl.ds(0, slots_s.shape[0])], slots_s),
            )
        )
    ]
    own_copy = pltpu.make_async_copy(state_hbm, own, copy_sem.at[0])
    cot_copy = pltpu.make_async_copy(cot_hbm, cot, copy_sem.at[1])
    pl.semaphore_wait(barrier, 3)

    def piece(trip, way, i, source):
        at = pl.ds(pl.multiple_of(i * PIECE, PIECE), PIECE)
        return pltpu.make_async_remote_copy(
            src_ref=source.at[at, :],
            dst_ref=inbox.at[trip, way, at, :],
            send_sem=send_sem.at[trip, way, i],
            recv_sem=recv_sem.at[trip, way, i],
            device_id={"node": targets[way]},
            device_id_type=MESH,
        )

    def start_chunk(trip, way, k, source):
        for i in range(PIECES):
            piece(trip, way, k * PIECES + i, source).start()

    def receive_chunk(trip, way, k):
        for i in range(PIECES):
            piece(trip, way, k * PIECES + i, own).wait_recv()

    def send_sides(trip, k, source):
        @pl.when(position != RING - 1)
        def _():
            start_chunk(trip, 0, k, source)

        @pl.when(position != 0)
        def _():
            start_chunk(trip, 1, k, source)

    def relay_chunk(trip, k):
        mirrored = inbox.at[trip, 2]
        for i in range(PIECES):
            j = k * PIECES + i
            piece(trip, 2, j, mirrored).wait_recv()

            @pl.when(position == RING - 1)
            def _():
                piece(trip, 0, j, mirrored).start()

            @pl.when(position == 0)
            def _():
                piece(trip, 1, j, mirrored).start()

    def fill(win, quarter, k, block):
        spread_rows(win, quarter * rows + k * CHUNK, block.astype(F32))

    def start_first(k):
        send_sides(0, k, state_hbm)

        @pl.when(jnp.logical_or(jnp.logical_not(at_end), k < WINDOW))
        def _():
            start_chunk(0, 2, k, state_hbm)

    each(CHUNKS, start_first)
    for copy in operand_copies:
        copy.start()
    own_copy.start()
    cot_copy.start()
    for copy in operand_copies:
        copy.wait()

    spread_table(table_ref, table_t)
    for layer in range(2):
        pad_columns(padded.at[layer], rel_t.at[layer])
    places_out[...] = edges_v[0] * 4
    lane = lax.broadcasted_iota(jnp.int32, (1, LANES), 1) // DIM
    for c in range(4):
        heads = jnp.zeros((1, LANES), jnp.int32)
        vectors = jnp.zeros((1, LANES), F32)
        for k in range(4):
            heads = jnp.where(lane == k, head_s[4 * c + k], heads)
            vectors = jnp.where(lane == k, table_ref[chosen_s[4 * c + k]][0:1], vectors)
        head_ref[:, c * LANES : (c + 1) * LANES] = heads
        query_ref[:, c * LANES : (c + 1) * LANES] = vectors.astype(BF16).astype(F32)
    for layer in range(2):
        high, low = split_pair(block_diagonal(weight_ref[layer]))
        wide_ref[2 * layer] = high
        wide_ref[2 * layer + 1] = low
    bias_zero = jnp.concatenate([bias_ref[0:1, :]] * 8, axis=1)
    bias_one = jnp.concatenate([bias_ref[1:2, :]] * 8, axis=1)
    first_row = node * rows

    own_copy.wait()
    each(CHUNKS, lambda k: fill(win_a, 1, k, own[chunk_rows(k), :]))

    def relations_of(layer, target, k):
        relation_rows(target, padded.at[layer], edges_v, 2 * k)
        relation_rows(target, padded.at[layer], edges_v, 2 * k + 1)

    def take_first_mirror(k):
        relations_of(0, rel_a, k)
        relations_of(1, rel_b, k)
        relay_chunk(0, k)

        @pl.when(jnp.logical_and(at_end, k + WINDOW < CHUNKS))
        def _():
            start_chunk(0, 2, k + WINDOW, state_hbm)

        fill(win_a, 3, k, inbox[0, 2, chunk_rows(k), :])

    def take_first_sides(k):
        for way, quarter in ((0, 0), (1, 2)):
            receive_chunk(0, way, k)
            fill(win_a, quarter, k, inbox[0, way, chunk_rows(k), :])

    each(CHUNKS, take_first_mirror)
    rel_copy = pltpu.make_async_copy(rel_b, rel_out, copy_sem.at[2])
    rel_copy.start()
    each(CHUNKS, take_first_sides)

    def next_state(state, update, quarter, k, half):
        sigma = jax.nn.sigmoid(update)
        place = pl.ds(pl.multiple_of(quarter * rows + k * CHUNK, CHUNK), CHUNK)
        slope_ref[place, half * 256 : half * 256 + 256] = (sigma * (1.0 + update * (1.0 - sigma))).astype(BF16)
        result = (state.astype(F32) + update * sigma).astype(BF16)
        for c in range(2):
            flat(win_b)[pl.ds((quarter * rows + k * CHUNK) * 4 + half * 2 + c, CHUNK, stride=4), :] = result[
                :, c * LANES : (c + 1) * LANES
            ].astype(F32)
        return result

    def remote_state(way, quarter, k):
        at = chunk_rows(k)
        for half in range(2):
            cols = slice(half * 256, half * 256 + 256)
            mixed = inbox[1, way, at, cols]
            update = half_dot(mixed, wide_ref[0], 0) + half_dot(mixed, wide_ref[1], 0) + bias_zero
            next_state(inbox[0, way, at, cols], update, quarter, k, half)

    def take_second_mirror(k):
        relay_chunk(1, k)
        remote_state(2, 3, k)

    def take_second_sides(k):
        for way, quarter in ((0, 0), (1, 2)):
            receive_chunk(1, way, k)
            remote_state(way, quarter, k)

    def zero_step(k):
        sum_chunk(k, first_row, slots_s, edges_v, head_ref, query_ref, win_a, rel_a, message_ref, mixed_ref)
        at = chunk_rows(k)
        mixed_own[at, :] = mixed_ref[...].astype(BF16)
        start_chunk(1, 2, k, mixed_own)
        send_sides(1, k, mixed_own)
        for half in range(2):
            cols = slice(half * 256, half * 256 + 256)
            update = split_dot(mixed_ref[:, cols], wide_ref[0], wide_ref[1]) + bias_zero
            middle[at, cols] = next_state(own[at, cols], update, 1, k, half)
        @pl.when(k >= 2)
        def _():
            take_second_mirror(k - 2)

        @pl.when(k >= 5)
        def _():
            take_second_sides(k - 5)

    each(CHUNKS, zero_step)
    take_second_sides(CHUNKS - 5)
    take_second_mirror(CHUNKS - 2)
    take_second_sides(CHUNKS - 4)
    take_second_mirror(CHUNKS - 1)
    each(3, lambda k: take_second_sides(k + CHUNKS - 3))
    cot_copy.wait()
    window_copies = [pltpu.make_async_copy(slope_ref, slope_out, copy_sem.at[3])]
    for quarter, source in enumerate((inbox.at[1, 0], mixed_own, inbox.at[1, 1], inbox.at[1, 2])):
        window_copies.append(
            pltpu.make_async_copy(source, mixed_out.at[pl.ds(quarter * rows, rows), :], copy_sem.at[4 + quarter])
        )
    for copy in window_copies:
        copy.start()

    def result_copies(k):
        at = chunk_rows(k)
        return (
            pltpu.make_async_copy(state_ref.at[at, :], state_out.at[at, :], copy_sem.at[8 + 2 * k]),
            pltpu.make_async_copy(grad_ref.at[at, :], grad_out.at[at, :], copy_sem.at[9 + 2 * k]),
        )

    def one_step(k, carry):
        product, bias_sum = carry
        sum_chunk(k, first_row, slots_s, edges_v, head_ref, query_ref, win_b, rel_b, message_ref, mixed_ref)
        at = chunk_rows(k)
        for half in range(2):
            cols = slice(half * 256, half * 256 + 256)
            mixed = mixed_ref[:, cols]
            update = split_dot(mixed, wide_ref[2], wide_ref[3]) + bias_one
            sigma = jax.nn.sigmoid(update)
            state_ref[at, cols] = (middle[at, cols].astype(F32) + update * sigma).astype(BF16)
            grad = cot[at, cols].astype(F32) * (sigma * (1.0 + update * (1.0 - sigma)))
            rounded = grad.astype(BF16)
            back = half_dot(rounded, wide_ref[2], 1) + half_dot(rounded, wide_ref[3], 1)
            grad_ref[at, cols] = back.astype(BF16)
            for c in range(2):
                part = slice(c * LANES, (c + 1) * LANES)
                product += product_of(mixed[:, part].astype(BF16), rounded[:, part])
                bias_sum += jnp.sum(grad[:, part], axis=0, keepdims=True)
        for copy in result_copies(k):
            copy.start()
        return product, bias_sum

    product, bias_sum = lax.fori_loop(
        0, CHUNKS, one_step, (jnp.zeros((LANES, LANES), F32), jnp.zeros((1, LANES), F32))
    )
    sums_out[0:8, :] = block_sums(product)
    sums_out[8:16, :] = fold_lanes(jnp.broadcast_to(bias_sum, (8, LANES)))
    for trip in range(2):
        for way in range(3):
            each(CHUNKS * PIECES, lambda i: piece(trip, way, i, own).wait_send())
    rel_copy.wait()
    for copy in window_copies:
        copy.wait()
    each(CHUNKS, lambda k: [copy.wait() for copy in result_copies(k)])


def scatter_kernel(
    state_in, mixed_in, slope_in, rel_in, cot_in, places_in, edges_in, grad_in, sums_in, state_out, sums_out,
    first_ref, second_ref, third_ref, fourth_ref, rel_ref, mixed_ref, slope_ref, cot_ref, state_ref, term_ref,
    places_s, edges_v, grad_ref, copy_sem,
):
    copies = [
        pltpu.make_async_copy(source, target, copy_sem.at[i])
        for i, (source, target) in enumerate(
            ((state_in, state_ref), (mixed_in, mixed_ref), (slope_in, slope_ref), (cot_in, cot_ref))
        )
    ]
    part_rows = rel_ref.shape[0] // 4

    def rel_part(i):
        at = pl.ds(pl.multiple_of(i * part_rows, part_rows), part_rows)
        return pltpu.make_async_copy(rel_in.at[at, :], rel_ref.at[at, :], copy_sem.at[5 + i])

    early = [
        pltpu.make_async_copy(source, target, copy_sem.at[9 + i])
        for i, (source, target) in enumerate(((places_in, places_s), (edges_in, edges_v), (grad_in, grad_ref)))
    ]
    for copy in early:
        copy.start()
    rel_part(0).start()
    totals = (first_ref, second_ref, third_ref, fourth_ref)
    tiles, slot_total = edges_v.shape[1:]
    half_total = slot_total // 2

    def clear(i):
        at = pl.ds(pl.multiple_of(i * 256, 256), 256)
        for total in totals:
            total[at, :] = jnp.zeros((256, LANES), F32)

    each(first_ref.shape[0] // 256, clear)
    for copy in early:
        copy.wait()
    rel_part(0).wait()
    for i in range(1, 4):
        rel_part(i).start()
    for copy in copies:
        copy.start()
    state_copy = pltpu.make_async_copy(state_ref, state_out, copy_sem.at[4])

    def make_terms(tile, half):
        edges = slice(half * half_total, half * half_total + half_total)
        onehot = target_onehot(edges_v, tile)[:, edges]
        start = pl.multiple_of(tile * slot_total + half * half_total, half_total)
        scale = rel_ref[pl.ds(start, half_total), :]
        picked = product_of(onehot, grad_ref[pl.ds(pl.multiple_of(tile * TILE, TILE), TILE), :])
        for c in range(4):
            place = pl.ds(4 * half * half_total + c, half_total, stride=4)
            term_ref[place, :] = picked[:, c * LANES : (c + 1) * LANES] * scale

    def add_terms(tile, half):
        base = slot_base(tile)
        for edge in range(half * half_total, (half + 1) * half_total):
            total = totals[edge % SUMS]
            place = pl.ds(pl.multiple_of(places_s[base + slot_step(edge)], 4), 4)
            total[place, :] = total[place, :] + term_ref[4 * edge : 4 * edge + 4, :]

    make_terms(0, 0)

    def tile_step(tile):
        @pl.when(jnp.logical_and(tile & 3 == 3, tile < tiles - 1))
        def _():
            rel_part(tile // 4 + 1).wait()

        add_terms(tile, 0)
        make_terms(tile, 1)
        add_terms(tile, 1)
        make_terms(jnp.minimum(tile + 1, tiles - 1), 0)

    each(tiles, tile_step)
    for copy in copies:
        copy.wait()
    state_copy.start()

    rows = cot_ref.shape[0]

    def collect(quarter, i, carry):
        product, bias_sum = carry
        start = quarter * rows + pl.multiple_of(i * COLLECT, COLLECT)
        at = pl.ds(start, COLLECT)
        grads, mixed = [], []
        for c in range(4):
            cols = slice(c * LANES, (c + 1) * LANES)
            place = pl.ds(start * 4 + c, COLLECT, stride=4)
            terms = (first_ref[place, :] + second_ref[place, :]) + (third_ref[place, :] + fourth_ref[place, :])
            if quarter == 1:
                own_rows = pl.ds(pl.multiple_of(i * COLLECT, COLLECT), COLLECT)
                terms += cot_ref[own_rows, cols].astype(F32)
            grad = terms * slope_ref[at, cols].astype(F32)
            bias_sum += jnp.sum(grad, axis=0, keepdims=True)
            grads.append(grad.astype(BF16))
            mixed.append(mixed_ref[at, cols])
        product += product_of(jnp.concatenate(mixed, axis=0), jnp.concatenate(grads, axis=0))
        return product, bias_sum

    sums = (jnp.zeros((LANES, LANES), F32), jnp.zeros((1, LANES), F32))
    for quarter in range(4):
        sums = lax.fori_loop(0, rows // COLLECT, functools.partial(collect, quarter), sums)
    product, bias_sum = sums
    sums_out[0:8, :] = block_sums(product)
    sums_out[8:16, :] = sums_in[0:8, :]
    sub = lax.broadcasted_iota(jnp.int32, (8, LANES), 0)
    sums_out[16:24, :] = jnp.where(sub == 0, fold_lanes(jnp.broadcast_to(bias_sum, (8, LANES))), sums_in[8:16, :])
    state_copy.wait()


def total_kernel(
    sums_ref, total_out, mine, first_buf, second_buf, first_send, first_recv, second_send, second_recv
):
    node = lax.axis_index("node")
    query = lax.axis_index("query")
    position = lax.rem(node, RING)
    half = node // RING
    in_first = half * 4 + query
    barrier = pltpu.get_barrier_semaphore()

    def first_peer(j):
        return {"node": (j // 4) * RING + position, "query": lax.rem(j, 4)}

    def second_peer(j):
        return {"node": half * RING + j, "query": query}

    for d in range(1, 8):
        pl.semaphore_signal(barrier, inc=1, device_id=first_peer(lax.rem(in_first + d, 8)), device_id_type=MESH)
    for d in range(1, RING):
        pl.semaphore_signal(barrier, inc=1, device_id=second_peer(lax.rem(position + d, RING)), device_id_type=MESH)
    pl.semaphore_wait(barrier, 22)

    def stage(source, buf, send, recv, me, peer, count):
        def piece(slot, to):
            return pltpu.make_async_remote_copy(
                src_ref=source, dst_ref=buf.at[slot], send_sem=send.at[to], recv_sem=recv.at[slot],
                device_id=peer(to), device_id_type=MESH,
            )

        others = [lax.rem(me + d, count) for d in range(1, count)]
        for to in others:
            piece(me, to).start()
        buf[me] = source[...]
        for other in others:
            piece(other, other).wait_recv()
        total = buf[0]
        for j in range(1, count):
            total = total + buf[j]
        return total, lambda: [piece(me, to).wait_send() for to in others]

    total, finish_first = stage(sums_ref, first_buf, first_send, first_recv, in_first, first_peer, 8)
    mine[...] = total
    total, finish_second = stage(mine, second_buf, second_send, second_recv, position, second_peer, RING)
    total_out[...] = total
    finish_first()
    finish_second()


def unpack_kernel(total_ref, weight_out, bias_out):
    total = total_ref[...]
    for l in range(2):
        packed = total[8 * l : 8 * l + 8, :]
        for k in range(4):
            moved = packed if k == 0 else pltpu.roll(packed, LANES - 32 * k, 1)
            weight_out[l, 8 * k : 8 * k + 8, :] = moved[:, 0:32]
    bias_out[...] = total[16:18, 0:32]


def in_memory_order(table):
    cols = table.shape[-1]
    return table.reshape(-1, 8, cols // LANES, LANES).transpose(0, 2, 1, 3).reshape(table.size)


def body(
    entity_state, edge_tiles, query_head, query_relation, query_table, rel_vectors, mix_weight, mix_bias, cotangent
):
    rows, cols = entity_state.shape
    tiles, unused, slot_total = edge_tiles.shape
    edge_count = tiles * slot_total
    rel_rows = rel_vectors.shape[1]
    padded_rows = -(-rel_rows // LANES) * LANES
    edges = edge_tiles.transpose(1, 0, 2)
    slots = in_memory_order(edges)
    table_t = query_table.T
    rel_t = rel_vectors.transpose(0, 2, 1)
    smem = pl.BlockSpec(memory_space=pltpu.SMEM)
    vmem = pl.BlockSpec(memory_space=pltpu.VMEM)
    anywhere = pl.BlockSpec(memory_space=pl.ANY)
    half = jax.ShapeDtypeStruct((rows, cols), BF16)
    wide = jax.ShapeDtypeStruct((4 * rows, cols), BF16)
    packet = (24, LANES)
    block = pltpu.VMEM((rows, cols), BF16)
    window = pltpu.VMEM((rows * 4, 4, LANES), F32)
    edge_rows = pltpu.VMEM((edge_count, LANES), F32)
    padded = pltpu.VMEM((2, DIM, padded_rows), F32)
    message = pltpu.VMEM((slot_total * 4, LANES), F32)
    state_two, grad_mixed, mixed_zero, slope_zero, rel_one, sums, places = pl.pallas_call(
        forward_kernel,
        out_shape=(
            half,
            half,
            wide,
            wide,
            jax.ShapeDtypeStruct((edge_count, LANES), F32),
            jax.ShapeDtypeStruct((16, LANES), F32),
            jax.ShapeDtypeStruct((tiles, slot_total), jnp.int32),
        ),
        in_specs=[anywhere] * 6 + [smem] * 2 + [vmem] * 2,
        out_specs=(anywhere,) * 5 + (vmem,) * 2,
        scratch_shapes=[block] * 6
        + [
            pltpu.VMEM((4 * rows, cols), BF16),
            pltpu.VMEM((2, 3, rows, cols), BF16),
            window,
            window,
            edge_rows,
            edge_rows,
            padded,
            pltpu.VMEM((rel_rows, 4, LANES), F32),
            pltpu.VMEM((2, slot_total * 4, LANES), F32),
            pltpu.VMEM((CHUNK, cols), F32),
            pltpu.VMEM((4, 256, 256), BF16),
            pltpu.VMEM((1, cols), jnp.int32),
            pltpu.VMEM((1, cols), F32),
            pltpu.SMEM((edge_count,), jnp.int32),
            pltpu.VMEM(edges.shape, jnp.int32),
            pltpu.VMEM(table_t.shape, F32),
            pltpu.VMEM(rel_t.shape, F32),
            pltpu.SemaphoreType.DMA((12 + 2 * CHUNKS,)),
            pltpu.SemaphoreType.DMA((2, 3, CHUNKS * PIECES)),
            pltpu.SemaphoreType.DMA((2, 3, CHUNKS * PIECES)),
        ],
        compiler_params=pltpu.CompilerParams(
            vmem_limit_bytes=VMEM_BYTES, collective_id=0, has_side_effects=True
        ),
        name="two_layers",
    )(
        entity_state, cotangent, slots, edges, table_t, rel_t, query_head, query_relation, mix_weight, mix_bias
    )
    state_out, sums = pl.pallas_call(
        scatter_kernel,
        out_shape=(half, jax.ShapeDtypeStruct(packet, F32)),
        in_specs=[anywhere] * 8 + [vmem],
        out_specs=(anywhere, vmem),
        scratch_shapes=[pltpu.VMEM((rows * 16, LANES), F32)] * SUMS
        + [
            edge_rows,
            pltpu.VMEM((4 * rows, cols), BF16),
            pltpu.VMEM((4 * rows, cols), BF16),
            block,
            block,
            message,
            pltpu.SMEM((edge_count,), jnp.int32),
            pltpu.VMEM(edges.shape, jnp.int32),
            block,
            pltpu.SemaphoreType.DMA((12,)),
        ],
        compiler_params=pltpu.CompilerParams(vmem_limit_bytes=VMEM_BYTES),
        name="scatter_terms",
    )(state_two, mixed_zero, slope_zero, rel_one, cotangent, in_memory_order(places), edges, grad_mixed, sums)
    total = pl.pallas_call(
        total_kernel,
        out_shape=jax.ShapeDtypeStruct(packet, F32),
        in_specs=[vmem],
        out_specs=vmem,
        scratch_shapes=[
            pltpu.VMEM(packet, F32),
            pltpu.VMEM((8,) + packet, F32),
            pltpu.VMEM((RING,) + packet, F32),
            pltpu.SemaphoreType.DMA((8,)),
            pltpu.SemaphoreType.DMA((8,)),
            pltpu.SemaphoreType.DMA((RING,)),
            pltpu.SemaphoreType.DMA((RING,)),
        ],
        compiler_params=pltpu.CompilerParams(collective_id=1, has_side_effects=True),
        name="total_sums",
    )(sums)
    weight_grads, bias_grads = pl.pallas_call(
        unpack_kernel,
        out_shape=(jax.ShapeDtypeStruct((2, DIM, DIM), F32), jax.ShapeDtypeStruct((2, DIM), F32)),
        in_specs=[vmem],
        out_specs=(vmem,) * 2,
        name="unpack_sums",
    )(total)
    return state_out, weight_grads, bias_grads


def solution(mesh):
    placed = (
        P("node", "query"),
        P("node", None, None),
        P("query"),
        P("query"),
        P(),
        P(),
        P(),
        P(),
        P("node", "query"),
    )
    return jax.shard_map(
        body, mesh=mesh, in_specs=placed, out_specs=(P("node", "query"), P(), P()), check_vma=False
    )
```
